32 devices in a mesh: dp: 16 (over z, x, core), tensor: 2 (over y).
Axes of the slice: x: 2, y: 2, z: 4, core: 2. Of those that a mesh axis runs over, the one named last changes fastest.
Arguments:
- tokens: bfloat16 [24576, 768], P(('dp', 'tensor')), may hold values from -6 to 6
- token_mask: int32 [1536, 16], P('dp'), may hold values from 0 to 1, as said below
- norm_gains: float32 [2, 768], replicated, may hold values from 0.5 to 1.5
- gain_moments: float32 [2, 768], replicated, may hold values from 76.8 to 614.4
- cotangent: bfloat16 [1536, 768], P(('dp', 'tensor')), may hold values from -6 to 6
- master: float32 [768, 96, 96], P(('dp', 'tensor'))
- stat_left: float32 [768, 96, 96], P(('dp', 'tensor')), as said below
- stat_right: float32 [768, 96, 96], P(('dp', 'tensor')), as said below
- root_left: float32 [768, 96, 96], P(('dp', 'tensor')), as said below
- root_right: float32 [768, 96, 96], P(('dp', 'tensor')), as said below
Outputs:
- pooled: float32 [1536, 768], P(('dp', 'tensor'))
- input_grad: float32 [24576, 768], P(('dp', 'tensor'))
- gain_grads: float32 [2, 768], replicated
- gain_moments_new: float32 [2, 768], replicated
- norm_gains_new: float32 [2, 768], replicated
- grad_blocks: float32 [768, 96, 96], P(('dp', 'tensor'))
- left_new: float32 [768, 96, 96], P(('dp', 'tensor'))
- right_new: float32 [768, 96, 96], P(('dp', 'tensor'))
- master_new: float32 [768, 96, 96], P(('dp', 'tensor'))
- master_copy: bfloat16 [768, 96, 96], P(('dp', 'tensor'))
The draws below stay inside these ranges and needn't reach their ends.
Inputs may be any that keep to these rules, and one draw needn't show every extreme that they name: `token_mask`: each caption's mask is 1 on its first n slots and 0 after, n from 4 to 16; the first caption has n = 4 and the last n = 16. `stat_left`: each block is symmetric positive definite. `stat_right`: each block is symmetric positive definite. `root_left`: each block is symmetric positive definite. `root_right`: each block is symmetric positive definite.
All inputs are finite; a program needn't handle non-finite values.
Results may differ from the reference program's by a relative error of at most 0.0097.
Values may be sent and summed in bfloat16 or wider, within the bound.
No kernel may reach another device: no remote copies, remote signals or barrier semaphores. Data moves between devices by JAX's collectives and lax.ppermute only.
A program may use at most 192 MiB of HBM per device.

```python
import math
import jax
import jax.numpy as jnp
from jax import lax

D = 768
HEADS = 12
HD = 64
FF = 3072
SLOTS = 16
BLOCK = 96
CAP_DEV = 96
CAPTIONS = 1536
TOKENS = 24576
NBLK = 384
NBT = 768
NOWN = 24
N_DP = 16
N_TENSOR = 2


def draw_token_mask(key, part):
    lengths = jax.random.randint(key, (CAPTIONS,), 4, SLOTS + 1)
    lengths = lengths.at[0].set(4).at[CAPTIONS - 1].set(SLOTS)
    slot_ids = jnp.arange(SLOTS, dtype=jnp.int32)[None, :]
    return (slot_ids < lengths[:, None]).astype(jnp.int32)


def block_scales():
    block_ids = jnp.arange(NBT)
    per_tensor = NBT // NBLK
    list_pos = block_ids // (per_tensor * NOWN) * NOWN + block_ids % NOWN
    param_total = 4 * D * D + 2 * D * FF
    first_end = 3 * D * D * NBLK // param_total
    second_end = first_end + D * D * NBLK // param_total
    third_end = second_end + D * FF * NBLK // param_total
    return jnp.where(list_pos < first_end, D ** (-0.5), jnp.where(list_pos < second_end, 3.0 * D ** (-0.5), jnp.where(list_pos < third_end, D ** (-0.5), FF ** (-0.5))))


def draw_master(key, part):
    scales = block_scales().astype(jnp.float32)
    return jax.random.normal(key, (NBT, BLOCK, BLOCK), jnp.float32) * scales[:, None, None]


def spd_blocks(key, low_diag, high_diag, off_bound, scale_level):
    first_key, second_key = jax.random.split(key)
    diagonal = jnp.exp(jax.random.uniform(first_key, (NBT, BLOCK), jnp.float32, math.log(low_diag), math.log(high_diag))) * scale_level
    off_diag = jax.random.uniform(second_key, (NBT, BLOCK, BLOCK), jnp.float32, -1.0, 1.0) * (off_bound * scale_level / BLOCK)
    off_diag = 0.5 * (off_diag + jnp.swapaxes(off_diag, 1, 2))
    identity = jnp.eye(BLOCK, dtype=jnp.float32)
    return off_diag * (1.0 - identity) + diagonal[:, :, None] * identity


def draw_stat_left(key, part):
    return spd_blocks(jax.random.fold_in(key, 11), 2.0, 8.0, 2.0, 0.02 * BLOCK * CAPTIONS)


def draw_stat_right(key, part):
    return spd_blocks(jax.random.fold_in(key, 12), 2.0, 8.0, 2.0, 0.02 * BLOCK * CAPTIONS)


def draw_root_left(key, part):
    return spd_blocks(jax.random.fold_in(key, 13), 0.8, 1.25, 0.5, (0.08 * BLOCK * CAPTIONS) ** (-0.25))


def draw_root_right(key, part):
    return spd_blocks(jax.random.fold_in(key, 14), 0.8, 1.25, 0.5, (0.08 * BLOCK * CAPTIONS) ** (-0.25))


def steps_of(rng, dims, cuts, low, top_value):
    level = 1.0
    for position, blocks in cuts:
        heights = jax.random.uniform(jax.random.fold_in(jax.random.fold_in(rng, 6), position), (blocks,), jnp.float32, low / len(cuts), top_value / len(cuts))
        level = level * jnp.repeat(jnp.exp(heights), dims[position] // blocks).reshape((-1,) + (1,) * (len(dims) - 1 - position))
    return level


def gaussian(key, extent, deviation, limit, cuts=(), held_as=jnp.bfloat16):
    entries = jax.random.normal(key, extent, jnp.float32) * deviation
    if len(cuts) > 0:
        entries = steps_of(key, extent, cuts, -0.22, 0.18) * entries
    return jnp.clip(entries, min=-limit, max=limit).astype(held_as)


def setup_inputs(seed: int = 0) -> dict:
    key_list = jax.random.split(jax.random.key(seed), 11)
    tokens = gaussian(key_list[0], (TOKENS, D), 1.0, 6.0, ((0, 32),))
    token_mask = draw_token_mask(jax.random.fold_in(key_list[10], 71), 0)
    norm_gains = jnp.clip(1.0 + 0.1 * jax.random.normal(key_list[2], (2, D), jnp.float32), 0.5, 1.5)
    gain_moments = jnp.clip(jnp.exp(jax.random.uniform(key_list[3], (2, D), jnp.float32, math.log(76.8), math.log(614.4))), 76.8, 614.4)
    cotangent = gaussian(key_list[4], (CAPTIONS, D), 1.0, 6.0, ((0, 32),))
    master = draw_master(jax.random.fold_in(key_list[10], 71), 0)
    stat_left = draw_stat_left(jax.random.fold_in(key_list[10], 71), 0)
    stat_right = draw_stat_right(jax.random.fold_in(key_list[10], 71), 0)
    root_left = draw_root_left(jax.random.fold_in(key_list[10], 71), 0)
    root_right = draw_root_right(jax.random.fold_in(key_list[10], 71), 0)
    return {"tokens": tokens, "token_mask": token_mask, "norm_gains": norm_gains, "gain_moments": gain_moments, "cotangent": cotangent, "master": master, "stat_left": stat_left, "stat_right": stat_right, "root_left": root_left, "root_right": root_right}


EPSILON = 1e-06
DECAY_RATE = 0.5
STEP_RATE = 0.25
GAIN_RATE = 0.3
MASKED_SCORE = -1e+30
PRECISE = lax.Precision.HIGHEST

@jax.custom_vjp
def low(v):
    return lax.optimization_barrier(v.astype(jnp.bfloat16)).astype(jnp.float32)

@jax.custom_vjp
def low_back(v):
    return v

def low_keep(v):
    return (low(v), None)

def low_pass(kept, grad):
    return (grad,)

def back_keep(v):
    return (v, None)

def back_low(kept, grad):
    return (low(grad),)
low.defvjp(low_keep, low_pass)
low_back.defvjp(back_keep, back_low)

def layer_norm(values, gain):
    center = values - lax.optimization_barrier(jnp.mean(values, axis=-1, keepdims=True))
    spread = lax.optimization_barrier(jnp.mean(center * center, axis=-1, keepdims=True))
    return center * lax.rsqrt(spread + EPSILON) * gain

def block_pooled(inputs, mask_float, gain_pair, use_qkv, use_out, use_up, use_down):
    captions = inputs.shape[0]
    flat_rows = inputs.reshape(captions * SLOTS, D)
    normed = low(layer_norm(flat_rows, gain_pair[0]))
    mixed_qkv = low(low_back(jnp.dot(normed, low(use_qkv), precision=PRECISE)))
    mixed_qkv = mixed_qkv.reshape(captions, SLOTS, N_TENSOR, 3, HEADS // N_TENSOR, HD)
    queries = mixed_qkv[:, :, :, 0].reshape(captions, SLOTS, HEADS, HD)
    key_rows = mixed_qkv[:, :, :, 1].reshape(captions, SLOTS, HEADS, HD)
    value_rows = mixed_qkv[:, :, :, 2].reshape(captions, SLOTS, HEADS, HD)
    scores = low_back(jnp.einsum('cqhe,ckhe->chqk', queries, key_rows, precision=PRECISE) * HD ** (-0.5))
    scores = jnp.where(mask_float[:, None, None, :] > 0, scores, MASKED_SCORE)
    weights = low(jax.nn.softmax(scores, axis=-1))
    attended = jnp.einsum('chqk,ckhe->cqhe', weights, value_rows, precision=PRECISE)
    attended = low(low_back(attended.reshape(captions * SLOTS, D)))
    after_attn = flat_rows + low_back(jnp.dot(attended, low(use_out), precision=PRECISE))
    normed_two = low(layer_norm(after_attn, gain_pair[1]))
    up_proj = low_back(jnp.dot(normed_two, low(use_up), precision=PRECISE))
    hidden = low(jax.nn.gelu(up_proj))
    mlp_out = low_back(jnp.dot(hidden, low(use_down), precision=PRECISE))
    output = (after_attn + mlp_out).reshape(captions, SLOTS, D)
    return lax.optimization_barrier(jnp.sum(output * mask_float[:, :, None], axis=1)) / lax.optimization_barrier(jnp.sum(mask_float, axis=1))[:, None]

def to_blocks(matrix):
    num_rows, num_cols = matrix.shape
    return matrix.reshape(num_rows // BLOCK, BLOCK, num_cols // BLOCK, BLOCK).transpose(0, 2, 1, 3).reshape(-1, BLOCK, BLOCK)

def shard_shapes():
    return ((D, 3 * D // N_TENSOR), (D // N_TENSOR, D), (D, FF // N_TENSOR), (FF // N_TENSOR, D))

def unpack(blocks):
    matrices = []
    offset = 0
    for num_rows, num_cols in shard_shapes():
        num_blocks = num_rows // BLOCK * (num_cols // BLOCK)
        chosen = blocks[offset:offset + num_blocks]
        matrices.append(chosen.reshape(num_rows // BLOCK, num_cols // BLOCK, BLOCK, BLOCK).transpose(0, 2, 1, 3).reshape(num_rows, num_cols))
        offset += num_blocks
    return matrices

def reference(tokens, token_mask, norm_gains, gain_moments, cotangent, master, stat_left, stat_right, root_left, root_right):
    per_tensor = master.reshape(N_DP, N_TENSOR, NOWN, BLOCK, BLOCK).transpose(1, 0, 2, 3, 4).reshape(N_TENSOR, NBLK, BLOCK, BLOCK)
    shards = [unpack(per_tensor[tensor_id]) for tensor_id in range(N_TENSOR)]
    w_qkv = jnp.concatenate([shard[0] for shard in shards], axis=1)
    w_out = jnp.concatenate([shard[1] for shard in shards], axis=0)
    w_up = jnp.concatenate([shard[2] for shard in shards], axis=1)
    w_down = jnp.concatenate([shard[3] for shard in shards], axis=0)
    matrices = (w_qkv, w_out, w_up, w_down)
    groups = CAPTIONS // CAP_DEV
    inputs_all = tokens.astype(jnp.float32).reshape(groups, CAP_DEV, SLOTS, D)
    masks_all = token_mask.astype(jnp.float32).reshape(groups, CAP_DEV, SLOTS)
    cotan_all = cotangent.astype(jnp.float32).reshape(groups, CAP_DEV, D)

    def scan_step(totals, group_data):
        inputs, mask_float, group_cotan = group_data

        def forward(values, gain_pair, use_qkv, use_out, use_up, use_down):
            return block_pooled(values, mask_float, gain_pair, use_qkv, use_out, use_up, use_down)
        pooled_part, pullback = jax.vjp(forward, inputs, norm_gains, *matrices)
        gradients = pullback(group_cotan)
        totals = tuple((earlier + later for earlier, later in zip(totals, gradients[1:])))
        return (totals, (pooled_part, gradients[0]))
    initial = (jnp.zeros_like(norm_gains),) + tuple((jnp.zeros_like(matrix) for matrix in matrices))
    summed, (pooled, input_grad) = lax.scan(scan_step, initial, (inputs_all, masks_all, cotan_all))
    pooled = pooled.reshape(CAPTIONS, D)
    input_grad = input_grad.reshape(TOKENS, D)
    grad_gain, grad_qkv, grad_out, grad_up, grad_down = summed
    col_qkv = 3 * D // N_TENSOR
    row_out = D // N_TENSOR
    col_up = FF // N_TENSOR
    row_down = FF // N_TENSOR
    lists = []
    for tensor_id in range(N_TENSOR):
        pieces = [to_blocks(grad_qkv[:, tensor_id * col_qkv:(tensor_id + 1) * col_qkv]), to_blocks(grad_out[tensor_id * row_out:(tensor_id + 1) * row_out]), to_blocks(grad_up[:, tensor_id * col_up:(tensor_id + 1) * col_up]), to_blocks(grad_down[tensor_id * row_down:(tensor_id + 1) * row_down])]
        lists.append(jnp.concatenate(pieces, axis=0))
    grad_blocks = jnp.stack(lists, 0).reshape(N_TENSOR, N_DP, NOWN, BLOCK, BLOCK).transpose(1, 0, 2, 3, 4).reshape(NBT, BLOCK, BLOCK)
    left_new = DECAY_RATE * stat_left + (1.0 - DECAY_RATE) * jnp.einsum('nij,nkj->nik', grad_blocks, grad_blocks, precision=PRECISE)
    right_new = DECAY_RATE * stat_right + (1.0 - DECAY_RATE) * jnp.einsum('nji,njk->nik', grad_blocks, grad_blocks, precision=PRECISE)
    right_side = jnp.einsum('nij,njk->nik', grad_blocks, root_right, precision=PRECISE)
    direction = jnp.einsum('nij,njk->nik', root_left, right_side, precision=PRECISE)
    master_new = master - STEP_RATE * direction
    moments_new = DECAY_RATE * gain_moments + (1.0 - DECAY_RATE) * grad_gain * grad_gain
    gains_new = norm_gains - GAIN_RATE * grad_gain / (jnp.sqrt(moments_new) + 1e-08)
    return (pooled, input_grad, grad_gain, moments_new, gains_new, grad_blocks, left_new, right_new, master_new, master_new.astype(jnp.bfloat16))
```

```python
import functools

import jax
import jax.numpy as jnp
from jax import lax
from jax.experimental import pallas as pl
from jax.experimental.pallas import tpu as pltpu
from jax.sharding import PartitionSpec as P

D = 768
HEADS = 12
HD = 64
FF = 3072
BLOCK = 96
SLOTS = 16
HALVES = 2
STRIP = 4 * BLOCK
STRIPS = 96
GROUP = 128
PAIR = 2 * HD

EPSILON = 1e-06
DECAY_RATE = 0.5
STEP_RATE = 0.25
GAIN_RATE = 0.3
MASKED_SCORE = -1e30
PRECISE = lax.Precision.HIGHEST
F32 = jnp.float32
BF16 = jnp.bfloat16
VMEM_BYTES = 56 << 20


def mm(left, right, left_dim=1, right_dim=0):
    return lax.dot_general(
        left, right, (((left_dim,), (right_dim,)), ((), ())), preferred_element_type=F32
    )


def flat(block):
    return block.reshape(-1, block.shape[-1])


def norm_parts(values):
    center = values - jnp.mean(values, axis=-1, keepdims=True)
    inverse = lax.rsqrt(jnp.mean(center * center, axis=-1, keepdims=True) + EPSILON)
    return center * inverse, inverse


def norm_back(xhat, inverse, gain, grad):
    scaled = grad * gain
    return inverse * (
        scaled
        - jnp.mean(scaled, axis=-1, keepdims=True)
        - xhat * jnp.mean(scaled * xhat, axis=-1, keepdims=True)
    )


def score_bias(mask_row):
    rows = lax.broadcasted_iota(jnp.int32, (GROUP, GROUP), 0) // SLOTS
    cols = lax.broadcasted_iota(jnp.int32, (GROUP, GROUP), 1) // SLOTS
    seen = (rows == cols) & (jnp.broadcast_to(mask_row, (GROUP, GROUP)) > 0)
    bias = jnp.where(seen, 0.0, MASKED_SCORE)
    return jnp.concatenate([bias, bias], axis=0)


def split_pair(values):
    first = lax.broadcasted_iota(jnp.int32, (GROUP, PAIR), 1) < HD
    zero = jnp.zeros_like(values)
    return jnp.concatenate(
        [jnp.where(first, values, zero), jnp.where(first, zero, values)], axis=0
    )


def join_pair(stacked):
    first = lax.broadcasted_iota(jnp.int32, (GROUP, PAIR), 1) < HD
    return jnp.where(first, stacked[:GROUP], stacked[GROUP:])


def pair_probs(queries, key_rows, bias):
    scores = mm(split_pair(queries), key_rows, 1, 1) * HD ** (-0.5) + bias
    shifted = jnp.exp(scores - jnp.max(scores, axis=-1, keepdims=True))
    return shifted / jnp.sum(shifted, axis=-1, keepdims=True)


def attention_forward(
    tok, gains, mask, w_qkv, w_out, normed, qkv, attended, after, normed_two, total
):
    half = pl.program_id(0)
    rows = tok.shape[0]

    @pl.when(half == 0)
    def _():
        @pl.loop(0, rows // GROUP)
        def _(i):
            span = pl.ds(pl.multiple_of(i * GROUP, GROUP), GROUP)
            xhat, _ = norm_parts(tok[span, :].astype(F32))
            normed[span, :] = (xhat * gains[0:1, :]).astype(BF16)

    for part in range(3):
        qkv[part] = mm(normed[...], flat(w_qkv[0, :, part])).astype(BF16)

    @pl.loop(0, rows // GROUP)
    def _(i):
        span = pl.ds(pl.multiple_of(i * GROUP, GROUP), GROUP)
        bias = score_bias(mask[i])
        for pair in range(STRIP // PAIR):
            lanes = slice(pair * PAIR, (pair + 1) * PAIR)
            probs = pair_probs(qkv[0, span, lanes], qkv[1, span, lanes], bias)
            mixed = mm(probs.astype(BF16), qkv[2, span, lanes])
            attended[0, span, lanes] = join_pair(mixed).astype(BF16)

    for part in range(2):
        lanes = slice(part * STRIP, (part + 1) * STRIP)
        partial = mm(attended[0], flat(w_out[0, :, part]))

        @pl.when(half == 0)
        def _():
            total[:, lanes] = partial

        @pl.when(half > 0)
        def _():
            total[:, lanes] += partial

    @pl.when(half == HALVES - 1)
    def _():
        @pl.loop(0, rows // GROUP)
        def _(i):
            span = pl.ds(pl.multiple_of(i * GROUP, GROUP), GROUP)
            summed = tok[span, :].astype(F32) + total[span, :]
            after[span, :] = summed
            xhat, _ = norm_parts(summed)
            normed_two[span, :] = (xhat * gains[1:2, :]).astype(BF16)


GELU_A = 0.7978845608028654
GELU_B = 0.044715


def gelu_both(v):
    square = v * v
    inner = jnp.tanh(GELU_A * v * (1.0 + GELU_B * square))
    half_up = 0.5 * (1.0 + inner)
    slope = half_up + (0.5 * GELU_A) * v * (1.0 - inner * inner) * (1.0 + (3.0 * GELU_B) * square)
    return v * half_up, slope


def spread(cot, share):
    captions = cot.shape[0]
    return (
        jnp.broadcast_to(cot[:, None, :], (captions, SLOTS, cot.shape[-1])).reshape(
            captions * SLOTS, cot.shape[-1]
        )
        * share
    )


def mlp_both(
    normed_two,
    after,
    cot,
    share,
    w_up,
    w_down,
    pooled,
    grad_normed_two,
    grad_up_w,
    grad_down_w,
    out_low,
    hidden,
    grad_up,
    total,
):
    step = pl.program_id(0)
    rows = normed_two.shape[0]
    chunk = 256

    @pl.when(step == 0)
    def _():
        total[...] = after[...]
        grad_normed_two[...] = jnp.zeros_like(grad_normed_two)

        @pl.loop(0, rows // GROUP)
        def _(i):
            span = pl.ds(pl.multiple_of(i * GROUP, GROUP), GROUP)
            caps = pl.ds(pl.multiple_of(i * (GROUP // SLOTS), GROUP // SLOTS), GROUP // SLOTS)
            out_low[span, :] = spread(cot[caps, :], share[span, :]).astype(BF16)

    @pl.loop(0, rows // chunk)
    def _(i):
        span = pl.ds(pl.multiple_of(i * chunk, chunk), chunk)
        up = mm(normed_two[span, :], flat(w_up[0, :, 0]))
        grad_hidden = mm(out_low[span, 0:STRIP], flat(w_down[0, :, 0]), 1, 1)
        grad_hidden += mm(out_low[span, STRIP:], flat(w_down[0, :, 1]), 1, 1)
        act, slope = gelu_both(up)
        act = act.astype(BF16)
        grad = (grad_hidden * slope).astype(BF16)
        hidden[span, :] = act
        grad_up[span, :] = grad
        for part in range(2):
            lanes = slice(part * STRIP, (part + 1) * STRIP)
            total[span, lanes] += mm(act, flat(w_down[0, :, part]))
        grad_normed_two[span, :] += mm(grad, flat(w_up[0, :, 0]), 1, 1)

    for part in range(2):
        lanes = slice(part * STRIP, (part + 1) * STRIP)
        grad_w = mm(hidden[...], out_low[:, lanes], 0, 0)
        grad_down_w[0, :, part] = grad_w.astype(BF16).reshape(4, BLOCK, STRIP)
    grad_w = mm(normed_two[...], grad_up[...], 0, 0)
    grad_up_w[0, :, 0] = grad_w.astype(BF16).reshape(8, BLOCK, STRIP)

    @pl.when(step == pl.num_programs(0) - 1)
    def _():
        @pl.loop(0, rows // GROUP)
        def _(i):
            span = pl.ds(pl.multiple_of(i * GROUP, GROUP), GROUP)
            caps = pl.ds(pl.multiple_of(i * (GROUP // SLOTS), GROUP // SLOTS), GROUP // SLOTS)
            weighted = (total[span, :] * share[span, :]).reshape(GROUP // SLOTS, SLOTS, D)
            pooled[caps, :] = jnp.sum(weighted, axis=1)


def attention_backward(
    tok,
    gains,
    mask,
    normed,
    qkv,
    attended,
    after,
    cot,
    share,
    grad_normed_two,
    w_qkv,
    w_out,
    input_grad,
    gain_part,
    grad_qkv_w,
    grad_out_w,
    grad_after,
    after_low,
    grad_att,
    grad_mixed,
    grad_normed,
):
    half = pl.program_id(0)
    rows = tok.shape[0]

    @pl.when(half == 0)
    def _():
        gain_part[...] = jnp.zeros_like(gain_part)

        @pl.loop(0, rows // GROUP)
        def _(i):
            span = pl.ds(pl.multiple_of(i * GROUP, GROUP), GROUP)
            caps = pl.ds(pl.multiple_of(i * (GROUP // SLOTS), GROUP // SLOTS), GROUP // SLOTS)
            xhat, inverse = norm_parts(after[span, :])
            grad = grad_normed_two[span, :]
            gain_part[1:2, :] += jnp.sum(grad * xhat, axis=0, keepdims=True)
            value = spread(cot[caps, :], share[span, :]) + norm_back(
                xhat, inverse, gains[1:2, :], grad
            )
            grad_after[span, :] = value
            after_low[span, :] = value.astype(BF16)

    grad = mm(after_low[:, 0:STRIP], flat(w_out[0, :, 0]), 1, 1)
    grad += mm(after_low[:, STRIP:], flat(w_out[0, :, 1]), 1, 1)
    grad_att[...] = grad.astype(BF16)
    for part in range(2):
        lanes = slice(part * STRIP, (part + 1) * STRIP)
        grad_w = mm(attended[0], after_low[:, lanes], 0, 0)
        grad_out_w[0, :, part] = grad_w.astype(BF16).reshape(4, BLOCK, STRIP)

    @pl.loop(0, rows // GROUP)
    def _(i):
        span = pl.ds(pl.multiple_of(i * GROUP, GROUP), GROUP)
        bias = score_bias(mask[i])
        for pair in range(STRIP // PAIR):
            lanes = slice(pair * PAIR, (pair + 1) * PAIR)
            queries, key_rows, value_rows = (qkv[part, span, lanes] for part in range(3))
            probs = pair_probs(queries, key_rows, bias)
            grads = split_pair(grad_att[span, lanes])
            grad_probs = mm(grads, value_rows, 1, 1)
            inner = jnp.sum(probs * grad_probs, axis=-1, keepdims=True)
            grad_scores = (probs * (grad_probs - inner)).astype(BF16)
            scale = HD ** (-0.5)
            grad_mixed[0, span, lanes] = (join_pair(mm(grad_scores, key_rows)) * scale).astype(BF16)
            grad_mixed[1, span, lanes] = (
                mm(grad_scores, split_pair(queries), 0, 0) * scale
            ).astype(BF16)
            grad_mixed[2, span, lanes] = mm(probs.astype(BF16), grads, 0, 0).astype(BF16)

    for part in range(3):
        grad_w = mm(normed[...], grad_mixed[part], 0, 0)
        grad_qkv_w[0, :, part] = grad_w.astype(BF16).reshape(8, BLOCK, STRIP)
    back = mm(grad_mixed[0], flat(w_qkv[0, :, 0]), 1, 1)
    back += mm(grad_mixed[1], flat(w_qkv[0, :, 1]), 1, 1)
    back += mm(grad_mixed[2], flat(w_qkv[0, :, 2]), 1, 1)

    @pl.when(half == 0)
    def _():
        grad_normed[...] = back

    @pl.when(half > 0)
    def _():
        grad_normed[...] += back

    @pl.when(half == HALVES - 1)
    def _():
        @pl.loop(0, rows // GROUP)
        def _(i):
            span = pl.ds(pl.multiple_of(i * GROUP, GROUP), GROUP)
            xhat, inverse = norm_parts(tok[span, :].astype(F32))
            grad = grad_normed[span, :]
            gain_part[0:1, :] += jnp.sum(grad * xhat, axis=0, keepdims=True)
            input_grad[span, :] = grad_after[span, :] + norm_back(
                xhat, inverse, gains[0:1, :], grad
            )


def whole(shape):
    return pl.BlockSpec(shape, lambda i: (0,) * len(shape))


def shape_of(*shape, dtype=BF16):
    return jax.ShapeDtypeStruct(shape, dtype)


def cost(flops, bytes_accessed):
    return pl.CostEstimate(flops=flops, bytes_accessed=bytes_accessed, transcendentals=0)


PARAMS = dict(dimension_semantics=("arbitrary",), vmem_limit_bytes=VMEM_BYTES)


def run_forward(tok, gains, mask, strips):
    rows = tok.shape[0]
    by_three = strips.reshape(HALVES, 32, 3, BLOCK, STRIP)
    by_two = strips.reshape(HALVES, 48, 2, BLOCK, STRIP)
    return pl.pallas_call(
        attention_forward,
        grid=(HALVES,),
        in_specs=[
            whole((rows, D)),
            whole((2, D)),
            whole((rows // GROUP, 1, GROUP)),
            pl.BlockSpec((1, 8, 3, BLOCK, STRIP), lambda i: (i, 0, 0, 0, 0)),
            pl.BlockSpec((1, 4, 2, BLOCK, STRIP), lambda i: (i, 3, 0, 0, 0)),
        ],
        out_specs=[
            whole((rows, D)),
            pl.BlockSpec((3, rows, STRIP), lambda i: (i, 0, 0)),
            pl.BlockSpec((1, rows, STRIP), lambda i: (i, 0, 0)),
            whole((rows, D)),
            whole((rows, D)),
        ],
        out_shape=[
            shape_of(rows, D),
            shape_of(6, rows, STRIP),
            shape_of(2, rows, STRIP),
            shape_of(rows, D, dtype=F32),
            shape_of(rows, D),
        ],
        scratch_shapes=[pltpu.VMEM((rows, D), F32)],
        compiler_params=pltpu.CompilerParams(**PARAMS),
        cost_estimate=cost(4_600_000_000, 16_000_000),
        name="attention_forward",
    )(tok, gains, mask, by_three, by_two)


def run_mlp(normed_two, after, cot, share, strips):
    rows = normed_two.shape[0]
    by_four = strips.reshape(HALVES, 24, 4, BLOCK, STRIP)
    by_two = strips.reshape(HALVES, 48, 2, BLOCK, STRIP)
    return pl.pallas_call(
        mlp_both,
        grid=(8,),
        in_specs=[
            whole((rows, D)),
            whole((rows, D)),
            whole((rows // SLOTS, D)),
            whole((rows, 1)),
            pl.BlockSpec((1, 8, 1, BLOCK, STRIP), lambda i: (i // 4, 1, i % 4, 0, 0)),
            pl.BlockSpec((1, 4, 2, BLOCK, STRIP), lambda i: (i // 4, 8 + i % 4, 0, 0, 0)),
        ],
        out_specs=[
            whole((rows // SLOTS, D)),
            whole((rows, D)),
            pl.BlockSpec((1, 8, 1, BLOCK, STRIP), lambda i: (i // 4, 0, i % 4, 0, 0)),
            pl.BlockSpec((1, 4, 2, BLOCK, STRIP), lambda i: (i // 4, i % 4, 0, 0, 0)),
        ],
        out_shape=[
            shape_of(rows // SLOTS, D, dtype=F32),
            shape_of(rows, D, dtype=F32),
            shape_of(HALVES, 8, 4, BLOCK, STRIP),
            shape_of(HALVES, 16, 2, BLOCK, STRIP),
        ],
        scratch_shapes=[
            pltpu.VMEM((rows, D), BF16),
            pltpu.VMEM((rows, STRIP), BF16),
            pltpu.VMEM((rows, STRIP), BF16),
            pltpu.VMEM((rows, D), F32),
        ],
        compiler_params=pltpu.CompilerParams(**PARAMS),
        cost_estimate=cost(22_000_000_000, 30_000_000),
        name="mlp_both",
    )(normed_two, after, cot, share, by_four, by_two)


def run_backward(tok, gains, mask, normed, qkv, attended, after, cot, share, grad_two, strips):
    rows = tok.shape[0]
    by_three = strips.reshape(HALVES, 32, 3, BLOCK, STRIP)
    by_two = strips.reshape(HALVES, 48, 2, BLOCK, STRIP)
    return pl.pallas_call(
        attention_backward,
        grid=(HALVES,),
        in_specs=[
            whole((rows, D)),
            whole((2, D)),
            whole((rows // GROUP, 1, GROUP)),
            whole((rows, D)),
            pl.BlockSpec((3, rows, STRIP), lambda i: (i, 0, 0)),
            pl.BlockSpec((1, rows, STRIP), lambda i: (i, 0, 0)),
            whole((rows, D)),
            whole((rows // SLOTS, D)),
            whole((rows, 1)),
            whole((rows, D)),
            pl.BlockSpec((1, 8, 3, BLOCK, STRIP), lambda i: (i, 0, 0, 0, 0)),
            pl.BlockSpec((1, 4, 2, BLOCK, STRIP), lambda i: (i, 3, 0, 0, 0)),
        ],
        out_specs=[
            whole((rows, D)),
            whole((2, D)),
            pl.BlockSpec((1, 8, 3, BLOCK, STRIP), lambda i: (i, 0, 0, 0, 0)),
            pl.BlockSpec((1, 4, 2, BLOCK, STRIP), lambda i: (i, 0, 0, 0, 0)),
        ],
        out_shape=[
            shape_of(rows, D, dtype=F32),
            shape_of(2, D, dtype=F32),
            shape_of(HALVES, 8, 3, BLOCK, STRIP),
            shape_of(HALVES, 4, 2, BLOCK, STRIP),
        ],
        scratch_shapes=[
            pltpu.VMEM((rows, D), F32),
            pltpu.VMEM((rows, D), BF16),
            pltpu.VMEM((rows, STRIP), BF16),
            pltpu.VMEM((3, rows, STRIP), BF16),
            pltpu.VMEM((rows, D), F32),
        ],
        compiler_params=pltpu.CompilerParams(**PARAMS),
        cost_estimate=cost(12_000_000_000, 25_000_000),
        name="attention_backward",
    )(tok, gains, mask, normed, qkv, attended, after, cot, share, grad_two, by_three, by_two)


def to_strips(blocks):
    count = blocks.shape[0] // 4
    return blocks.reshape(count, 4, BLOCK, BLOCK).transpose(0, 2, 1, 3).reshape(count, BLOCK, STRIP)


def to_blocks(strips):
    count = strips.shape[0]
    return strips.reshape(count, BLOCK, 4, BLOCK).transpose(0, 2, 1, 3).reshape(-1, BLOCK, BLOCK)


EVERY = ("tensor", "dp")


def gather_weights(master):
    low = master.astype(BF16)
    own = low.shape[0]
    if own % 4 == 0:
        strips = to_strips(low).reshape(-1, STRIP)
        strips = lax.all_gather(strips, EVERY, axis=0, tiled=True)
        return strips.reshape(HALVES, STRIPS, BLOCK, STRIP)
    blocks = lax.all_gather(low, EVERY, axis=0, tiled=True)
    return to_strips(blocks).reshape(HALVES, STRIPS, BLOCK, STRIP)


def scatter_grads(strips, own):
    if own % 4 == 0:
        mine = lax.psum_scatter(
            strips.reshape(-1, STRIP), EVERY, scatter_dimension=0, tiled=True
        )
        return to_blocks(mine.reshape(-1, BLOCK, STRIP)).astype(F32)
    blocks = to_blocks(strips.reshape(-1, BLOCK, STRIP))
    return lax.psum_scatter(blocks, EVERY, scatter_dimension=0, tiled=True).astype(F32)


def body(
    tokens,
    token_mask,
    norm_gains,
    gain_moments,
    cotangent,
    master,
    stat_left,
    stat_right,
    root_left,
    root_right,
):
    rows = tokens.shape[0]
    own_caps = cotangent.shape[0]
    strips = gather_weights(master)
    group_mask = token_mask.astype(F32)
    own_mask = lax.dynamic_slice_in_dim(
        group_mask, lax.axis_index("tensor") * own_caps, own_caps, 0
    )
    share = (own_mask / jnp.sum(own_mask, axis=1, keepdims=True)).reshape(rows, 1)
    mask = own_mask.reshape(rows // GROUP, 1, GROUP)
    cot = cotangent.astype(F32)
    normed, qkv, attended, after, normed_two = run_forward(tokens, norm_gains, mask, strips)
    pooled, grad_two, grad_up_w, grad_down_w = run_mlp(normed_two, after, cot, share, strips)
    input_grad, gain_part, grad_qkv_w, grad_out_w = run_backward(
        tokens, norm_gains, mask, normed, qkv, attended, after, cot, share, grad_two, strips
    )
    all_grads = jnp.concatenate(
        [
            part.reshape(HALVES, -1, BLOCK, STRIP)
            for part in (grad_qkv_w, grad_out_w, grad_up_w, grad_down_w)
        ],
        axis=1,
    )
    grad_blocks = scatter_grads(all_grads, master.shape[0])
    gain_grads = lax.psum(gain_part, ("dp", "tensor"))
    moments_new = DECAY_RATE * gain_moments + (1.0 - DECAY_RATE) * gain_grads * gain_grads
    gains_new = norm_gains - GAIN_RATE * gain_grads / (jnp.sqrt(moments_new) + 1e-08)
    left_new = DECAY_RATE * stat_left + (1.0 - DECAY_RATE) * jnp.einsum(
        "nij,nkj->nik", grad_blocks, grad_blocks, precision=PRECISE
    )
    right_new = DECAY_RATE * stat_right + (1.0 - DECAY_RATE) * jnp.einsum(
        "nji,njk->nik", grad_blocks, grad_blocks, precision=PRECISE
    )
    right_side = jnp.einsum("nij,njk->nik", grad_blocks, root_right, precision=PRECISE)
    direction = jnp.einsum("nij,njk->nik", root_left, right_side, precision=PRECISE)
    master_new = master - STEP_RATE * direction
    return (
        pooled,
        input_grad,
        gain_grads,
        moments_new,
        gains_new,
        grad_blocks,
        left_new,
        right_new,
        master_new,
        master_new.astype(BF16),
    )


def solution(mesh):
    rows = P(("dp", "tensor"), None)
    blocks = P(("dp", "tensor"), None, None)
    return jax.shard_map(
        body,
        mesh=mesh,
        in_specs=(rows, P("dp", None), P(), P(), rows) + (blocks,) * 5,
        out_specs=(rows, rows, P(), P(), P()) + (blocks,) * 5,
        check_vma=False,
    )
```

```python
import functools

import jax
import jax.numpy as jnp
from jax import lax
from jax.experimental import pallas as pl
from jax.experimental.pallas import tpu as pltpu
from jax.sharding import PartitionSpec as P

D = 768
HEADS = 12
HD = 64
FF = 3072
BLOCK = 96
SLOTS = 16
HALVES = 2
STRIP = 4 * BLOCK
STRIPS = 96
OWN = 6
GROUP = 128
CAPS = GROUP // SLOTS
PAIR = 2 * HD

EPSILON = 1e-06
DECAY_RATE = 0.5
STEP_RATE = 0.25
GAIN_RATE = 0.3
MASKED_SCORE = -1e30
PRECISE = lax.Precision.HIGHEST
F32 = jnp.float32
BF16 = jnp.bfloat16


def mm(left, right, left_dim=1, right_dim=0):
    return lax.dot_general(
        left, right, (((left_dim,), (right_dim,)), ((), ())), preferred_element_type=F32
    )


def side_by_side(ref, lead, count):
    parts = [ref[lead + (slice(None), i)].reshape(-1, STRIP) for i in range(count)]
    return jnp.concatenate(parts, axis=1)


def norm_parts(values):
    center = values - jnp.mean(values, axis=-1, keepdims=True)
    inverse = lax.rsqrt(jnp.mean(center * center, axis=-1, keepdims=True) + EPSILON)
    return center * inverse, inverse


def norm_back(xhat, inverse, gain, grad):
    scaled = grad * gain
    return inverse * (
        scaled
        - jnp.mean(scaled, axis=-1, keepdims=True)
        - xhat * jnp.mean(scaled * xhat, axis=-1, keepdims=True)
    )


def split_pair(values):
    first = lax.broadcasted_iota(jnp.int32, (GROUP, PAIR), 1) < HD
    zero = jnp.zeros_like(values)
    return jnp.concatenate(
        [jnp.where(first, values, zero), jnp.where(first, zero, values)], axis=0
    )


def join_pair(stacked):
    first = lax.broadcasted_iota(jnp.int32, (GROUP, PAIR), 1) < HD
    return jnp.where(first, stacked[:GROUP], stacked[GROUP:])


def caption_of():
    return lax.broadcasted_iota(jnp.int32, (SLOTS, 2 * GROUP), 1) % GROUP // SLOTS


def compact(full, caption):
    kept = full[0:SLOTS]
    for i in range(1, CAPS):
        kept = jnp.where(caption == i, full[i * SLOTS : (i + 1) * SLOTS], kept)
    return kept


def expand(kept, caption):
    zero = jnp.zeros_like(kept)
    return jnp.concatenate(
        [jnp.where(caption == i, kept, zero).astype(BF16) for i in range(CAPS)], axis=0
    )


def pair_probs(queries, key_rows, bias, caption):
    scores = compact(mm(key_rows, queries, 1, 1), caption) * HD ** (-0.5) + bias
    shifted = jnp.exp(scores - jnp.max(scores, axis=0, keepdims=True))
    return shifted / jnp.sum(shifted, axis=0, keepdims=True)


def key_bias(mask):
    bias = jnp.where(mask > 0, 0.0, MASKED_SCORE)
    return jnp.concatenate([bias, bias], axis=1)


def span_of(i, size=GROUP):
    return pl.ds(pl.multiple_of(i * size, size), size)


def attention_forward(
    tok, gains, mask, by_three, by_two, normed, qkv, attended, after, normed_two, w_qkv, w_out, sems
):
    rows = tok.shape[0]
    copies = []
    for half in range(HALVES):
        copies.append(
            pltpu.make_async_copy(by_three.at[half, 0:8], w_qkv.at[half], sems.at[half])
        )
    for half in range(HALVES):
        copies.append(
            pltpu.make_async_copy(by_two.at[half, 12:16], w_out.at[half], sems.at[2 + half])
        )
    for copy in copies:
        copy.start()

    @pl.loop(0, rows // GROUP)
    def _(i):
        span = span_of(i)
        xhat, _ = norm_parts(tok[span, :].astype(F32))
        normed[span, :] = (xhat * gains[0:1, :]).astype(BF16)

    for half in range(HALVES):
        copies[half].wait()
        mixed = mm(normed[...], side_by_side(w_qkv, (half,), 3)).astype(BF16)
        for part in range(3):
            qkv[3 * half + part] = mixed[:, part * STRIP : (part + 1) * STRIP]

    @pl.loop(0, rows // GROUP)
    def _(i):
        span = span_of(i)
        bias = key_bias(mask[i])
        caption = caption_of()
        for half in range(HALVES):
            for pair in range(STRIP // PAIR):
                lanes = slice(pair * PAIR, (pair + 1) * PAIR)
                wide = slice(half * STRIP + pair * PAIR, half * STRIP + (pair + 1) * PAIR)
                probs = pair_probs(
                    split_pair(qkv[3 * half, span, lanes]),
                    qkv[3 * half + 1, span, lanes],
                    bias,
                    caption,
                )
                mixed = mm(expand(probs, caption), qkv[3 * half + 2, span, lanes], 0, 0)
                attended[span, wide] = join_pair(mixed).astype(BF16)

    copies[2].wait()
    copies[3].wait()
    weight = jnp.concatenate([side_by_side(w_out, (half,), 2) for half in range(HALVES)], axis=0)
    after[...] = mm(attended[...], weight)

    @pl.loop(0, rows // GROUP)
    def _(i):
        span = span_of(i)
        summed = tok[span, :].astype(F32) + after[span, :]
        after[span, :] = summed
        xhat, _ = norm_parts(summed)
        normed_two[span, :] = (xhat * gains[1:2, :]).astype(BF16)


GELU_A = 0.7978845608028654
GELU_B = 0.044715


def gelu_both(v):
    square = v * v
    inner = jnp.tanh(GELU_A * v * (1.0 + GELU_B * square))
    half_up = 0.5 * (1.0 + inner)
    slope = half_up + (0.5 * GELU_A) * v * (1.0 - inner * inner) * (1.0 + (3.0 * GELU_B) * square)
    return v * half_up, slope


def spread(cot, share):
    captions = cot.shape[0]
    wide = jnp.broadcast_to(cot[:, None, :], (captions, SLOTS, cot.shape[-1]))
    return wide.reshape(captions * SLOTS, cot.shape[-1]) * share


class Emitter:
    def __init__(self, targets, runs, stage, sems, coords):
        self.stage, self.sems, self.core = stage, sems, coords[0]
        self.whole = targets[0] if len(targets) == 1 else None
        self.batches = [] if self.whole is not None else list(zip(runs, targets[0::2], targets[1::2]))

    def start(self, slot, value, half, strip, planes):
        self.stage[slot] = value
        source, sem = self.stage.at[slot], self.sems.at[slot]
        if self.whole is not None:
            pltpu.make_async_copy(source, self.whole.at[half, strip], sem).start()
            return
        plane = strip // (4 * OWN)
        place = (strip // (2 * OWN)) % 2
        owner = (strip // OWN) % 2
        for run, kept, sent in self.batches:
            inside = [z for z in planes if z in run]
            if not inside:
                continue
            here = True if len(inside) == len(planes) else (plane >= run[0]) & (plane <= run[-1])
            spot = (plane - run[0], half, place, strip % OWN)

            @pl.when(here & (owner == self.core))
            def _():
                pltpu.make_async_copy(source, kept.at[spot], sem).start()

            @pl.when(here & (owner != self.core))
            def _():
                pltpu.make_async_copy(source, sent.at[spot], sem).start()

    def wait(self, slot):
        target = self.whole.at[0, 0] if self.whole is not None else self.batches[0][1].at[0, 0, 0, 0]
        pltpu.make_async_copy(self.stage.at[slot], target, self.sems.at[slot]).wait()


def mlp_both(coords, normed_two, cot, share, w_up, w_down, *rest):
    hidden, grad_normed_two, *targets, out_low, grad_up, stage, sems = rest
    step = pl.program_id(0)
    rows = normed_two.shape[0]
    emit = Emitter(targets, ((2, 3), (1,)), stage, sems, coords)

    @pl.when(step == 0)
    def _():
        @pl.loop(0, rows // GROUP)
        def _(i):
            caps = span_of(i, CAPS)
            out_low[span_of(i), :] = spread(cot[caps, :], share[span_of(i), :]).astype(BF16)

        grad_normed_two[...] = jnp.zeros_like(grad_normed_two)

    up_weight = side_by_side(w_up, (0,), 2)
    down_weight = side_by_side(w_down, (0,), 2)
    chunk = 256
    for i in range(rows // chunk):
        span = slice(i * chunk, (i + 1) * chunk)
        act, slope = gelu_both(mm(normed_two[span, :], up_weight))
        hidden[0, span, :] = act.astype(BF16)
        grad = (mm(out_low[span, :], down_weight, 1, 1) * slope).astype(BF16)
        grad_up[span, :] = grad
        grad_normed_two[span, :] += mm(grad, up_weight, 1, 1)

    half = step // 2
    column = lax.rem(step, 2)
    slot = column * 32

    @pl.when(step >= 2)
    def _():
        for i in range(32):
            emit.wait(slot + i)

    grad_w = mm(hidden[0], out_low[...], 0, 0).astype(BF16)
    for row in range(8):
        for part in range(2):
            strip = 64 + 16 * column + 2 * row + part
            value = grad_w[row * BLOCK : (row + 1) * BLOCK, part * STRIP : (part + 1) * STRIP]
            emit.start(slot + 2 * row + part, value, half, strip, (2, 3))
    grad_w = mm(normed_two[...], grad_up[...], 0, 0).astype(BF16)
    for row in range(8):
        for part in range(2):
            strip = 32 + 4 * row + 2 * column + part
            value = grad_w[row * BLOCK : (row + 1) * BLOCK, part * STRIP : (part + 1) * STRIP]
            planes = (1,) if row < 4 else (2,)
            emit.start(slot + 16 + 2 * row + part, value, half, strip, planes)

    @pl.when(step == pl.num_programs(0) - 1)
    def _():
        for i in range(64):
            emit.wait(i)


def mlp_out(after, hidden, share, w_down, pooled, total):
    step = pl.program_id(0)
    rows = after.shape[0]
    product = mm(hidden[0], side_by_side(w_down, (0,), 2))

    @pl.when(step == 0)
    def _():
        total[...] = after[...] + product

    @pl.when(step > 0)
    def _():
        total[...] += product

    @pl.when(step == pl.num_programs(0) - 1)
    def _():
        @pl.loop(0, rows // GROUP)
        def _(i):
            weighted = (total[span_of(i), :] * share[span_of(i), :]).reshape(CAPS, SLOTS, D)
            pooled[span_of(i, CAPS), :] = jnp.sum(weighted, axis=1)


def output_backward(
    held, coords, gains, attended, after, cot, share, grad_normed_two, by_two, *rest
):
    grad_after, gain_part, grad_att, *targets = rest[held:-5]
    after_low, w_out, weight_sem, stage, sems = rest[-5:]
    rows = after.shape[0]
    emit = Emitter(targets, ((1,),), stage, sems, coords)
    copies = [
        pltpu.make_async_copy(by_two.at[half, 12:16], w_out.at[half], weight_sem.at[half])
        for half in range(HALVES)
    ]
    for copy in copies:
        copy.start()
    gain_part[...] = jnp.zeros_like(gain_part)

    @pl.loop(0, rows // GROUP)
    def _(i):
        span = span_of(i)
        xhat, inverse = norm_parts(after[span, :])
        grad = grad_normed_two[span, :]
        gain_part[...] += jnp.sum(grad * xhat, axis=0, keepdims=True)
        value = spread(cot[span_of(i, CAPS), :], share[span, :]) + norm_back(
            xhat, inverse, gains[1:2, :], grad
        )
        grad_after[span, :] = value
        after_low[span, :] = value.astype(BF16)

    grad_w = mm(attended[...], after_low[...], 0, 0).astype(BF16)
    for half in range(HALVES):
        for row in range(4):
            for part in range(2):
                top = (4 * half + row) * BLOCK
                value = grad_w[top : top + BLOCK, part * STRIP : (part + 1) * STRIP]
                emit.start(half * 8 + 2 * row + part, value, half, 24 + 2 * row + part, (1,))

    for copy in copies:
        copy.wait()
    weight = jnp.concatenate([side_by_side(w_out, (half,), 2) for half in range(HALVES)], axis=0)
    grad_att[...] = mm(after_low[...], weight, 1, 1).astype(BF16)
    for slot in range(16):
        emit.wait(slot)


def attention_backward(held, coords, mask, normed, qkv, grad_att, *rest):
    grad_mixed, *targets, stage, sems = rest[held:]
    rows = normed.shape[0]
    emit = Emitter(targets, ((0,),), stage, sems, coords)

    @pl.loop(0, rows // GROUP)
    def _(i):
        span = span_of(i)
        bias = key_bias(mask[i])
        caption = caption_of()
        scale = HD ** (-0.5)
        for half in range(HALVES):
            for pair in range(STRIP // PAIR):
                lanes = slice(pair * PAIR, (pair + 1) * PAIR)
                wide = slice(half * STRIP + pair * PAIR, half * STRIP + (pair + 1) * PAIR)
                queries = split_pair(qkv[3 * half, span, lanes])
                key_rows = qkv[3 * half + 1, span, lanes]
                value_rows = qkv[3 * half + 2, span, lanes]
                probs = pair_probs(queries, key_rows, bias, caption)
                grads = split_pair(grad_att[span, wide])
                grad_probs = compact(mm(value_rows, grads, 1, 1), caption)
                inner = jnp.sum(probs * grad_probs, axis=0, keepdims=True)
                grad_scores = expand(probs * (grad_probs - inner), caption)
                grad_mixed[3 * half, span, lanes] = (
                    join_pair(mm(grad_scores, key_rows, 0, 0)) * scale
                ).astype(BF16)
                grad_mixed[3 * half + 1, span, lanes] = (mm(grad_scores, queries) * scale).astype(
                    BF16
                )
                grad_mixed[3 * half + 2, span, lanes] = mm(expand(probs, caption), grads).astype(
                    BF16
                )

    for half in range(HALVES):
        grads = jnp.concatenate([grad_mixed[3 * half + part] for part in range(3)], axis=1)
        grad_w = mm(normed[...], grads, 0, 0).astype(BF16)
        for row in range(8):
            for part in range(3):
                strip = 3 * row + part
                value = grad_w[row * BLOCK : (row + 1) * BLOCK, part * STRIP : (part + 1) * STRIP]
                emit.start(half * 24 + strip, value, half, strip, (0,))
    for slot in range(48):
        emit.wait(slot)


def input_backward(tok, gains, grad_mixed, grad_after, w_qkv, input_grad, gain_part):
    half = pl.program_id(0)
    rows = tok.shape[0]
    grads = jnp.concatenate([grad_mixed[part] for part in range(3)], axis=1)
    back = mm(grads, side_by_side(w_qkv, (0,), 3), 1, 1)

    @pl.when(half == 0)
    def _():
        input_grad[...] = back

    @pl.when(half == HALVES - 1)
    def _():
        input_grad[...] += back
        gain_part[...] = jnp.zeros_like(gain_part)

        @pl.loop(0, rows // GROUP)
        def _(i):
            span = span_of(i)
            xhat, inverse = norm_parts(tok[span, :].astype(F32))
            grad = input_grad[span, :]
            gain_part[...] += jnp.sum(grad * xhat, axis=0, keepdims=True)
            input_grad[span, :] = grad_after[span, :] + norm_back(
                xhat, inverse, gains[0:1, :], grad
            )


def whole(*shape):
    return pl.BlockSpec(shape, lambda *_: (0,) * len(shape))


def shape_of(*shape, dtype=BF16):
    return jax.ShapeDtypeStruct(shape, dtype)


ANY = pl.BlockSpec(memory_space=pl.ANY)
SMEM = pl.BlockSpec(memory_space=pltpu.SMEM)


def call(kernel, name, in_specs, outs, scratch, flops, args, grid=(1,), aliases=None, mib=40):
    moved = sum(math_size(a.shape) * a.dtype.itemsize for a in args)
    moved += sum(math_size(s.shape) * s.dtype.itemsize for _, s in outs)
    return pl.pallas_call(
        kernel,
        grid=grid,
        in_specs=in_specs,
        out_specs=[spec for spec, _ in outs],
        out_shape=[shape for _, shape in outs],
        scratch_shapes=scratch,
        input_output_aliases=aliases or {},
        compiler_params=pltpu.CompilerParams(
            dimension_semantics=("arbitrary",) * len(grid), vmem_limit_bytes=mib << 20
        ),
        cost_estimate=pl.CostEstimate(flops=flops, bytes_accessed=moved, transcendentals=0),
        name=name,
    )(*args)


def math_size(shape):
    size = 1
    for extent in shape:
        size *= extent
    return size


UNIT = 2 * 768 * 768 * 768


def run_forward(tok, gains, mask, strips):
    rows = tok.shape[0]
    by_three = strips.reshape(HALVES, 32, 3, BLOCK, STRIP)
    by_two = strips.reshape(HALVES, 48, 2, BLOCK, STRIP)
    return call(
        attention_forward,
        "attention_forward",
        [whole(rows, D), whole(2, D), whole(rows // GROUP, SLOTS, GROUP), ANY, ANY],
        [
            (whole(rows, D), shape_of(rows, D)),
            (whole(6, rows, STRIP), shape_of(6, rows, STRIP)),
            (whole(rows, D), shape_of(rows, D)),
            (whole(rows, D), shape_of(rows, D, dtype=F32)),
            (whole(rows, D), shape_of(rows, D)),
        ],
        [
            pltpu.VMEM((HALVES, 8, 3, BLOCK, STRIP), BF16),
            pltpu.VMEM((HALVES, 4, 2, BLOCK, STRIP), BF16),
            pltpu.SemaphoreType.DMA((4,)),
        ],
        5 * UNIT,
        (tok, gains, mask, by_three, by_two),
    )


def targets_of(runs, split):
    if split:
        shapes = [shape_of(len(run), HALVES, 2, OWN, BLOCK, STRIP) for run in runs for _ in range(2)]
    else:
        shapes = [shape_of(HALVES, STRIPS, BLOCK, STRIP)]
    return [(ANY, shape) for shape in shapes]


def up_spec():
    return pl.BlockSpec((1, 8, 2, BLOCK, STRIP), lambda i: (i // 2, 1, i % 2, 0, 0))


def down_spec():
    return pl.BlockSpec((1, 8, 2, BLOCK, STRIP), lambda i: (i // 2, 4 + i % 2, 0, 0, 0))


def stage_of(count):
    return [pltpu.VMEM((count, BLOCK, STRIP), BF16), pltpu.SemaphoreType.DMA((count,))]


def run_mlp(coords, normed_two, cot, share, strips, split):
    rows = normed_two.shape[0]
    by_four = strips.reshape(HALVES, 24, 4, BLOCK, STRIP)
    by_two = strips.reshape(HALVES, 48, 2, BLOCK, STRIP)
    return call(
        mlp_both,
        "mlp_both",
        [SMEM, whole(rows, D), whole(rows // SLOTS, D), whole(rows, 1), up_spec(), down_spec()],
        [
            (pl.BlockSpec((1, rows, D), lambda i: (i, 0, 0)), shape_of(4, rows, D)),
            (whole(rows, D), shape_of(rows, D, dtype=F32)),
        ]
        + targets_of(((2, 3), (1,)), split),
        [pltpu.VMEM((rows, D), BF16), pltpu.VMEM((rows, D), BF16)] + stage_of(64),
        20 * UNIT,
        (coords, normed_two, cot, share, by_four, by_two),
        grid=(4,),
    )


def run_mlp_out(after, hidden, share, strips):
    rows = after.shape[0]
    by_two = strips.reshape(HALVES, 48, 2, BLOCK, STRIP)
    return call(
        mlp_out,
        "mlp_out",
        [whole(rows, D), pl.BlockSpec((1, rows, D), lambda i: (i, 0, 0)), whole(rows, 1), down_spec()],
        [(whole(rows // SLOTS, D), shape_of(rows // SLOTS, D, dtype=F32))],
        [pltpu.VMEM((rows, D), F32)],
        4 * UNIT,
        (after, hidden, share, by_two),
        grid=(4,),
    )[0]


def run_output(coords, gains, attended, after, cot, share, grad_two, strips, held, split):
    rows = after.shape[0]
    by_two = strips.reshape(HALVES, 48, 2, BLOCK, STRIP)
    return call(
        functools.partial(output_backward, len(held)),
        "output_backward",
        [
            SMEM,
            whole(2, D),
            whole(rows, D),
            whole(rows, D),
            whole(rows // SLOTS, D),
            whole(rows, 1),
            whole(rows, D),
            ANY,
        ]
        + [ANY] * len(held),
        [
            (whole(rows, D), shape_of(rows, D, dtype=F32)),
            (whole(1, D), shape_of(1, D, dtype=F32)),
            (whole(rows, D), shape_of(rows, D)),
        ]
        + targets_of(((1,),), split),
        [
            pltpu.VMEM((rows, D), BF16),
            pltpu.VMEM((HALVES, 4, 2, BLOCK, STRIP), BF16),
            pltpu.SemaphoreType.DMA((HALVES,)),
        ]
        + stage_of(16),
        2 * UNIT,
        (coords, gains, attended, after, cot, share, grad_two, by_two, *held),
        aliases={8 + i: 3 + i for i in range(len(held))},
    )


def run_backward(coords, mask, normed, qkv, grad_att, held, split):
    rows = normed.shape[0]
    return call(
        functools.partial(attention_backward, len(held)),
        "attention_backward",
        [SMEM, whole(rows // GROUP, SLOTS, GROUP), whole(rows, D), whole(6, rows, STRIP), whole(rows, D)]
        + [ANY] * len(held),
        [(whole(6, rows, STRIP), shape_of(6, rows, STRIP))] + targets_of(((0,),), split),
        stage_of(48),
        7 * UNIT,
        (coords, mask, normed, qkv, grad_att, *held),
        aliases={5 + i: 1 + i for i in range(len(held))},
    )


def run_input(tok, gains, grad_mixed, grad_after, strips):
    rows = tok.shape[0]
    by_three = strips.reshape(HALVES, 32, 3, BLOCK, STRIP)
    return call(
        input_backward,
        "input_backward",
        [
            whole(rows, D),
            whole(2, D),
            pl.BlockSpec((3, rows, STRIP), lambda i: (i, 0, 0)),
            whole(rows, D),
            pl.BlockSpec((1, 8, 3, BLOCK, STRIP), lambda i: (i, 0, 0, 0, 0)),
        ],
        [
            (whole(rows, D), shape_of(rows, D, dtype=F32)),
            (whole(1, D), shape_of(1, D, dtype=F32)),
        ],
        [],
        3 * UNIT,
        (tok, gains, grad_mixed, grad_after, by_three),
        grid=(HALVES,),
    )


def to_strips(blocks):
    count = blocks.shape[0] // 4
    return blocks.reshape(count, 4, BLOCK, BLOCK).transpose(0, 2, 1, 3).reshape(count, BLOCK, STRIP)


def to_blocks(strips):
    count = strips.shape[0]
    return strips.reshape(count, BLOCK, 4, BLOCK).transpose(0, 2, 1, 3).reshape(-1, BLOCK, BLOCK)


EVERY = ("tensor", "dp")


def gather_weights(master):
    low = master.astype(BF16)
    own = low.shape[0]
    if own % 4 == 0:
        strips = to_strips(low).reshape(-1, STRIP)
        strips = lax.all_gather(strips, EVERY, axis=0, tiled=True)
        return strips.reshape(HALVES, STRIPS, BLOCK, STRIP)
    blocks = lax.all_gather(low, EVERY, axis=0, tiled=True)
    return to_strips(blocks).reshape(HALVES, STRIPS, BLOCK, STRIP)


def scatter_flat(strips, own):
    if own % 4 == 0:
        mine = lax.psum_scatter(
            strips.reshape(-1, STRIP), EVERY, scatter_dimension=0, tiled=True
        )
        return to_blocks(mine.reshape(-1, BLOCK, STRIP)).astype(F32)
    blocks = to_blocks(strips.reshape(-1, BLOCK, STRIP))
    return lax.psum_scatter(blocks, EVERY, scatter_dimension=0, tiled=True).astype(F32)


def added(left, right):
    return (left.astype(F32) + right.astype(F32)).astype(BF16)


def pick(array, index, axis):
    return lax.dynamic_index_in_dim(array, index, axis, keepdims=False)


OTHER_CORE = [(i, i ^ 1) for i in range(16)]
OTHER_X = [(i, i ^ 2) for i in range(16)]
OTHER_Y = [(0, 1), (1, 0)]
NEAR_Z = [(i, i ^ 4) for i in range(16)]
FAR_Z = [(i, i ^ 8) for i in range(16)]


def reduce_planes(kept, sent, place, half):
    total = added(kept, lax.ppermute(sent, "dp", OTHER_CORE))
    first, second = total[:, :, :, 0:3], total[:, :, :, 3:6]
    first_in = lax.ppermute(pick(first, 1 - half, 1), "tensor", OTHER_Y)
    second_in = lax.ppermute(pick(second, 1 - place, 2), "dp", OTHER_X)
    first = added(pick(first, half, 1), first_in)
    second = added(pick(second, place, 2), second_in)
    first_in = lax.ppermute(pick(first, 1 - place, 1), "dp", OTHER_X)
    second_in = lax.ppermute(pick(second, 1 - half, 1), "tensor", OTHER_Y)
    first = added(pick(first, place, 1), first_in)
    second = added(pick(second, half, 1), second_in)
    return jnp.concatenate([first, second], axis=1)


def near_sum(even_part, odd_part, plane):
    even = plane % 2 == 0
    arrived = lax.ppermute(jnp.where(even, odd_part, even_part), "dp", NEAR_Z)
    return added(jnp.where(even, even_part, odd_part), arrived)


def scatter_split(upper, one, zero, coords):
    place, plane, half = coords[1], coords[2], coords[3]
    upper = reduce_planes(*upper, place, half)
    high = near_sum(upper[0], upper[1], plane)
    one = reduce_planes(*one, place, half)
    zero = reduce_planes(*zero, place, half)
    low = near_sum(zero[0], one[0], plane)
    here = plane >= 2
    arrived = lax.ppermute(jnp.where(here, low, high), "dp", FAR_Z)
    return jnp.where(here, high, low).astype(F32) + arrived.astype(F32)


def body(
    tokens,
    token_mask,
    norm_gains,
    gain_moments,
    cotangent,
    master,
    stat_left,
    stat_right,
    root_left,
    root_right,
):
    rows = tokens.shape[0]
    own_caps = cotangent.shape[0]
    own = master.shape[0]
    split = lax.axis_size("dp") == 16 and lax.axis_size("tensor") == 2
    dp_pos, half = lax.axis_index("dp"), lax.axis_index("tensor")
    coords = jnp.stack([dp_pos % 2, dp_pos // 2 % 2, dp_pos // 4, half]).astype(jnp.int32)
    strips = gather_weights(master)
    group_mask = token_mask.astype(F32)
    own_mask = lax.dynamic_slice_in_dim(group_mask, half * own_caps, own_caps, 0)
    share = (own_mask / jnp.sum(own_mask, axis=1, keepdims=True)).reshape(rows, 1)
    mask = jnp.repeat(own_mask.reshape(rows // GROUP, CAPS, SLOTS), SLOTS, axis=1).swapaxes(1, 2)
    cot = cotangent.astype(F32)
    normed, qkv, attended, after, normed_two = run_forward(tokens, norm_gains, mask, strips)
    hidden, grad_two, *held = run_mlp(coords, normed_two, cot, share, strips, split)
    upper, held = (held[:2], held[2:]) if split else (None, held)
    grad_after, gain_two, grad_att, *held = run_output(
        coords, norm_gains, attended, after, cot, share, grad_two, strips, held, split
    )
    one, held = (held, []) if split else (None, held)
    grad_mixed, *held = run_backward(coords, mask, normed, qkv, grad_att, held, split)
    input_grad, gain_one = run_input(tokens, norm_gains, grad_mixed, grad_after, strips)
    pooled = run_mlp_out(after, hidden, share, strips)
    if split:
        grad_blocks = to_blocks(scatter_split(upper, one, held, coords))
    else:
        grad_blocks = scatter_flat(held[0], own)
    gain_part = jnp.concatenate([gain_one, gain_two], axis=0)
    gain_grads = lax.psum(gain_part, ("dp", "tensor"))
    moments_new = DECAY_RATE * gain_moments + (1.0 - DECAY_RATE) * gain_grads * gain_grads
    gains_new = norm_gains - GAIN_RATE * gain_grads / (jnp.sqrt(moments_new) + 1e-08)
    left_new = DECAY_RATE * stat_left + (1.0 - DECAY_RATE) * jnp.einsum(
        "nij,nkj->nik", grad_blocks, grad_blocks, precision=PRECISE
    )
    right_new = DECAY_RATE * stat_right + (1.0 - DECAY_RATE) * jnp.einsum(
        "nji,njk->nik", grad_blocks, grad_blocks, precision=PRECISE
    )
    right_side = jnp.einsum("nij,njk->nik", grad_blocks, root_right, precision=PRECISE)
    direction = jnp.einsum("nij,njk->nik", root_left, right_side, precision=PRECISE)
    master_new = master - STEP_RATE * direction
    return (
        pooled,
        input_grad,
        gain_grads,
        moments_new,
        gains_new,
        grad_blocks,
        left_new,
        right_new,
        master_new,
        master_new.astype(BF16),
    )


def solution(mesh):
    rows = P(("dp", "tensor"), None)
    blocks = P(("dp", "tensor"), None, None)
    return jax.shard_map(
        body,
        mesh=mesh,
        in_specs=(rows, P("dp", None), P(), P(), rows) + (blocks,) * 5,
        out_specs=(rows, rows, P(), P(), P()) + (blocks,) * 5,
        check_vma=False,
    )
```

```python
import functools

import jax
import jax.numpy as jnp
from jax import lax
from jax.experimental import pallas as pl
from jax.experimental.pallas import tpu as pltpu
from jax.sharding import PartitionSpec as P

D = 768
HEADS = 12
HD = 64
FF = 3072
BLOCK = 96
SLOTS = 16
HALVES = 2
STRIP = 4 * BLOCK
STRIPS = 96
OWN = 6
GROUP = 128
CAPS = GROUP // SLOTS
PAIR = 2 * HD

EPSILON = 1e-06
DECAY_RATE = 0.5
STEP_RATE = 0.25
GAIN_RATE = 0.3
MASKED_SCORE = -1e30
PRECISE = lax.Precision.HIGHEST
F32 = jnp.float32
BF16 = jnp.bfloat16


def mm(left, right, left_dim=1, right_dim=0):
    return lax.dot_general(
        left, right, (((left_dim,), (right_dim,)), ((), ())), preferred_element_type=F32
    )


def side_by_side(ref, lead, count):
    parts = [ref[lead + (slice(None), i)].reshape(-1, STRIP) for i in range(count)]
    return jnp.concatenate(parts, axis=1)


def norm_parts(values):
    center = values - jnp.mean(values, axis=-1, keepdims=True)
    inverse = lax.rsqrt(jnp.mean(center * center, axis=-1, keepdims=True) + EPSILON)
    return center * inverse, inverse


def norm_back(xhat, inverse, gain, grad):
    scaled = grad * gain
    return inverse * (
        scaled
        - jnp.mean(scaled, axis=-1, keepdims=True)
        - xhat * jnp.mean(scaled * xhat, axis=-1, keepdims=True)
    )


def split_pair(values):
    first = lax.broadcasted_iota(jnp.int32, (GROUP, PAIR), 1) < HD
    zero = jnp.zeros_like(values)
    return jnp.concatenate(
        [jnp.where(first, values, zero), jnp.where(first, zero, values)], axis=0
    )


def join_pair(stacked):
    first = lax.broadcasted_iota(jnp.int32, (GROUP, PAIR), 1) < HD
    return jnp.where(first, stacked[:GROUP], stacked[GROUP:])


def caption_of():
    return lax.broadcasted_iota(jnp.int32, (SLOTS, 2 * GROUP), 1) % GROUP // SLOTS


def compact(full, caption):
    kept = full[0:SLOTS]
    for i in range(1, CAPS):
        kept = jnp.where(caption == i, full[i * SLOTS : (i + 1) * SLOTS], kept)
    return kept


def expand(kept, caption):
    zero = jnp.zeros_like(kept)
    return jnp.concatenate(
        [jnp.where(caption == i, kept, zero).astype(BF16) for i in range(CAPS)], axis=0
    )


def pair_probs(queries, key_rows, bias, caption):
    scores = compact(mm(key_rows, queries, 1, 1), caption) * HD ** (-0.5) + bias
    shifted = jnp.exp(scores - jnp.max(scores, axis=0, keepdims=True))
    return shifted / jnp.sum(shifted, axis=0, keepdims=True)


def key_bias(mask):
    bias = jnp.where(mask > 0, 0.0, MASKED_SCORE)
    return jnp.concatenate([bias, bias], axis=1)


def span_of(i, size=GROUP):
    return pl.ds(pl.multiple_of(i * size, size), size)


def attention_forward(
    tok, gains, mask, by_three, by_two, normed, qkv, attended, after, normed_two, w_qkv, w_out, sems
):
    rows = tok.shape[0]
    copies = []
    for half in range(HALVES):
        copies.append(
            pltpu.make_async_copy(by_three.at[half, 0:8], w_qkv.at[half], sems.at[half])
        )
    for half in range(HALVES):
        copies.append(
            pltpu.make_async_copy(by_two.at[half, 12:16], w_out.at[half], sems.at[2 + half])
        )
    for copy in copies:
        copy.start()

    @pl.loop(0, rows // GROUP)
    def _(i):
        span = span_of(i)
        xhat, _ = norm_parts(tok[span, :].astype(F32))
        normed[span, :] = (xhat * gains[0:1, :]).astype(BF16)

    for half in range(HALVES):
        copies[half].wait()
        mixed = mm(normed[...], side_by_side(w_qkv, (half,), 3)).astype(BF16)
        for part in range(3):
            qkv[3 * half + part] = mixed[:, part * STRIP : (part + 1) * STRIP]

    @pl.loop(0, rows // GROUP)
    def _(i):
        span = span_of(i)
        bias = key_bias(mask[i])
        caption = caption_of()
        for half in range(HALVES):
            for pair in range(STRIP // PAIR):
                lanes = slice(pair * PAIR, (pair + 1) * PAIR)
                wide = slice(half * STRIP + pair * PAIR, half * STRIP + (pair + 1) * PAIR)
                probs = pair_probs(
                    split_pair(qkv[3 * half, span, lanes]),
                    qkv[3 * half + 1, span, lanes],
                    bias,
                    caption,
                )
                mixed = mm(expand(probs, caption), qkv[3 * half + 2, span, lanes], 0, 0)
                attended[span, wide] = join_pair(mixed).astype(BF16)

    copies[2].wait()
    copies[3].wait()
    weight = jnp.concatenate([side_by_side(w_out, (half,), 2) for half in range(HALVES)], axis=0)
    after[...] = mm(attended[...], weight)

    @pl.loop(0, rows // GROUP)
    def _(i):
        span = span_of(i)
        summed = tok[span, :].astype(F32) + after[span, :]
        after[span, :] = summed
        xhat, _ = norm_parts(summed)
        normed_two[span, :] = (xhat * gains[1:2, :]).astype(BF16)


GELU_A = 0.7978845608028654
GELU_B = 0.044715


def gelu_both(v):
    square = v * v
    inner = jnp.tanh(GELU_A * v * (1.0 + GELU_B * square))
    half_up = 0.5 * (1.0 + inner)
    slope = half_up + (0.5 * GELU_A) * v * (1.0 - inner * inner) * (1.0 + (3.0 * GELU_B) * square)
    return v * half_up, slope


class Emitter:
    def __init__(self, targets, runs, coords):
        self.core = coords[0]
        self.whole = targets[0] if len(targets) == 1 else None
        self.batches = [] if self.whole is not None else list(zip(runs, targets[0::2], targets[1::2]))

    def store(self, value, half, strip, planes):
        if self.whole is not None:
            self.whole[half, strip] = value
            return
        plane = strip // (4 * OWN)
        place = (strip // (2 * OWN)) % 2
        owner = (strip // OWN) % 2
        for run, kept, sent in self.batches:
            inside = [z for z in planes if z in run]
            if not inside:
                continue
            here = True if len(inside) == len(planes) else (plane >= run[0]) & (plane <= run[-1])
            spot = (plane - run[0], half, place, strip % OWN)

            @pl.when(here & (owner == self.core))
            def _():
                kept[spot] = value

            @pl.when(here & (owner != self.core))
            def _():
                sent[spot] = value


def mlp_both(coords, normed_two, out_low, w_up, w_down, *rest):
    hidden, grad_normed_two, *targets, grad_up = rest
    step = pl.program_id(0)
    rows = normed_two.shape[0]
    emit = Emitter(targets, ((2, 3), (1,)), coords)

    @pl.when(step == 0)
    def _():
        grad_normed_two[...] = jnp.zeros_like(grad_normed_two)

    up_weight = side_by_side(w_up, (0,), 2)
    down_weight = side_by_side(w_down, (0,), 2)
    chunk = 256
    for i in range(rows // chunk):
        span = slice(i * chunk, (i + 1) * chunk)
        act, slope = gelu_both(mm(normed_two[span, :], up_weight))
        hidden[step, span, :] = act.astype(BF16)
        grad = (mm(out_low[span, :], down_weight, 1, 1) * slope).astype(BF16)
        grad_up[span, :] = grad
        grad_normed_two[span, :] += mm(grad, up_weight, 1, 1)

    half = step // 2
    column = lax.rem(step, 2)
    down_grad = mm(hidden[step], out_low[...], 0, 0).astype(BF16)
    up_grad = mm(normed_two[...], grad_up[...], 0, 0).astype(BF16)
    for row in range(8):
        for part in range(2):
            block = slice(row * BLOCK, (row + 1) * BLOCK), slice(part * STRIP, (part + 1) * STRIP)
            emit.store(down_grad[block], half, 64 + 16 * column + 2 * row + part, (2, 3))
            planes = (1,) if row < 4 else (2,)
            emit.store(up_grad[block], half, 32 + 4 * row + 2 * column + part, planes)


def mlp_out(after, hidden, share, w_down, pooled, total):
    step = pl.program_id(0)
    rows = after.shape[0]
    product = mm(hidden[step], side_by_side(w_down, (0,), 2))

    @pl.when(step == 0)
    def _():
        total[...] = after[...] + product

    @pl.when(step > 0)
    def _():
        total[...] += product

    @pl.when(step == pl.num_programs(0) - 1)
    def _():
        @pl.loop(0, rows // GROUP)
        def _(i):
            weighted = (total[span_of(i), :] * share[span_of(i), :]).reshape(CAPS, SLOTS, D)
            pooled[span_of(i, CAPS), :] = jnp.sum(weighted, axis=1)


def output_backward(held, coords, gains, attended, after, grad_out, grad_normed_two, by_two, *rest):
    grad_after, gain_part, grad_att, *targets = rest[held:-3]
    after_low, w_out, weight_sem = rest[-3:]
    rows = after.shape[0]
    emit = Emitter(targets, ((1,),), coords)
    copies = [
        pltpu.make_async_copy(by_two.at[half, 12:16], w_out.at[half], weight_sem.at[half])
        for half in range(HALVES)
    ]
    for copy in copies:
        copy.start()
    gain_part[...] = jnp.zeros_like(gain_part)

    @pl.loop(0, rows // GROUP)
    def _(i):
        span = span_of(i)
        xhat, inverse = norm_parts(after[span, :])
        grad = grad_normed_two[span, :]
        gain_part[...] += jnp.sum(grad * xhat, axis=0, keepdims=True)
        value = grad_out[span, :] + norm_back(xhat, inverse, gains[1:2, :], grad)
        grad_after[span, :] = value
        after_low[span, :] = value.astype(BF16)

    for copy in copies:
        copy.wait()
    weight = jnp.concatenate([side_by_side(w_out, (half,), 2) for half in range(HALVES)], axis=0)
    grad_att[...] = mm(after_low[...], weight, 1, 1).astype(BF16)
    grad_w = mm(attended[...], after_low[...], 0, 0).astype(BF16)
    for half in range(HALVES):
        for row in range(4):
            for part in range(2):
                top = (4 * half + row) * BLOCK
                value = grad_w[top : top + BLOCK, part * STRIP : (part + 1) * STRIP]
                emit.store(value, half, 24 + 2 * row + part, (1,))


def attention_backward(held, coords, mask, normed, qkv, grad_att, *rest):
    grad_mixed, *targets = rest[held:]
    rows = normed.shape[0]
    emit = Emitter(targets, ((0,),), coords)

    @pl.loop(0, rows // GROUP)
    def _(i):
        span = span_of(i)
        bias = key_bias(mask[i])
        caption = caption_of()
        scale = HD ** (-0.5)
        for half in range(HALVES):
            for pair in range(STRIP // PAIR):
                lanes = slice(pair * PAIR, (pair + 1) * PAIR)
                wide = slice(half * STRIP + pair * PAIR, half * STRIP + (pair + 1) * PAIR)
                queries = split_pair(qkv[3 * half, span, lanes])
                key_rows = qkv[3 * half + 1, span, lanes]
                value_rows = qkv[3 * half + 2, span, lanes]
                probs = pair_probs(queries, key_rows, bias, caption)
                grads = split_pair(grad_att[span, wide])
                grad_probs = compact(mm(value_rows, grads, 1, 1), caption)
                inner = jnp.sum(probs * grad_probs, axis=0, keepdims=True)
                grad_scores = expand(probs * (grad_probs - inner), caption)
                grad_mixed[3 * half, span, lanes] = (
                    join_pair(mm(grad_scores, key_rows, 0, 0)) * scale
                ).astype(BF16)
                grad_mixed[3 * half + 1, span, lanes] = (mm(grad_scores, queries) * scale).astype(
                    BF16
                )
                grad_mixed[3 * half + 2, span, lanes] = mm(expand(probs, caption), grads).astype(
                    BF16
                )

    for half in range(HALVES):
        grads = jnp.concatenate([grad_mixed[3 * half + part] for part in range(3)], axis=1)
        grad_w = mm(normed[...], grads, 0, 0).astype(BF16)
        for row in range(8):
            for part in range(3):
                strip = 3 * row + part
                value = grad_w[row * BLOCK : (row + 1) * BLOCK, part * STRIP : (part + 1) * STRIP]
                emit.store(value, half, strip, (0,))


def input_backward(tok, gains, grad_mixed, grad_after, gain_two, w_qkv, input_grad, gain_part):
    half = pl.program_id(0)
    rows = tok.shape[0]
    grads = jnp.concatenate([grad_mixed[3 * half + part] for part in range(3)], axis=1)
    back = mm(grads, side_by_side(w_qkv, (0,), 3), 1, 1)

    @pl.when(half == 0)
    def _():
        input_grad[...] = back

    @pl.when(half == HALVES - 1)
    def _():
        input_grad[...] += back
        gain_part[0] = jnp.zeros_like(gain_two)
        gain_part[1] = gain_two[...]

        @pl.loop(0, rows // GROUP)
        def _(i):
            span = span_of(i)
            xhat, inverse = norm_parts(tok[span, :].astype(F32))
            grad = input_grad[span, :]
            gain_part[0] += jnp.sum(grad * xhat, axis=0, keepdims=True)
            input_grad[span, :] = grad_after[span, :] + norm_back(
                xhat, inverse, gains[0:1, :], grad
            )


def shape_of(*shape, dtype=BF16):
    return jax.ShapeDtypeStruct(shape, dtype)


HBM = pl.BlockSpec(memory_space=pl.ANY)
VMEM = pl.BlockSpec(memory_space=pltpu.VMEM)
SMEM = pl.BlockSpec(memory_space=pltpu.SMEM)


def call(kernel, name, in_specs, outs, scratch, flops, args, grid=(1,), aliases=None, mib=10):
    args = tuple(
        pltpu.with_memory_space_constraint(a, pltpu.HBM) if a.ndim == 5 else a for a in args
    )
    moved = sum(math_size(a.shape) * a.dtype.itemsize for a in args)
    moved += sum(math_size(s.shape) * s.dtype.itemsize for _, s in outs)
    return pl.pallas_call(
        kernel,
        grid=grid,
        in_specs=in_specs,
        out_specs=[spec for spec, _ in outs],
        out_shape=[shape for _, shape in outs],
        scratch_shapes=scratch,
        input_output_aliases=aliases or {},
        compiler_params=pltpu.CompilerParams(
            dimension_semantics=("arbitrary",) * len(grid), vmem_limit_bytes=mib << 20
        ),
        cost_estimate=pl.CostEstimate(flops=flops, bytes_accessed=moved, transcendentals=0),
        name=name,
    )(*args)


def math_size(shape):
    size = 1
    for extent in shape:
        size *= extent
    return size


UNIT = 2 * 768 * 768 * 768


def run_forward(tok, gains, mask, strips):
    rows = tok.shape[0]
    by_three = strips.reshape(HALVES, 32, 3, BLOCK, STRIP)
    by_two = strips.reshape(HALVES, 48, 2, BLOCK, STRIP)
    return call(
        attention_forward,
        "attention_forward",
        [VMEM, VMEM, VMEM, HBM, HBM],
        [
            (VMEM, shape_of(rows, D)),
            (VMEM, shape_of(6, rows, STRIP)),
            (VMEM, shape_of(rows, D)),
            (VMEM, shape_of(rows, D, dtype=F32)),
            (VMEM, shape_of(rows, D)),
        ],
        [
            pltpu.VMEM((HALVES, 8, 3, BLOCK, STRIP), BF16),
            pltpu.VMEM((HALVES, 4, 2, BLOCK, STRIP), BF16),
            pltpu.SemaphoreType.DMA((4,)),
        ],
        5 * UNIT,
        (tok, gains, mask, by_three, by_two),
        mib=10,
    )


def targets_of(runs, split):
    if split:
        shapes = [shape_of(len(run), HALVES, 2, OWN, BLOCK, STRIP) for run in runs for _ in range(2)]
    else:
        shapes = [shape_of(HALVES, STRIPS, BLOCK, STRIP)]
    return [(VMEM, shape) for shape in shapes]


def up_spec():
    return pl.BlockSpec((1, 8, 2, BLOCK, STRIP), lambda i: (i // 2, 1, i % 2, 0, 0))


def down_spec():
    return pl.BlockSpec((1, 8, 2, BLOCK, STRIP), lambda i: (i // 2, 4 + i % 2, 0, 0, 0))


def run_mlp(coords, normed_two, out_low, strips, split):
    rows = normed_two.shape[0]
    by_four = strips.reshape(HALVES, 24, 4, BLOCK, STRIP)
    by_two = strips.reshape(HALVES, 48, 2, BLOCK, STRIP)
    return call(
        mlp_both,
        "mlp_both",
        [SMEM, VMEM, VMEM, up_spec(), down_spec()],
        [(VMEM, shape_of(4, rows, D)), (VMEM, shape_of(rows, D, dtype=F32))]
        + targets_of(((2, 3), (1,)), split),
        [pltpu.VMEM((rows, D), BF16)],
        20 * UNIT,
        (coords, normed_two, out_low, by_four, by_two),
        grid=(4,),
        mib=16,
    )


def run_mlp_out(after, hidden, share, strips):
    rows = after.shape[0]
    by_two = strips.reshape(HALVES, 48, 2, BLOCK, STRIP)
    return call(
        mlp_out,
        "mlp_out",
        [VMEM, VMEM, VMEM, down_spec()],
        [(VMEM, shape_of(rows // SLOTS, D, dtype=F32))],
        [pltpu.VMEM((rows, D), F32)],
        4 * UNIT,
        (after, hidden, share, by_two),
        grid=(4,),
        mib=8,
    )[0]


def run_output(coords, gains, attended, after, grad_out, grad_two, strips, held, split):
    rows = after.shape[0]
    by_two = strips.reshape(HALVES, 48, 2, BLOCK, STRIP)
    return call(
        functools.partial(output_backward, len(held)),
        "output_backward",
        [SMEM, VMEM, VMEM, VMEM, VMEM, VMEM, HBM] + [VMEM] * len(held),
        [
            (VMEM, shape_of(rows, D, dtype=F32)),
            (VMEM, shape_of(1, D, dtype=F32)),
            (VMEM, shape_of(rows, D)),
        ]
        + targets_of(((1,),), split),
        [
            pltpu.VMEM((rows, D), BF16),
            pltpu.VMEM((HALVES, 4, 2, BLOCK, STRIP), BF16),
            pltpu.SemaphoreType.DMA((HALVES,)),
        ],
        2 * UNIT,
        (coords, gains, attended, after, grad_out, grad_two, by_two, *held),
        aliases={7 + i: 3 + i for i in range(len(held))},
        mib=12,
    )


def run_backward(coords, mask, normed, qkv, grad_att, held, split):
    rows = normed.shape[0]
    return call(
        functools.partial(attention_backward, len(held)),
        "attention_backward",
        [SMEM, VMEM, VMEM, VMEM, VMEM] + [VMEM] * len(held),
        [(VMEM, shape_of(6, rows, STRIP))] + targets_of(((0,),), split),
        [],
        7 * UNIT,
        (coords, mask, normed, qkv, grad_att, *held),
        aliases={5 + i: 1 + i for i in range(len(held))},
        mib=8,
    )


def run_input(tok, gains, grad_mixed, grad_after, gain_two, strips):
    rows = tok.shape[0]
    by_three = strips.reshape(HALVES, 32, 3, BLOCK, STRIP)
    return call(
        input_backward,
        "input_backward",
        [
            VMEM,
            VMEM,
            VMEM,
            VMEM,
            VMEM,
            pl.BlockSpec((1, 8, 3, BLOCK, STRIP), lambda i: (i, 0, 0, 0, 0)),
        ],
        [
            (VMEM, shape_of(rows, D, dtype=F32)),
            (VMEM, shape_of(2, 1, D, dtype=F32)),
        ],
        [],
        3 * UNIT,
        (tok, gains, grad_mixed, grad_after, gain_two, by_three),
        grid=(HALVES,),
        mib=10,
    )


def to_strips(blocks):
    count = blocks.shape[0] // 4
    return blocks.reshape(count, 4, BLOCK, BLOCK).transpose(0, 2, 1, 3).reshape(count, BLOCK, STRIP)


def to_blocks(strips):
    count = strips.shape[0]
    return strips.reshape(count, BLOCK, 4, BLOCK).transpose(0, 2, 1, 3).reshape(-1, BLOCK, BLOCK)


EVERY = ("tensor", "dp")


def gather_weights(master):
    low = master.astype(BF16)
    own = low.shape[0]
    if own % 4 == 0:
        strips = to_strips(low).reshape(-1, STRIP)
        strips = lax.all_gather(strips, EVERY, axis=0, tiled=True)
        return strips.reshape(HALVES, STRIPS, BLOCK, STRIP)
    blocks = lax.all_gather(low, EVERY, axis=0, tiled=True)
    return to_strips(blocks).reshape(HALVES, STRIPS, BLOCK, STRIP)


def scatter_flat(strips, own):
    if own % 4 == 0:
        mine = lax.psum_scatter(
            strips.reshape(-1, STRIP), EVERY, scatter_dimension=0, tiled=True
        )
        return to_blocks(mine.reshape(-1, BLOCK, STRIP)).astype(F32)
    blocks = to_blocks(strips.reshape(-1, BLOCK, STRIP))
    return lax.psum_scatter(blocks, EVERY, scatter_dimension=0, tiled=True).astype(F32)


def fence(*values):
    return lax.optimization_barrier(values)


OTHER_CORE = [(i, i ^ 1) for i in range(16)]
OTHER_X = [(i, i ^ 2) for i in range(16)]
OTHER_Y = [(0, 1), (1, 0)]


def by_plane(*moves):
    return [(4 * a + i, 4 * b + i) for a, b in moves for i in range(4)]


def split_sum(coords, kept, arrived, sent_one, sent_two, kept_one, kept_two):
    place, half = coords[1], coords[3]

    @pl.loop(0, 2 * kept.shape[0])
    def _(step):
        plane, i = step // 2, lax.rem(step, 2)
        one, two = pl.ds(0, 3), pl.ds(3, 3)
        sent_one[plane, i] = kept[plane, 1 - half, i, one] + arrived[plane, 1 - half, i, one]
        kept_one[plane, i] = kept[plane, half, i, one] + arrived[plane, half, i, one]
        sent_two[plane, i] = kept[plane, i, 1 - place, two] + arrived[plane, i, 1 - place, two]
        kept_two[plane, i] = kept[plane, i, place, two] + arrived[plane, i, place, two]


def split_again(coords, one, two, one_in, two_in, sent_one, sent_two, kept_one, kept_two):
    place, half = coords[1], coords[3]

    @pl.loop(0, one.shape[0])
    def _(plane):
        sent_one[plane] = one[plane, 1 - place] + one_in[plane, 1 - place]
        kept_one[plane] = one[plane, place] + one_in[plane, place]
        sent_two[plane] = two[plane, 1 - half] + two_in[plane, 1 - half]
        kept_two[plane] = two[plane, half] + two_in[plane, half]


def join_sum(coords, one, two, one_in, two_in, *outs):
    for i, out in enumerate(outs):
        plane = 0 if len(outs) == 1 else lax.rem(coords[2] + i, 2)
        out[0:3] = one[plane] + one_in[plane]
        out[3:6] = two[plane] + two_in[plane]


def sum_of(left, right, out):
    @pl.loop(0, left.shape[0])
    def _(i):
        out[i] = left[i] + right[i]


def run_split(coords, kept, arrived):
    shape = shape_of(kept.shape[0], 2, 3, BLOCK, STRIP)
    outs = call(
        split_sum,
        "split_sum",
        [SMEM, VMEM, VMEM],
        [(VMEM, shape)] * 4,
        [],
        math_size(kept.shape),
        (coords, kept, arrived),
        mib=4,
    )
    return outs[:2], outs[2:]


def run_again(coords, kept, arrived):
    shape = shape_of(kept[0].shape[0], 3, BLOCK, STRIP)
    outs = call(
        split_again,
        "split_again",
        [SMEM] + [VMEM] * 4,
        [(VMEM, shape)] * 4,
        [],
        2 * math_size(kept[0].shape),
        (coords, *kept, *arrived),
        mib=4,
    )
    return outs[:2], outs[2:]


def run_join(coords, kept, arrived):
    return call(
        join_sum,
        "join_sum",
        [SMEM] + [VMEM] * 4,
        [(VMEM, shape_of(OWN, BLOCK, STRIP))] * kept[0].shape[0],
        [],
        2 * math_size(kept[0].shape),
        (coords, *kept, *arrived),
        mib=4,
    )


def run_sum(left, right):
    return call(
        sum_of,
        "sum_of",
        [VMEM] * 2,
        [(VMEM, jax.ShapeDtypeStruct(left.shape, left.dtype))],
        [],
        math_size(left.shape),
        (left, right),
        mib=4,
    )[0]


def core_hop(sent):
    return lax.ppermute(sent, "dp", OTHER_CORE)


def first_hop(sent):
    return lax.ppermute(sent[0], "tensor", OTHER_Y), lax.ppermute(sent[1], "dp", OTHER_X)


def second_hop(sent):
    return lax.ppermute(sent[0], "dp", OTHER_X), lax.ppermute(sent[1], "tensor", OTHER_Y)


def precise(left, right, left_dim=1, right_dim=0):
    left_high, right_high = left.astype(BF16), right.astype(BF16)
    left_low = (left - left_high.astype(F32)).astype(BF16)
    right_low = (right - right_high.astype(F32)).astype(BF16)
    small = mm(left_high, right_low, left_dim, right_dim) + mm(
        left_low, right_high, left_dim, right_dim
    )
    return mm(left_high, right_high, left_dim, right_dim) + small


def update(
    coords, high, high_in, one, one_in, zero, zero_in, master, stat_left, stat_right, root_left, root_right, *outs
):
    grad_out, left_out, right_out, master_out, copy_out, grad = outs
    plane = coords[2]
    strip = pl.program_id(0)
    for condition, own, arrived in (
        (plane >= 2, high, high_in),
        (plane == 1, one, one_in),
        (plane == 0, zero, zero_in),
    ):

        @pl.when(condition)
        def _():
            grad[...] = own[strip].astype(F32) + arrived[strip].astype(F32)

    for i in range(4):
        block = 4 * strip + i
        g = grad[:, i * BLOCK : (i + 1) * BLOCK]
        grad_out[i] = g
        left_out[i] = DECAY_RATE * stat_left[block] + (1.0 - DECAY_RATE) * precise(g, g, 1, 1)
        right_out[i] = DECAY_RATE * stat_right[block] + (1.0 - DECAY_RATE) * precise(g, g, 0, 0)
        direction = precise(root_left[block], precise(g, root_right[block]))
        new = master[block] - STEP_RATE * direction
        master_out[i] = new
        copy_out[i] = new.astype(BF16)


def run_update(coords, sums, blocks):
    count = blocks[0].shape[0]
    tile = pl.BlockSpec((4, BLOCK, BLOCK), lambda i: (i, 0, 0))
    shape = shape_of(count, BLOCK, BLOCK, dtype=F32)
    return call(
        update,
        "update",
        [SMEM] + [VMEM] * (len(sums) + len(blocks)),
        [(tile, shape)] * 4 + [(tile, shape_of(count, BLOCK, BLOCK))],
        [pltpu.VMEM((BLOCK, STRIP), F32)],
        12 * 2 * count * BLOCK**3,
        (coords, *sums, *blocks),
        grid=(count // 4,),
        mib=12,
    )


def sum_hops():
    hops = []
    for axis in ("tensor", "dp"):
        size, step = lax.axis_size(axis), 1
        while step < size:
            hops.append((axis, [(i, i ^ step) for i in range(size)]))
            step *= 2
    return hops


def add_hop(value, hop):
    return run_sum(value, lax.ppermute(value, *hop))


def plain_update(grad, master, stat_left, stat_right, root_left, root_right):
    left_new = DECAY_RATE * stat_left + (1.0 - DECAY_RATE) * jnp.einsum(
        "nij,nkj->nik", grad, grad, precision=PRECISE
    )
    right_new = DECAY_RATE * stat_right + (1.0 - DECAY_RATE) * jnp.einsum(
        "nji,njk->nik", grad, grad, precision=PRECISE
    )
    right_side = jnp.einsum("nij,njk->nik", grad, root_right, precision=PRECISE)
    direction = jnp.einsum("nij,njk->nik", root_left, right_side, precision=PRECISE)
    master_new = master - STEP_RATE * direction
    return grad, left_new, right_new, master_new, master_new.astype(BF16)


def body(
    tokens,
    token_mask,
    norm_gains,
    gain_moments,
    cotangent,
    master,
    stat_left,
    stat_right,
    root_left,
    root_right,
):
    rows = tokens.shape[0]
    own_caps = cotangent.shape[0]
    own = master.shape[0]
    split = lax.axis_size("dp") == 16 and lax.axis_size("tensor") == 2
    dp_pos, half = lax.axis_index("dp"), lax.axis_index("tensor")
    coords = jnp.stack([dp_pos % 2, dp_pos // 2 % 2, dp_pos // 4, half]).astype(jnp.int32)
    strips = gather_weights(master)
    group_mask = token_mask.astype(F32)
    own_mask = lax.dynamic_slice_in_dim(group_mask, half * own_caps, own_caps, 0)
    share = (own_mask / jnp.sum(own_mask, axis=1, keepdims=True)).reshape(rows, 1)
    mask = jnp.repeat(own_mask.reshape(rows // GROUP, CAPS, SLOTS), SLOTS, axis=1).swapaxes(1, 2)
    cot = cotangent.astype(F32)
    grad_out = (cot[:, None, :] * share.reshape(own_caps, SLOTS, 1)).reshape(rows, D)
    out_low = grad_out.astype(BF16)
    normed, qkv, attended, after, normed_two = run_forward(tokens, norm_gains, mask, strips)
    hidden, grad_two, *held = run_mlp(coords, normed_two, out_low, strips, split)
    hops = sum_hops()
    blocks = (master, stat_left, stat_right, root_left, root_right)
    if not split:
        grad_after, gain_two, grad_att, *held = run_output(
            coords, norm_gains, attended, after, grad_out, grad_two, strips, held, split
        )
        grad_mixed, *held = run_backward(coords, mask, normed, qkv, grad_att, held, split)
        input_grad, gain_grads = run_input(
            tokens, norm_gains, grad_mixed, grad_after, gain_two, strips
        )
        pooled = run_mlp_out(after, hidden, share, strips)
        for hop in hops:
            gain_grads = add_hop(gain_grads, hop)
        updated = plain_update(scatter_flat(held[0], own), *blocks)
    else:
        upper_kept, upper_sent, one_kept, one_sent = held
        upper_in = core_hop(upper_sent)
        grad_after, gain_two, grad_att, *one = run_output(
            coords, norm_gains, attended, after, grad_out, grad_two, strips, (one_kept, one_sent), split
        )
        upper_in, grad_att, one = fence(upper_in, grad_att, one)

        upper_sent, upper_kept = run_split(coords, upper_kept, upper_in)
        upper_sent, grad_att, one = fence(upper_sent, grad_att, one)
        upper_in = first_hop(upper_sent)
        one_in = core_hop(one[1])
        grad_mixed, *zero = run_backward(coords, mask, normed, qkv, grad_att, [], split)
        upper_in, one_in, grad_mixed, zero = fence(upper_in, one_in, grad_mixed, zero)

        upper_sent, upper_kept = run_again(coords, upper_kept, upper_in)
        one_sent, one_kept = run_split(coords, one[0], one_in)
        upper_sent, one_sent, zero, grad_mixed = fence(upper_sent, one_sent, zero, grad_mixed)
        zero_in = core_hop(zero[1])
        upper_in = second_hop(upper_sent)
        one_in = first_hop(one_sent)
        input_grad, gain_grads = run_input(
            tokens, norm_gains, grad_mixed, grad_after, gain_two, strips
        )
        zero_in, gain_grads, hidden = fence(zero_in, gain_grads, hidden)

        zero_sent, zero_kept = run_split(coords, zero[0], zero_in)
        zero_sent, gain_grads, hidden = fence(zero_sent, gain_grads, hidden)
        zero_in = first_hop(zero_sent)
        gain_grads = add_hop(gain_grads, hops[0])
        pooled = run_mlp_out(after, hidden, share, strips)
        upper_in, one_in, gain_grads, pooled = fence(upper_in, one_in, gain_grads, pooled)

        one_sent, one_kept = run_again(coords, one_kept, one_in)
        one_in = second_hop(one_sent)
        high, other = run_join(coords, upper_kept, upper_in)
        high_in = lax.ppermute(other, "dp", by_plane((0, 1), (1, 0), (2, 3), (3, 2)))
        gain_grads = add_hop(gain_grads, hops[1])
        zero_in, one_in, high_in, gain_grads = fence(zero_in, one_in, high_in, gain_grads)

        zero_sent, zero_kept = run_again(coords, zero_kept, zero_in)
        zero_in = second_hop(zero_sent)
        (one_sum,) = run_join(coords, one_kept, one_in)
        one_in = lax.ppermute(one_sum, "dp", by_plane((0, 1), (2, 3)))
        high = run_sum(high, high_in)
        high_in = lax.ppermute(high, "dp", by_plane((0, 2), (1, 3)))
        gain_grads = add_hop(gain_grads, hops[2])
        zero_in, one_in, gain_grads = fence(zero_in, one_in, gain_grads)

        (zero_sum,) = run_join(coords, zero_kept, zero_in)
        zero_in = lax.ppermute(zero_sum, "dp", by_plane((1, 0), (3, 2)))
        one_sum = run_sum(one_sum, one_in)
        one_in = lax.ppermute(one_sum, "dp", by_plane((3, 1)))
        gain_grads = add_hop(gain_grads, hops[3])
        zero_in, high_in, gain_grads = fence(zero_in, high_in, gain_grads)

        zero_sum = run_sum(zero_sum, zero_in)
        zero_in = lax.ppermute(zero_sum, "dp", by_plane((2, 0)))
        gain_grads = add_hop(gain_grads, hops[4])
        updated = run_update(coords, (high, high_in, one_sum, one_in, zero_sum, zero_in), blocks)
    gain_grads = gain_grads.reshape(2, D)
    moments_new = DECAY_RATE * gain_moments + (1.0 - DECAY_RATE) * gain_grads * gain_grads
    gains_new = norm_gains - GAIN_RATE * gain_grads / (jnp.sqrt(moments_new) + 1e-08)
    return (pooled, input_grad, gain_grads, moments_new, gains_new, *updated)


def solution(mesh):
    rows = P(("dp", "tensor"), None)
    blocks = P(("dp", "tensor"), None, None)
    return jax.shard_map(
        body,
        mesh=mesh,
        in_specs=(rows, P("dp", None), P(), P(), rows) + (blocks,) * 5,
        out_specs=(rows, rows, P(), P(), P()) + (blocks,) * 5,
        check_vma=False,
    )
```

```python
import functools

import jax
import jax.numpy as jnp
from jax import lax
from jax.experimental import pallas as pl
from jax.experimental.pallas import tpu as pltpu
from jax.sharding import PartitionSpec as P

D = 768
HEADS = 12
HD = 64
FF = 3072
BLOCK = 96
SLOTS = 16
HALVES = 2
STRIP = 4 * BLOCK
STRIPS = 96
OWN = 6
GROUP = 128
CAPS = GROUP // SLOTS
UPPER = (2, 3)
LOWER = (0, 1)
PAIR = 2 * HD

EPSILON = 1e-06
DECAY_RATE = 0.5
STEP_RATE = 0.25
GAIN_RATE = 0.3
MASKED_SCORE = -1e30
PRECISE = lax.Precision.HIGHEST
F32 = jnp.float32
BF16 = jnp.bfloat16


def mm(left, right, left_dim=1, right_dim=0):
    return lax.dot_general(
        left, right, (((left_dim,), (right_dim,)), ((), ())), preferred_element_type=F32
    )


def weight_of(ref, half, rows, columns):
    parts = [ref[half, rows, column].reshape(-1, STRIP) for column in columns]
    return jnp.concatenate(parts, axis=1)


def out_weight(by_two):
    halves = [weight_of(by_two, half, slice(12, 16), (0, 1)) for half in range(HALVES)]
    return jnp.concatenate(halves, axis=0)


def norm_parts(values):
    center = values - jnp.mean(values, axis=-1, keepdims=True)
    inverse = lax.rsqrt(jnp.mean(center * center, axis=-1, keepdims=True) + EPSILON)
    return center * inverse, inverse


def norm_back(xhat, inverse, gain, grad):
    scaled = grad * gain
    return inverse * (
        scaled
        - jnp.mean(scaled, axis=-1, keepdims=True)
        - xhat * jnp.mean(scaled * xhat, axis=-1, keepdims=True)
    )


def split_pair(values):
    first = lax.broadcasted_iota(jnp.int32, (GROUP, PAIR), 1) < HD
    zero = jnp.zeros_like(values)
    return jnp.concatenate(
        [jnp.where(first, values, zero), jnp.where(first, zero, values)], axis=0
    )


def join_pair(stacked):
    first = lax.broadcasted_iota(jnp.int32, (GROUP, PAIR), 1) < HD
    return jnp.where(first, stacked[:GROUP], stacked[GROUP:])


def caption_of():
    return lax.broadcasted_iota(jnp.int32, (SLOTS, 2 * GROUP), 1) % GROUP // SLOTS


def compact(full, caption):
    kept = full[0:SLOTS]
    for i in range(1, CAPS):
        kept = jnp.where(caption == i, full[i * SLOTS : (i + 1) * SLOTS], kept)
    return kept


def expand(kept, caption):
    zero = jnp.zeros_like(kept)
    return jnp.concatenate(
        [jnp.where(caption == i, kept, zero).astype(BF16) for i in range(CAPS)], axis=0
    )


def pair_probs(queries, key_rows, bias, caption):
    scores = compact(mm(key_rows, queries, 1, 1), caption) * HD ** (-0.5) + bias
    shifted = jnp.exp(scores - jnp.max(scores, axis=0, keepdims=True))
    return shifted / jnp.sum(shifted, axis=0, keepdims=True)


def key_bias(mask):
    bias = jnp.where(mask > 0, 0.0, MASKED_SCORE)
    return jnp.concatenate([bias, bias], axis=1)


def span_of(i, size=GROUP):
    return pl.ds(pl.multiple_of(i * size, size), size)


def pool(values, share):
    parts = [
        values[:, i : i + PAIR] * share for i in range(0, values.shape[1], PAIR)
    ]
    weighted = jnp.concatenate(parts, axis=1)
    return jnp.sum(weighted.reshape(-1, SLOTS, values.shape[1]), axis=1)


def attention_forward(
    tok, gains, mask, share, by_three, by_two, normed, qkv, attended, after, normed_two, after_pooled
):
    rows = tok.shape[0]

    @pl.loop(0, rows // GROUP)
    def _(i):
        span = span_of(i)
        xhat, _ = norm_parts(tok[span, :].astype(F32))
        normed[span, :] = (xhat * gains[0:1, :]).astype(BF16)

    for half in range(HALVES):
        mixed = mm(normed[...], weight_of(by_three, half, slice(0, 8), range(3))).astype(BF16)
        for part in range(3):
            qkv[3 * half + part] = mixed[:, part * STRIP : (part + 1) * STRIP]

    @pl.loop(0, rows // GROUP)
    def _(i):
        span = span_of(i)
        bias = key_bias(mask[i])
        caption = caption_of()
        for half in range(HALVES):
            for pair in range(STRIP // PAIR):
                lanes = slice(pair * PAIR, (pair + 1) * PAIR)
                wide = slice(half * STRIP + pair * PAIR, half * STRIP + (pair + 1) * PAIR)
                probs = pair_probs(
                    split_pair(qkv[3 * half, span, lanes]),
                    qkv[3 * half + 1, span, lanes],
                    bias,
                    caption,
                )
                mixed = mm(expand(probs, caption), qkv[3 * half + 2, span, lanes], 0, 0)
                attended[span, wide] = join_pair(mixed).astype(BF16)

    after[...] = mm(attended[...], out_weight(by_two))

    @pl.loop(0, rows // GROUP)
    def _(i):
        span = span_of(i)
        summed = tok[span, :].astype(F32) + after[span, :]
        after[span, :] = summed
        after_pooled[span_of(i, CAPS), :] = pool(summed, share[span, :])
        xhat, _ = norm_parts(summed)
        normed_two[span, :] = (xhat * gains[1:2, :]).astype(BF16)


GELU_A = 0.7978845608028654
GELU_B = 0.044715


def gelu_both(v):
    square = v * v
    inner = jnp.tanh(GELU_A * v * (1.0 + GELU_B * square))
    half_up = 0.5 * (1.0 + inner)
    slope = half_up + (0.5 * GELU_A) * v * (1.0 - inner * inner) * (1.0 + (3.0 * GELU_B) * square)
    return v * half_up, slope


class Emitter:
    def __init__(self, targets, runs, coords):
        self.core = coords[0]
        self.whole = targets[0] if len(targets) == 1 else None
        self.batches = [] if self.whole is not None else list(zip(runs, targets[0::2], targets[1::2]))

    def store(self, value, half, strip, planes):
        if self.whole is not None:
            self.whole[half, strip] = value
            return
        plane = strip // (4 * OWN)
        place = (strip // (2 * OWN)) % 2
        owner = (strip // OWN) % 2
        for run, kept, sent in self.batches:
            inside = [z for z in planes if z in run]
            if not inside:
                continue
            here = len(inside) == len(planes) or (plane >= run[0]) & (plane <= run[-1])
            spot = (plane - run[0], half, place, strip % OWN)

            @pl.when(here & (owner == self.core))
            def _():
                kept[spot] = value

            @pl.when(here & (owner != self.core))
            def _():
                sent[spot] = value


def mlp_both(coords, normed_two, out_low, share, by_four, by_two, *rest):
    hidden_pooled, grad_normed_two, *targets, hidden, grad_up = rest
    step = pl.program_id(0)
    rows = normed_two.shape[0]
    emit = Emitter(targets, (UPPER, LOWER), coords)
    half = step // 2
    column = lax.rem(step, 2)

    @pl.when(step == 0)
    def _():
        grad_normed_two[...] = jnp.zeros_like(grad_normed_two)

    up_weight = weight_of(by_four, half, slice(8, 16), (2 * column, 2 * column + 1))
    down_weight = weight_of(by_two, half, pl.ds(32 + 8 * column, 8), (0, 1))
    chunk = 256
    for i in range(rows // chunk):
        span = slice(i * chunk, (i + 1) * chunk)
        act, slope = gelu_both(mm(normed_two[span, :], up_weight))
        act = act.astype(BF16)
        hidden[span, :] = act
        caps = slice(i * chunk // SLOTS, (i + 1) * chunk // SLOTS)
        hidden_pooled[step, caps, :] = pool(act.astype(F32), share[span, :])
        grad = (mm(out_low[span, :], down_weight, 1, 1) * slope).astype(BF16)
        grad_up[span, :] = grad
        grad_normed_two[span, :] += mm(grad, up_weight, 1, 1)

    down_grad = mm(hidden[...], out_low[...], 0, 0).astype(BF16)
    up_grad = mm(normed_two[...], grad_up[...], 0, 0).astype(BF16)
    for row in range(8):
        for part in range(2):
            block = slice(row * BLOCK, (row + 1) * BLOCK), slice(part * STRIP, (part + 1) * STRIP)
            emit.store(down_grad[block], half, 64 + 16 * column + 2 * row + part, (2, 3))
            planes = (1,) if row < 4 else (2,)
            emit.store(up_grad[block], half, 32 + 4 * row + 2 * column + part, planes)


def pool_out(after_pooled, hidden_pooled, by_two, pooled):
    pooled[...] = after_pooled[...]
    for step in range(4):
        value = hidden_pooled[step]
        high = value.astype(BF16)
        low = (value - high.astype(F32)).astype(BF16)
        start = 32 + 8 * (step % 2)
        weight = weight_of(by_two, step // 2, slice(start, start + 8), (0, 1))
        both = mm(jnp.concatenate([high, low], axis=0), weight)
        pooled[...] += both[: value.shape[0]] + both[value.shape[0] :]


def output_backward(held, coords, gains, attended, after, grad_out, grad_normed_two, by_two, *rest):
    grad_after, gain_part, grad_att, *targets, after_low = rest[held:]
    rows = after.shape[0]
    emit = Emitter(targets, (LOWER,), coords)
    gain_part[...] = jnp.zeros_like(gain_part)

    @pl.loop(0, rows // GROUP)
    def _(i):
        span = span_of(i)
        xhat, inverse = norm_parts(after[span, :])
        grad = grad_normed_two[span, :]
        gain_part[...] += jnp.sum(grad * xhat, axis=0, keepdims=True)
        value = grad_out[span, :] + norm_back(xhat, inverse, gains[1:2, :], grad)
        grad_after[span, :] = value
        after_low[span, :] = value.astype(BF16)

    grad_att[...] = mm(after_low[...], out_weight(by_two), 1, 1).astype(BF16)
    grad_w = mm(attended[...], after_low[...], 0, 0).astype(BF16)
    for half in range(HALVES):
        for row in range(4):
            for part in range(2):
                top = (4 * half + row) * BLOCK
                value = grad_w[top : top + BLOCK, part * STRIP : (part + 1) * STRIP]
                emit.store(value, half, 24 + 2 * row + part, (1,))


def attention_backward(held, coords, mask, normed, qkv, grad_att, *rest):
    grad_mixed, *targets = rest[held:]
    rows = normed.shape[0]
    emit = Emitter(targets, (LOWER,), coords)

    @pl.loop(0, rows // GROUP)
    def _(i):
        span = span_of(i)
        bias = key_bias(mask[i])
        caption = caption_of()
        scale = HD ** (-0.5)
        for half in range(HALVES):
            for pair in range(STRIP // PAIR):
                lanes = slice(pair * PAIR, (pair + 1) * PAIR)
                wide = slice(half * STRIP + pair * PAIR, half * STRIP + (pair + 1) * PAIR)
                queries = split_pair(qkv[3 * half, span, lanes])
                key_rows = qkv[3 * half + 1, span, lanes]
                value_rows = qkv[3 * half + 2, span, lanes]
                probs = pair_probs(queries, key_rows, bias, caption)
                grads = split_pair(grad_att[span, wide])
                grad_probs = compact(mm(value_rows, grads, 1, 1), caption)
                inner = jnp.sum(probs * grad_probs, axis=0, keepdims=True)
                grad_scores = expand(probs * (grad_probs - inner), caption)
                grad_mixed[3 * half, span, lanes] = (
                    join_pair(mm(grad_scores, key_rows, 0, 0)) * scale
                ).astype(BF16)
                grad_mixed[3 * half + 1, span, lanes] = (mm(grad_scores, queries) * scale).astype(
                    BF16
                )
                grad_mixed[3 * half + 2, span, lanes] = mm(expand(probs, caption), grads).astype(
                    BF16
                )

    for half in range(HALVES):
        grads = jnp.concatenate([grad_mixed[3 * half + part] for part in range(3)], axis=1)
        grad_w = mm(normed[...], grads, 0, 0).astype(BF16)
        for row in range(8):
            for part in range(3):
                strip = 3 * row + part
                value = grad_w[row * BLOCK : (row + 1) * BLOCK, part * STRIP : (part + 1) * STRIP]
                emit.store(value, half, strip, (0,))


def input_backward(tok, gains, grad_mixed, grad_after, gain_two, by_three, input_grad, gain_part):
    rows = tok.shape[0]
    grads = jnp.concatenate([grad_mixed[part] for part in range(6)], axis=1)
    halves = [weight_of(by_three, half, slice(0, 8), range(3)) for half in range(HALVES)]
    input_grad[...] = mm(grads, jnp.concatenate(halves, axis=1), 1, 1)
    gain_part[0] = jnp.zeros_like(gain_two)
    gain_part[1] = gain_two[...]

    @pl.loop(0, rows // GROUP)
    def _(i):
        span = span_of(i)
        xhat, inverse = norm_parts(tok[span, :].astype(F32))
        grad = input_grad[span, :]
        gain_part[0] += jnp.sum(grad * xhat, axis=0, keepdims=True)
        input_grad[span, :] = grad_after[span, :] + norm_back(xhat, inverse, gains[0:1, :], grad)


def shape_of(*shape, dtype=BF16):
    return jax.ShapeDtypeStruct(shape, dtype)


VMEM = pl.BlockSpec(memory_space=pltpu.VMEM)
SMEM = pl.BlockSpec(memory_space=pltpu.SMEM)


def call(kernel, name, in_specs, outs, scratch, flops, args, grid=(1,), aliases=None, mib=10):
    moved = sum(math_size(a.shape) * a.dtype.itemsize for a in args)
    moved += sum(math_size(s.shape) * s.dtype.itemsize for _, s in outs)
    return pl.pallas_call(
        kernel,
        grid=grid,
        in_specs=in_specs,
        out_specs=[spec for spec, _ in outs],
        out_shape=[shape for _, shape in outs],
        scratch_shapes=scratch,
        input_output_aliases=aliases or {},
        compiler_params=pltpu.CompilerParams(
            dimension_semantics=("arbitrary",) * len(grid), vmem_limit_bytes=mib << 20
        ),
        cost_estimate=pl.CostEstimate(flops=1, bytes_accessed=1, transcendentals=0),
        name=name,
    )(*args)


def math_size(shape):
    size = 1
    for extent in shape:
        size *= extent
    return size


UNIT = 2 * 768 * 768 * 768


def by_count(strips, count):
    return strips.reshape(HALVES, STRIPS // count, count, BLOCK, STRIP)


def run_forward(tok, gains, mask, share, strips):
    rows = tok.shape[0]
    return call(
        attention_forward,
        "attention_forward",
        [VMEM] * 6,
        [
            (VMEM, shape_of(rows, D)),
            (VMEM, shape_of(6, rows, STRIP)),
            (VMEM, shape_of(rows, D)),
            (VMEM, shape_of(rows, D, dtype=F32)),
            (VMEM, shape_of(rows, D)),
            (VMEM, shape_of(rows // SLOTS, D, dtype=F32)),
        ],
        [],
        5 * UNIT,
        (tok, gains, mask, share, by_count(strips, 3), by_count(strips, 2)),
        mib=3,
    )


def targets_of(runs, split):
    if split:
        shapes = [shape_of(len(run), HALVES, 2, OWN, BLOCK, STRIP) for run in runs for _ in range(2)]
    else:
        shapes = [shape_of(HALVES, STRIPS, BLOCK, STRIP)]
    return [(VMEM, shape) for shape in shapes]


def run_mlp(coords, normed_two, out_low, share, strips, split):
    rows = normed_two.shape[0]
    return call(
        mlp_both,
        "mlp_both",
        [SMEM] + [VMEM] * 5,
        [
            (VMEM, shape_of(4, rows // SLOTS, D, dtype=F32)),
            (VMEM, shape_of(rows, D, dtype=F32)),
        ]
        + targets_of((UPPER, LOWER), split),
        [pltpu.VMEM((rows, D), BF16), pltpu.VMEM((rows, D), BF16)],
        20 * UNIT,
        (coords, normed_two, out_low, share, by_count(strips, 4), by_count(strips, 2)),
        grid=(4,),
        mib=7,
    )


def run_pool(after_pooled, hidden_pooled, strips):
    return call(
        pool_out,
        "pool_out",
        [VMEM] * 3,
        [(VMEM, jax.ShapeDtypeStruct(after_pooled.shape, F32))],
        [],
        UNIT // 2,
        (after_pooled, hidden_pooled, by_count(strips, 2)),
        mib=4,
    )[0]


def run_output(coords, gains, attended, after, grad_out, grad_two, strips, held, split):
    rows = after.shape[0]
    return call(
        functools.partial(output_backward, len(held)),
        "output_backward",
        [SMEM] + [VMEM] * (6 + len(held)),
        [
            (VMEM, shape_of(rows, D, dtype=F32)),
            (VMEM, shape_of(1, D, dtype=F32)),
            (VMEM, shape_of(rows, D)),
        ]
        + targets_of((LOWER,), split),
        [pltpu.VMEM((rows, D), BF16)],
        2 * UNIT,
        (coords, gains, attended, after, grad_out, grad_two, by_count(strips, 2), *held),
        aliases={7 + i: 3 + i for i in range(len(held))},
        mib=6,
    )


def run_backward(coords, mask, normed, qkv, grad_att, held, split):
    rows = normed.shape[0]
    return call(
        functools.partial(attention_backward, len(held)),
        "attention_backward",
        [SMEM, VMEM, VMEM, VMEM, VMEM] + [VMEM] * len(held),
        [(VMEM, shape_of(6, rows, STRIP))] + targets_of((LOWER,), split),
        [],
        7 * UNIT,
        (coords, mask, normed, qkv, grad_att, *held),
        aliases={5 + i: 1 + i for i in range(len(held))},
        mib=6,
    )


def run_input(tok, gains, grad_mixed, grad_after, gain_two, strips):
    rows = tok.shape[0]
    return call(
        input_backward,
        "input_backward",
        [VMEM] * 6,
        [(VMEM, shape_of(rows, D, dtype=F32)), (VMEM, shape_of(2, 1, D, dtype=F32))],
        [],
        3 * UNIT,
        (tok, gains, grad_mixed, grad_after, gain_two, by_count(strips, 3)),
        mib=5,
    )


def to_strips(blocks):
    count = blocks.shape[0] // 4
    return blocks.reshape(count, 4, BLOCK, BLOCK).transpose(0, 2, 1, 3).reshape(count, BLOCK, STRIP)


def to_blocks(strips):
    count = strips.shape[0]
    return strips.reshape(count, BLOCK, 4, BLOCK).transpose(0, 2, 1, 3).reshape(-1, BLOCK, BLOCK)


EVERY = ("tensor", "dp")


def gather_weights(master):
    low = master.astype(BF16)
    own = low.shape[0]
    if own % 4 == 0:
        strips = to_strips(low).reshape(-1, STRIP)
        strips = lax.all_gather(strips, EVERY, axis=0, tiled=True)
        return strips.reshape(HALVES, STRIPS, BLOCK, STRIP)
    blocks = lax.all_gather(low, EVERY, axis=0, tiled=True)
    return to_strips(blocks).reshape(HALVES, STRIPS, BLOCK, STRIP)


def pack(master, out):
    for strip in range(master.shape[0] // 4):
        parts = [master[4 * strip + i].astype(BF16) for i in range(4)]
        out[0, strip] = jnp.concatenate(parts, axis=1)


def take_halves(by_x, by_y, from_x, from_y):
    for plane in range(by_x.shape[0]):
        from_x[plane] = by_x[plane, 0:3]
        from_y[plane] = by_y[plane, 3:6]


def take_both(one, two, out):
    out[0] = one[0]
    out[1] = two[0]


def place_own(held, planes, coords, own, by_x, by_y, across_one, across_two, *rest):
    whole, sent = rest[held:]
    core, place, plane, half = coords[0], coords[1], coords[2], coords[3]
    for i, apart in enumerate(planes):
        z = plane ^ apart

        def put(y, x, strips, value):
            sent[i, y, x, strips] = value
            whole[y, z, x, core, strips] = value

        put(half, place, slice(0, 6), own[i])
        put(half, 1 - place, slice(0, 6), by_x[i])
        put(1 - half, place, slice(0, 6), by_y[i])
        put(1 - half, 1 - place, slice(0, 3), across_one[i])
        put(1 - half, 1 - place, slice(3, 6), across_two[i])


def place_other(planes, coords, arrived, _, whole):
    core, plane = coords[0], coords[2]
    for i, apart in enumerate(planes):
        for y in range(2):
            for x in range(2):
                whole[y, plane ^ apart, x, 1 - core] = arrived[i, y, x]


WHOLE = (HALVES, 4, 2, 2, OWN, BLOCK, STRIP)


def run_pack(master):
    return call(
        pack,
        "pack",
        [VMEM],
        [(VMEM, shape_of(1, OWN, BLOCK, STRIP))],
        [],
        math_size(master.shape),
        (master,),
        mib=4,
    )[0]


def run_halves(by_x, by_y):
    shape = shape_of(by_x.shape[0], 3, BLOCK, STRIP)
    return call(
        take_halves, "take_halves", [VMEM] * 2, [(VMEM, shape)] * 2, [], 1, (by_x, by_y), mib=4
    )


def run_both(one, two):
    shape = shape_of(2, OWN, BLOCK, STRIP)
    return call(take_both, "take_both", [VMEM] * 2, [(VMEM, shape)], [], 1, (one, two), mib=4)[0]


def run_place_own(planes, coords, pieces, held):
    count = len(planes)
    return call(
        functools.partial(place_own, len(held), planes),
        "place_own",
        [SMEM] + [VMEM] * (5 + len(held)),
        [(VMEM, shape_of(*WHOLE)), (VMEM, shape_of(count, HALVES, 2, OWN, BLOCK, STRIP))],
        [],
        1,
        (coords, *pieces, *held),
        aliases={6: 0} if held else None,
        mib=4,
    )


def run_place_other(planes, coords, arrived, whole):
    return call(
        functools.partial(place_other, planes),
        "place_other",
        [SMEM] + [VMEM] * 2,
        [(VMEM, shape_of(*WHOLE))],
        [],
        1,
        (coords, arrived, whole),
        aliases={2: 0},
        mib=4,
    )[0]


def neighbour_hop(value):
    return lax.ppermute(value, "dp", OTHER_X), lax.ppermute(value, "tensor", OTHER_Y)


def across_hop(pieces):
    return lax.ppermute(pieces[0], "tensor", OTHER_Y), lax.ppermute(pieces[1], "dp", OTHER_X)


def gather_split(master, coords, prepare):
    own = run_pack(master)
    near = lax.ppermute(own, "dp", NEAR_Z)
    far = lax.ppermute(own, "dp", FAR_Z)
    own_by = neighbour_hop(own)
    own_by, near, far, own, prepared = fence(own_by, near, far, own, prepare())

    other = lax.ppermute(near, "dp", FAR_Z)
    own_across = across_hop(run_halves(*own_by))
    both = run_both(near, far)
    both_by = neighbour_hop(both)
    own_across, both_by, other = fence(own_across, both_by, other)

    other_by = neighbour_hop(other)
    both_across = across_hop(run_halves(*both_by))
    whole, sent = run_place_own((0,), coords, (own, *own_by, *own_across), ())
    own_in = core_hop(sent)
    both_across, other_by, own_in, whole = fence(both_across, other_by, own_in, whole)

    other_across = across_hop(run_halves(*other_by))
    whole, sent = run_place_own((1, 2), coords, (both, *both_by, *both_across), (whole,))
    both_in = core_hop(sent)
    whole = run_place_other((0,), coords, own_in, whole)
    other_across, both_in, whole = fence(other_across, both_in, whole)

    whole, sent = run_place_own((3,), coords, (other, *other_by, *other_across), (whole,))
    other_in = core_hop(sent)
    whole = run_place_other((1, 2), coords, both_in, whole)
    other_in, whole = fence(other_in, whole)
    whole = run_place_other((3,), coords, other_in, whole)
    return whole.reshape(HALVES, STRIPS, BLOCK, STRIP), prepared


def scatter_flat(strips, own):
    if own % 4 == 0:
        mine = lax.psum_scatter(
            strips.reshape(-1, STRIP), EVERY, scatter_dimension=0, tiled=True
        )
        return to_blocks(mine.reshape(-1, BLOCK, STRIP)).astype(F32)
    blocks = to_blocks(strips.reshape(-1, BLOCK, STRIP))
    return lax.psum_scatter(blocks, EVERY, scatter_dimension=0, tiled=True).astype(F32)


def fence(*values):
    return lax.optimization_barrier(values)


OTHER_CORE = [(i, i ^ 1) for i in range(16)]
OTHER_X = [(i, i ^ 2) for i in range(16)]
OTHER_Y = [(0, 1), (1, 0)]


def by_plane(*moves):
    return [(4 * a + i, 4 * b + i) for a, b in moves for i in range(4)]


NEAR_Z = by_plane((0, 1), (1, 0), (2, 3), (3, 2))
FAR_Z = by_plane((0, 2), (1, 3), (2, 0), (3, 1))


def split_sum(coords, kept, arrived, sent_one, sent_two, kept_one, kept_two):
    place, half = coords[1], coords[3]

    @pl.loop(0, 2 * kept.shape[0])
    def _(step):
        plane, i = step // 2, lax.rem(step, 2)
        one, two = pl.ds(0, 3), pl.ds(3, 3)
        sent_one[plane, i] = kept[plane, 1 - half, i, one] + arrived[plane, 1 - half, i, one]
        kept_one[plane, i] = kept[plane, half, i, one] + arrived[plane, half, i, one]
        sent_two[plane, i] = kept[plane, i, 1 - place, two] + arrived[plane, i, 1 - place, two]
        kept_two[plane, i] = kept[plane, i, place, two] + arrived[plane, i, place, two]


def split_again(coords, one, two, one_in, two_in, sent_one, sent_two, kept_one, kept_two):
    place, half = coords[1], coords[3]

    @pl.loop(0, one.shape[0])
    def _(plane):
        sent_one[plane] = one[plane, 1 - place] + one_in[plane, 1 - place]
        kept_one[plane] = one[plane, place] + one_in[plane, place]
        sent_two[plane] = two[plane, 1 - half] + two_in[plane, 1 - half]
        kept_two[plane] = two[plane, half] + two_in[plane, half]


def join_sum(coords, one, two, one_in, two_in, *outs):
    for i, out in enumerate(outs):
        plane = lax.rem(coords[2] + i, 2)
        out[0:3] = one[plane] + one_in[plane]
        out[3:6] = two[plane] + two_in[plane]


def sum_of(left, right, out):
    @pl.loop(0, left.shape[0])
    def _(i):
        out[i] = left[i] + right[i]


def run_split(coords, kept, arrived):
    shape = shape_of(kept.shape[0], 2, 3, BLOCK, STRIP)
    outs = call(
        split_sum,
        "split_sum",
        [SMEM, VMEM, VMEM],
        [(VMEM, shape)] * 4,
        [],
        math_size(kept.shape),
        (coords, kept, arrived),
        mib=4,
    )
    return outs[:2], outs[2:]


def run_again(coords, kept, arrived):
    shape = shape_of(kept[0].shape[0], 3, BLOCK, STRIP)
    outs = call(
        split_again,
        "split_again",
        [SMEM] + [VMEM] * 4,
        [(VMEM, shape)] * 4,
        [],
        2 * math_size(kept[0].shape),
        (coords, *kept, *arrived),
        mib=4,
    )
    return outs[:2], outs[2:]


def run_join(coords, kept, arrived):
    return call(
        join_sum,
        "join_sum",
        [SMEM] + [VMEM] * 4,
        [(VMEM, shape_of(OWN, BLOCK, STRIP))] * 2,
        [],
        2 * math_size(kept[0].shape),
        (coords, *kept, *arrived),
        mib=4,
    )


def run_sum(left, right):
    return call(
        sum_of,
        "sum_of",
        [VMEM] * 2,
        [(VMEM, jax.ShapeDtypeStruct(left.shape, left.dtype))],
        [],
        math_size(left.shape),
        (left, right),
        mib=4,
    )[0]


def core_hop(sent):
    return lax.ppermute(sent, "dp", OTHER_CORE)


def first_hop(sent):
    return lax.ppermute(sent[0], "tensor", OTHER_Y), lax.ppermute(sent[1], "dp", OTHER_X)


def second_hop(sent):
    return lax.ppermute(sent[0], "dp", OTHER_X), lax.ppermute(sent[1], "tensor", OTHER_Y)


def precise(left, right, left_dim=1, right_dim=0):
    left_high, right_high = left.astype(BF16), right.astype(BF16)
    left_low = (left - left_high.astype(F32)).astype(BF16)
    right_low = (right - right_high.astype(F32)).astype(BF16)
    small = mm(left_high, right_low, left_dim, right_dim) + mm(
        left_low, right_high, left_dim, right_dim
    )
    return mm(left_high, right_high, left_dim, right_dim) + small


def update(
    coords, high, high_in, low, low_in, master, stat_left, stat_right, root_left, root_right, *outs
):
    grad_out, left_out, right_out, master_out, copy_out, grad = outs
    strip = pl.program_id(0)
    for condition, own, arrived in (
        (coords[2] >= 2, high, high_in),
        (coords[2] < 2, low, low_in),
    ):

        @pl.when(condition)
        def _():
            grad[...] = own[strip].astype(F32) + arrived[strip].astype(F32)

    for i in range(4):
        block = 4 * strip + i
        g = grad[:, i * BLOCK : (i + 1) * BLOCK]
        grad_out[i] = g
        left_out[i] = DECAY_RATE * stat_left[block] + (1.0 - DECAY_RATE) * precise(g, g, 1, 1)
        right_out[i] = DECAY_RATE * stat_right[block] + (1.0 - DECAY_RATE) * precise(g, g, 0, 0)
        direction = precise(root_left[block], precise(g, root_right[block]))
        new = master[block] - STEP_RATE * direction
        master_out[i] = new
        copy_out[i] = new.astype(BF16)


def run_update(coords, sums, blocks):
    count = blocks[0].shape[0]
    tile = pl.BlockSpec((4, BLOCK, BLOCK), lambda i: (i, 0, 0))
    shape = shape_of(count, BLOCK, BLOCK, dtype=F32)
    return call(
        update,
        "update",
        [SMEM] + [VMEM] * (len(sums) + len(blocks)),
        [(tile, shape)] * 4 + [(tile, shape_of(count, BLOCK, BLOCK))],
        [pltpu.VMEM((BLOCK, STRIP), F32)],
        12 * 2 * count * BLOCK**3,
        (coords, *sums, *blocks),
        grid=(count // 4,),
        mib=4,
    )


def sum_hops():
    hops = []
    for axis in ("tensor", "dp"):
        size, step = lax.axis_size(axis), 1
        while step < size:
            hops.append((axis, [(i, i ^ step) for i in range(size)]))
            step *= 2
    return hops


def add_hop(value, hop):
    return run_sum(value, lax.ppermute(value, *hop))


def plain_update(grad, master, stat_left, stat_right, root_left, root_right):
    left_new = DECAY_RATE * stat_left + (1.0 - DECAY_RATE) * jnp.einsum(
        "nij,nkj->nik", grad, grad, precision=PRECISE
    )
    right_new = DECAY_RATE * stat_right + (1.0 - DECAY_RATE) * jnp.einsum(
        "nji,njk->nik", grad, grad, precision=PRECISE
    )
    right_side = jnp.einsum("nij,njk->nik", grad, root_right, precision=PRECISE)
    direction = jnp.einsum("nij,njk->nik", root_left, right_side, precision=PRECISE)
    master_new = master - STEP_RATE * direction
    return grad, left_new, right_new, master_new, master_new.astype(BF16)


def body(
    tokens,
    token_mask,
    norm_gains,
    gain_moments,
    cotangent,
    master,
    stat_left,
    stat_right,
    root_left,
    root_right,
):
    rows = tokens.shape[0]
    own_caps = cotangent.shape[0]
    own = master.shape[0]
    split = lax.axis_size("dp") == 16 and lax.axis_size("tensor") == 2
    dp_pos, half = lax.axis_index("dp"), lax.axis_index("tensor")
    coords = jnp.stack([dp_pos % 2, dp_pos // 2 % 2, dp_pos // 4, half]).astype(jnp.int32)

    def prepare():
        group_mask = token_mask.astype(F32)
        own_mask = lax.dynamic_slice_in_dim(group_mask, half * own_caps, own_caps, 0)
        share = 1.0 / jnp.sum(own_mask, axis=1, keepdims=True)
        mask = jnp.repeat(own_mask.reshape(rows // GROUP, CAPS, SLOTS), SLOTS, axis=1)
        weight = own_mask * share
        grad_out = cotangent.astype(F32)[:, None, :] * weight[:, :, None]
        wide = jnp.broadcast_to(weight[:, :, None], (own_caps, SLOTS, PAIR)).reshape(rows, PAIR)
        grad_out = grad_out.reshape(rows, D)
        return mask.swapaxes(1, 2), wide, grad_out, grad_out.astype(BF16)

    if split:
        strips, prepared = gather_split(master, coords, prepare)
    else:
        strips, prepared = gather_weights(master), prepare()
    mask, share, grad_out, out_low = prepared
    normed, qkv, attended, after, normed_two, after_pooled = run_forward(
        tokens, norm_gains, mask, share, strips
    )
    hidden_pooled, grad_two, *held = run_mlp(coords, normed_two, out_low, share, strips, split)
    hops = sum_hops()
    blocks = (master, stat_left, stat_right, root_left, root_right)
    if not split:
        grad_after, gain_two, grad_att, *held = run_output(
            coords, norm_gains, attended, after, grad_out, grad_two, strips, held, split
        )
        grad_mixed, *held = run_backward(coords, mask, normed, qkv, grad_att, held, split)
        input_grad, gain_grads = run_input(
            tokens, norm_gains, grad_mixed, grad_after, gain_two, strips
        )
        pooled = run_pool(after_pooled, hidden_pooled, strips)
        for hop in hops:
            gain_grads = add_hop(gain_grads, hop)
        updated = plain_update(scatter_flat(held[0], own), *blocks)
    else:
        upper_kept, upper_sent, *lower = held
        upper_in = core_hop(upper_sent)
        grad_after, gain_two, grad_att, *lower = run_output(
            coords, norm_gains, attended, after, grad_out, grad_two, strips, lower, split
        )
        upper_in, grad_att, lower = fence(upper_in, grad_att, lower)

        upper_sent, upper_kept = run_split(coords, upper_kept, upper_in)
        upper_sent, grad_att, lower = fence(upper_sent, grad_att, lower)
        upper_in = first_hop(upper_sent)
        grad_mixed, *lower = run_backward(coords, mask, normed, qkv, grad_att, lower, split)
        upper_in, grad_mixed, lower = fence(upper_in, grad_mixed, lower)

        lower_in = core_hop(lower[1])
        upper_sent, upper_kept = run_again(coords, upper_kept, upper_in)
        upper_in = second_hop(upper_sent)
        lower_in, upper_sent, grad_mixed = fence(lower_in, upper_sent, grad_mixed)

        lower_sent, lower_kept = run_split(coords, lower[0], lower_in)
        lower_sent, grad_mixed = fence(lower_sent, grad_mixed)
        lower_in = first_hop(lower_sent)
        input_grad, gain_grads = run_input(
            tokens, norm_gains, grad_mixed, grad_after, gain_two, strips
        )
        upper_in, gain_grads = fence(upper_in, gain_grads)

        high, high_sent = run_join(coords, upper_kept, upper_in)
        high_in = lax.ppermute(high_sent, "dp", NEAR_Z)
        gain_in = lax.ppermute(gain_grads, *hops[0])
        pooled = run_pool(after_pooled, hidden_pooled, strips)
        high_in, lower_in, gain_in, pooled = fence(high_in, lower_in, gain_in, pooled)

        lower_sent, lower_kept = run_again(coords, lower_kept, lower_in)
        lower_in = second_hop(lower_sent)
        high = run_sum(high, high_in)
        high_in = lax.ppermute(high, "dp", by_plane((0, 2), (1, 3)))
        gain_grads = run_sum(gain_grads, gain_in)
        gain_in = lax.ppermute(gain_grads, *hops[1])
        lower_in, gain_in = fence(lower_in, gain_in)

        low, low_sent = run_join(coords, lower_kept, lower_in)
        low_in = lax.ppermute(low_sent, "dp", NEAR_Z)
        gain_grads = run_sum(gain_grads, gain_in)
        gain_in = lax.ppermute(gain_grads, *hops[2])
        low_in, gain_in = fence(low_in, gain_in)

        low = run_sum(low, low_in)
        low_in = lax.ppermute(low, "dp", by_plane((2, 0), (3, 1)))
        gain_grads = run_sum(gain_grads, gain_in)
        for hop in hops[3:]:
            gain_grads = add_hop(gain_grads, hop)
        updated = run_update(coords, (high, high_in, low, low_in), blocks)
    gain_grads = gain_grads.reshape(2, D)
    moments_new = DECAY_RATE * gain_moments + (1.0 - DECAY_RATE) * gain_grads * gain_grads
    gains_new = norm_gains - GAIN_RATE * gain_grads / (jnp.sqrt(moments_new) + 1e-08)
    return (pooled, input_grad, gain_grads, moments_new, gains_new, *updated)


def solution(mesh):
    rows = P(("dp", "tensor"), None)
    blocks = P(("dp", "tensor"), None, None)
    return jax.shard_map(
        body,
        mesh=mesh,
        in_specs=(rows, P("dp", None), P(), P(), rows) + (blocks,) * 5,
        out_specs=(rows, rows, P(), P(), P()) + (blocks,) * 5,
        check_vma=False,
    )
```

```python
import functools

import jax
import jax.numpy as jnp
from jax import lax
from jax.experimental import pallas as pl
from jax.experimental.pallas import tpu as pltpu
from jax.sharding import PartitionSpec as P

D = 768
HEADS = 12
HD = 64
FF = 3072
BLOCK = 96
SLOTS = 16
HALVES = 2
STRIP = 4 * BLOCK
STRIPS = 96
OWN = 6
GROUP = 128
CAPS = GROUP // SLOTS
UPPER = (2, 3)
LOWER = (0, 1)
PAIR = 2 * HD

EPSILON = 1e-06
DECAY_RATE = 0.5
STEP_RATE = 0.25
GAIN_RATE = 0.3
MASKED_SCORE = -1e30
PRECISE = lax.Precision.HIGHEST
F32 = jnp.float32
BF16 = jnp.bfloat16


def mm(left, right, left_dim=1, right_dim=0):
    return lax.dot_general(
        left, right, (((left_dim,), (right_dim,)), ((), ())), preferred_element_type=F32
    )


def weight_of(strips, half, first, rows, width, columns):
    parts = [
        jnp.concatenate([strips[half, first + width * row + column] for row in range(rows)], axis=0)
        for column in columns
    ]
    return jnp.concatenate(parts, axis=1)


def out_weight(strips):
    halves = [weight_of(strips, half, 24, 4, 2, (0, 1)) for half in range(HALVES)]
    return jnp.concatenate(halves, axis=0)


def norm_parts(values):
    center = values - jnp.mean(values, axis=-1, keepdims=True)
    inverse = lax.rsqrt(jnp.mean(center * center, axis=-1, keepdims=True) + EPSILON)
    return center * inverse, inverse


def norm_back(xhat, inverse, gain, grad):
    scaled = grad * gain
    return inverse * (
        scaled
        - jnp.mean(scaled, axis=-1, keepdims=True)
        - xhat * jnp.mean(scaled * xhat, axis=-1, keepdims=True)
    )


def split_pair(values):
    first = lax.broadcasted_iota(jnp.int32, (GROUP, PAIR), 1) < HD
    zero = jnp.zeros_like(values)
    return jnp.concatenate(
        [jnp.where(first, values, zero), jnp.where(first, zero, values)], axis=0
    )


def join_pair(stacked):
    first = lax.broadcasted_iota(jnp.int32, (GROUP, PAIR), 1) < HD
    return jnp.where(first, stacked[:GROUP], stacked[GROUP:])


def caption_of():
    return lax.broadcasted_iota(jnp.int32, (SLOTS, 2 * GROUP), 1) % GROUP // SLOTS


def compact(full, caption):
    kept = full[0:SLOTS]
    for i in range(1, CAPS):
        kept = jnp.where(caption == i, full[i * SLOTS : (i + 1) * SLOTS], kept)
    return kept


def expand(kept, caption):
    zero = jnp.zeros_like(kept)
    return jnp.concatenate(
        [jnp.where(caption == i, kept, zero).astype(BF16) for i in range(CAPS)], axis=0
    )


def softmax_of(scores, bias):
    scores = scores * HD ** (-0.5) + bias
    shifted = jnp.exp(scores - jnp.max(scores, axis=0, keepdims=True))
    return shifted / jnp.sum(shifted, axis=0, keepdims=True)


def pairs_of():
    for half in range(HALVES):
        for start in range(0, STRIP, PAIR):
            yield half, slice(start, start + PAIR), slice(half * STRIP + start, half * STRIP + start + PAIR)


def columns(values, i):
    return values[:, 2 * GROUP * i : 2 * GROUP * (i + 1)]


def key_bias(mask):
    bias = jnp.where(mask > 0, 0.0, MASKED_SCORE)
    return jnp.concatenate([bias] * HEADS, axis=1)


def span_of(i, size=GROUP):
    return pl.ds(pl.multiple_of(i * size, size), size)


def prepare(coords, token_mask, cot, mask, share, out_wide, inverse):
    captions = cot.shape[0]
    first = pl.multiple_of(coords[3] * captions, captions)
    own = token_mask[pl.ds(first, captions), :].astype(F32)
    count = jnp.broadcast_to(jnp.sum(own, axis=1, keepdims=True), (captions, PAIR))
    inverse[...] = 1.0 / count
    key = lax.broadcasted_iota(jnp.int32, (SLOTS, GROUP), 0).astype(F32)
    here = (
        lax.broadcasted_iota(jnp.int32, (CAPS, GROUP), 0)
        == lax.broadcasted_iota(jnp.int32, (CAPS, GROUP), 1) // SLOTS
    )
    slot = lax.broadcasted_iota(jnp.int32, (CAPS, SLOTS, PAIR), 1).astype(F32)
    caption = lax.broadcasted_iota(jnp.int32, (CAPS, SLOTS, PAIR), 0)
    lane = lax.broadcasted_iota(jnp.int32, (CAPS, SLOTS, PAIR), 2)
    for i in range(captions // CAPS):
        span, caps = slice(i * GROUP, (i + 1) * GROUP), slice(i * CAPS, (i + 1) * CAPS)
        number = count[caps]
        by_query = jnp.sum(jnp.where(here, number, 0.0), axis=0, keepdims=True)
        mask[i] = jnp.where(key < by_query, 1.0, 0.0)
        true = slot < number[:, None, :]
        weight = jnp.where(true, 1.0 / number[:, None, :], 0.0)
        share[span, :] = weight.reshape(GROUP, PAIR)
        seen = jnp.where(true & (caption + i * CAPS == lane), 1.0, 0.0)
        out_wide[span, D:] = seen.reshape(GROUP, PAIR).astype(BF16)
        for j in range(0, D, PAIR):
            lanes = slice(j, j + PAIR)
            value = (cot[caps, lanes].astype(F32)[:, None, :] * weight).reshape(GROUP, PAIR)
            out_wide[span, lanes] = value.astype(BF16)


def pool(values, share):
    parts = [
        values[:, i : i + PAIR] * share for i in range(0, values.shape[1], PAIR)
    ]
    weighted = jnp.concatenate(parts, axis=1)
    return jnp.sum(weighted.reshape(-1, SLOTS, values.shape[1]), axis=1)


def attention_forward(
    tok, gains, mask, share, strips, normed, qkv, attended, after, normed_two, after_pooled
):
    rows = tok.shape[0]

    @pl.loop(0, rows // GROUP)
    def _(i):
        span = span_of(i)
        xhat, _ = norm_parts(tok[span, :].astype(F32))
        normed[span, :] = (xhat * gains[0:1, :]).astype(BF16)

    for half in range(HALVES):
        mixed = mm(normed[...], weight_of(strips, half, 0, 8, 3, range(3))).astype(BF16)
        for part in range(3):
            qkv[3 * half + part] = mixed[:, part * STRIP : (part + 1) * STRIP]

    @pl.loop(0, rows // GROUP)
    def _(i):
        span = span_of(i)
        caption = caption_of()
        pairs = list(pairs_of())
        scores = [
            compact(
                mm(qkv[3 * half + 1, span, lanes], split_pair(qkv[3 * half, span, lanes]), 1, 1),
                caption,
            )
            for half, lanes, _ in pairs
        ]
        probs = softmax_of(jnp.concatenate(scores, axis=1), key_bias(mask[i]))
        for pair, (half, lanes, wide) in enumerate(pairs):
            spread = expand(columns(probs, pair), caption)
            mixed = mm(spread, qkv[3 * half + 2, span, lanes], 0, 0)
            attended[span, wide] = join_pair(mixed).astype(BF16)

    after[...] = mm(attended[...], out_weight(strips))

    @pl.loop(0, rows // GROUP)
    def _(i):
        span = span_of(i)
        summed = tok[span, :].astype(F32) + after[span, :]
        after[span, :] = summed
        after_pooled[span_of(i, CAPS), :] = pool(summed, share[span, :])
        xhat, _ = norm_parts(summed)
        normed_two[span, :] = (xhat * gains[1:2, :]).astype(BF16)


GELU_A = 0.7978845608028654
GELU_B = 0.044715


def gelu_both(v):
    square = v * v
    inner = jnp.tanh(GELU_A * v * (1.0 + GELU_B * square))
    half_up = 0.5 * (1.0 + inner)
    slope = half_up + (0.5 * GELU_A) * v * (1.0 - inner * inner) * (1.0 + (3.0 * GELU_B) * square)
    return v * half_up, slope


class Emitter:
    def __init__(self, targets, runs, coords):
        self.core = coords[0]
        self.whole = targets[0] if len(targets) == 1 else None
        self.batches = [] if self.whole is not None else list(zip(runs, targets[0::2], targets[1::2]))

    def store(self, pieces, here=True):
        if self.whole is not None:

            @pl.when(here)
            def _():
                for value, half, strip in pieces:
                    self.whole[half, strip] = value

            return
        for core in range(2):

            @pl.when((self.core == core) & here)
            def _():
                for value, half, strip in pieces:
                    plane, place = strip // (4 * OWN), strip // (2 * OWN) % 2
                    for run, kept, sent in self.batches:
                        if plane in run:
                            target = kept if strip // OWN % 2 == core else sent
                            target[plane - run[0], half, place, strip % OWN] = value


def strips_of(grad, rows, columns):
    return [
        (i, j, grad[i * BLOCK : (i + 1) * BLOCK, j * STRIP : (j + 1) * STRIP])
        for i in range(rows)
        for j in range(columns)
    ]


def mlp_both(coords, normed_two, out_wide, strips, *rest):
    hidden_pooled, grad_normed_two, *targets, hidden, grad_up = rest
    step = pl.program_id(0)
    rows = normed_two.shape[0]
    emit = Emitter(targets, (UPPER, LOWER), coords)
    half = step // 2
    column = lax.rem(step, 2)

    @pl.when(step == 0)
    def _():
        grad_normed_two[...] = jnp.zeros_like(grad_normed_two)

    up_weight = weight_of(strips, half, 32 + 2 * column, 8, 4, (0, 1))
    down_weight = weight_of(strips, half, 64 + 16 * column, 8, 2, (0, 1))
    chunk = 256
    for i in range(rows // chunk):
        span = slice(i * chunk, (i + 1) * chunk)
        act, slope = gelu_both(mm(normed_two[span, :], up_weight))
        hidden[span, :] = act.astype(BF16)
        grad = (mm(out_wide[span, :D], down_weight, 1, 1) * slope).astype(BF16)
        grad_up[span, :] = grad
        grad_normed_two[span, :] += mm(grad, up_weight, 1, 1)

    both = mm(hidden[...], out_wide[...], 0, 0)
    hidden_pooled[step] = both[:, D:]
    down_strips = strips_of(both[:, :D].astype(BF16), 8, 2)
    up_strips = strips_of(mm(normed_two[...], grad_up[...], 0, 0).astype(BF16), 8, 2)
    for i in range(2):
        pieces = [(value, half, 64 + 16 * i + 2 * row + part) for row, part, value in down_strips]
        pieces += [(value, half, 32 + 4 * row + 2 * i + part) for row, part, value in up_strips]
        emit.store(pieces, column == i)


def pool_out(after_pooled, hidden_pooled, inverse, strips, pooled):
    captions = pooled.shape[0]
    pooled[...] = after_pooled[...]
    for step in range(4):
        value = hidden_pooled[step]
        high = value.astype(BF16)
        low = (value - high.astype(F32)).astype(BF16)
        weight = weight_of(strips, step // 2, 64 + 16 * (step % 2), 8, 2, (0, 1))
        both = mm(jnp.concatenate([high, low], axis=1), weight, 0, 0)
        total = both[:captions] + both[PAIR : PAIR + captions]
        pooled[...] += total * jnp.concatenate([inverse[...]] * (D // PAIR), axis=1)


def output_backward(
    held, coords, gains, attended, after, cot, share, grad_normed_two, strips, *rest
):
    grad_after, gain_part, grad_att, *targets, after_low = rest[held:]
    rows = after.shape[0]
    emit = Emitter(targets, (LOWER,), coords)
    gain_part[...] = jnp.zeros_like(gain_part)

    @pl.loop(0, rows // GROUP)
    def _(i):
        span = span_of(i)
        xhat, inverse = norm_parts(after[span, :])
        grad = grad_normed_two[span, :]
        gain_part[...] += jnp.sum(grad * xhat, axis=0, keepdims=True)
        weight = share[span, :].reshape(CAPS, SLOTS, PAIR)
        parts = [
            (cot[span_of(i, CAPS), j : j + PAIR].astype(F32)[:, None, :] * weight)
            for j in range(0, D, PAIR)
        ]
        grad_out = jnp.concatenate([part.reshape(GROUP, PAIR) for part in parts], axis=1)
        value = grad_out + norm_back(xhat, inverse, gains[1:2, :], grad)
        grad_after[span, :] = value
        after_low[span, :] = value.astype(BF16)

    grad_att[...] = mm(after_low[...], out_weight(strips), 1, 1).astype(BF16)
    grad_w = mm(attended[...], after_low[...], 0, 0).astype(BF16)
    emit.store(
        [
            (value, row // 4, 24 + 2 * (row % 4) + part)
            for row, part, value in strips_of(grad_w, 8, 2)
        ]
    )


def attention_backward(held, coords, mask, normed, qkv, grad_att, *rest):
    grad_mixed, *targets = rest[held:]
    rows = normed.shape[0]
    emit = Emitter(targets, (LOWER,), coords)

    @pl.loop(0, rows // GROUP)
    def _(i):
        span = span_of(i)
        caption = caption_of()
        scale = HD ** (-0.5)
        pairs = list(pairs_of())
        scores = [
            compact(
                mm(qkv[3 * half + 1, span, lanes], split_pair(qkv[3 * half, span, lanes]), 1, 1),
                caption,
            )
            for half, lanes, _ in pairs
        ]
        grad_probs = [
            compact(
                mm(qkv[3 * half + 2, span, lanes], split_pair(grad_att[span, wide]), 1, 1), caption
            )
            for half, lanes, wide in pairs
        ]
        probs = softmax_of(jnp.concatenate(scores, axis=1), key_bias(mask[i]))
        grad_probs = jnp.concatenate(grad_probs, axis=1)
        inner = jnp.sum(probs * grad_probs, axis=0, keepdims=True)
        grad_scores = probs * (grad_probs - inner)
        for pair, (half, lanes, wide) in enumerate(pairs):
            spread = expand(columns(grad_scores, pair), caption)
            back = mm(spread, qkv[3 * half + 1, span, lanes], 0, 0)
            grad_mixed[3 * half, span, lanes] = (join_pair(back) * scale).astype(BF16)
            back = mm(spread, split_pair(qkv[3 * half, span, lanes]))
            grad_mixed[3 * half + 1, span, lanes] = (back * scale).astype(BF16)
            spread = expand(columns(probs, pair), caption)
            grad_mixed[3 * half + 2, span, lanes] = mm(
                spread, split_pair(grad_att[span, wide])
            ).astype(BF16)

    for half in range(HALVES):
        grads = jnp.concatenate([grad_mixed[3 * half + part] for part in range(3)], axis=1)
        grad_w = mm(normed[...], grads, 0, 0).astype(BF16)
        emit.store([(value, half, 3 * row + part) for row, part, value in strips_of(grad_w, 8, 3)])


def input_backward(tok, gains, grad_mixed, grad_after, gain_two, strips, input_grad, gain_part):
    rows = tok.shape[0]
    grads = jnp.concatenate([grad_mixed[part] for part in range(6)], axis=1)
    halves = [weight_of(strips, half, 0, 8, 3, range(3)) for half in range(HALVES)]
    input_grad[...] = mm(grads, jnp.concatenate(halves, axis=1), 1, 1)
    gain_part[0] = jnp.zeros_like(gain_two)
    gain_part[1] = gain_two[...]

    @pl.loop(0, rows // GROUP)
    def _(i):
        span = span_of(i)
        xhat, inverse = norm_parts(tok[span, :].astype(F32))
        grad = input_grad[span, :]
        gain_part[0] += jnp.sum(grad * xhat, axis=0, keepdims=True)
        input_grad[span, :] = grad_after[span, :] + norm_back(xhat, inverse, gains[0:1, :], grad)


def shape_of(*shape, dtype=BF16):
    return jax.ShapeDtypeStruct(shape, dtype)


VMEM = pl.BlockSpec(memory_space=pltpu.VMEM)
SMEM = pl.BlockSpec(memory_space=pltpu.SMEM)


def call(kernel, name, in_specs, outs, scratch, flops, args, grid=(1,), aliases=None, mib=10):
    moved = sum(math_size(a.shape) * a.dtype.itemsize for a in args)
    moved += sum(math_size(s.shape) * s.dtype.itemsize for _, s in outs)
    return pl.pallas_call(
        kernel,
        grid=grid,
        in_specs=in_specs,
        out_specs=[spec for spec, _ in outs],
        out_shape=[shape for _, shape in outs],
        scratch_shapes=scratch,
        input_output_aliases=aliases or {},
        compiler_params=pltpu.CompilerParams(
            dimension_semantics=("arbitrary",) * len(grid), vmem_limit_bytes=mib << 20
        ),
        cost_estimate=pl.CostEstimate(flops=1, bytes_accessed=1, transcendentals=0),
        name=name,
    )(*args)


def math_size(shape):
    size = 1
    for extent in shape:
        size *= extent
    return size


UNIT = 2 * 768 * 768 * 768


def run_prepare(coords, token_mask, cot):
    captions = cot.shape[0]
    rows = captions * SLOTS
    return call(
        prepare,
        "prepare",
        [SMEM, VMEM, VMEM],
        [
            (VMEM, shape_of(rows // GROUP, SLOTS, GROUP, dtype=F32)),
            (VMEM, shape_of(rows, PAIR, dtype=F32)),
            (VMEM, shape_of(rows, D + PAIR)),
            (VMEM, shape_of(captions, PAIR, dtype=F32)),
        ],
        [],
        1,
        (coords, token_mask, cot),
        mib=6,
    )


def run_forward(tok, gains, mask, share, strips):
    rows = tok.shape[0]
    return call(
        attention_forward,
        "attention_forward",
        [VMEM] * 5,
        [
            (VMEM, shape_of(rows, D)),
            (VMEM, shape_of(6, rows, STRIP)),
            (VMEM, shape_of(rows, D)),
            (VMEM, shape_of(rows, D, dtype=F32)),
            (VMEM, shape_of(rows, D)),
            (VMEM, shape_of(rows // SLOTS, D, dtype=F32)),
        ],
        [],
        5 * UNIT,
        (tok, gains, mask, share, strips),
        mib=3,
    )


def targets_of(runs, split):
    if split:
        shapes = [shape_of(len(run), HALVES, 2, OWN, BLOCK, STRIP) for run in runs for _ in range(2)]
    else:
        shapes = [shape_of(HALVES, STRIPS, BLOCK, STRIP)]
    return [(VMEM, shape) for shape in shapes]


def run_mlp(coords, normed_two, out_wide, strips, split):
    rows = normed_two.shape[0]
    return call(
        mlp_both,
        "mlp_both",
        [SMEM] + [VMEM] * 3,
        [(VMEM, shape_of(4, D, PAIR, dtype=F32)), (VMEM, shape_of(rows, D, dtype=F32))]
        + targets_of((UPPER, LOWER), split),
        [pltpu.VMEM((rows, D), BF16), pltpu.VMEM((rows, D), BF16)],
        20 * UNIT,
        (coords, normed_two, out_wide, strips),
        grid=(4,),
        mib=8 if split else 44,
    )


def run_pool(after_pooled, hidden_pooled, inverse, strips):
    return call(
        pool_out,
        "pool_out",
        [VMEM] * 4,
        [(VMEM, jax.ShapeDtypeStruct(after_pooled.shape, F32))],
        [],
        UNIT // 2,
        (after_pooled, hidden_pooled, inverse, strips),
        mib=6,
    )[0]


def run_output(coords, gains, attended, after, cot, share, grad_two, strips, held, split):
    rows = after.shape[0]
    return call(
        functools.partial(output_backward, len(held)),
        "output_backward",
        [SMEM] + [VMEM] * (7 + len(held)),
        [
            (VMEM, shape_of(rows, D, dtype=F32)),
            (VMEM, shape_of(1, D, dtype=F32)),
            (VMEM, shape_of(rows, D)),
        ]
        + targets_of((LOWER,), split),
        [pltpu.VMEM((rows, D), BF16)],
        2 * UNIT,
        (coords, gains, attended, after, cot, share, grad_two, strips, *held),
        aliases={8 + i: 3 + i for i in range(len(held))},
        mib=6 if split else 56,
    )


def run_backward(coords, mask, normed, qkv, grad_att, held, split):
    rows = normed.shape[0]
    return call(
        functools.partial(attention_backward, len(held)),
        "attention_backward",
        [SMEM, VMEM, VMEM, VMEM, VMEM] + [VMEM] * len(held),
        [(VMEM, shape_of(6, rows, STRIP))] + targets_of((LOWER,), split),
        [],
        7 * UNIT,
        (coords, mask, normed, qkv, grad_att, *held),
        aliases={5 + i: 1 + i for i in range(len(held))},
        mib=6 if split else 56,
    )


def run_input(tok, gains, grad_mixed, grad_after, gain_two, strips):
    rows = tok.shape[0]
    return call(
        input_backward,
        "input_backward",
        [VMEM] * 6,
        [(VMEM, shape_of(rows, D, dtype=F32)), (VMEM, shape_of(2, 1, D, dtype=F32))],
        [],
        3 * UNIT,
        (tok, gains, grad_mixed, grad_after, gain_two, strips),
        mib=5,
    )


def to_strips(blocks):
    count = blocks.shape[0] // 4
    return blocks.reshape(count, 4, BLOCK, BLOCK).transpose(0, 2, 1, 3).reshape(count, BLOCK, STRIP)


def to_blocks(strips):
    count = strips.shape[0]
    return strips.reshape(count, BLOCK, 4, BLOCK).transpose(0, 2, 1, 3).reshape(-1, BLOCK, BLOCK)


EVERY = ("tensor", "dp")


def gather_weights(master):
    low = master.astype(BF16)
    own = low.shape[0]
    if own % 4 == 0:
        strips = to_strips(low).reshape(-1, STRIP)
        strips = lax.all_gather(strips, EVERY, axis=0, tiled=True)
        return strips.reshape(HALVES, STRIPS, BLOCK, STRIP)
    blocks = lax.all_gather(low, EVERY, axis=0, tiled=True)
    return to_strips(blocks).reshape(HALVES, STRIPS, BLOCK, STRIP)


def pack(master, out):
    for strip in range(master.shape[0] // 4):
        parts = [master[4 * strip + i].astype(BF16) for i in range(4)]
        out[0, strip] = jnp.concatenate(parts, axis=1)


def take_halves(by_x, by_y, from_x, from_y):
    for plane in range(by_x.shape[0]):
        from_x[plane] = by_x[plane, 0:3]
        from_y[plane] = by_y[plane, 3:6]


def take_both(one, two, out):
    out[0] = one[0]
    out[1] = two[0]


def place_own(held, planes, coords, own, by_x, by_y, across_one, across_two, *rest):
    whole, sent = rest[held:]
    core, place, plane, half = coords[0], coords[1], coords[2], coords[3]
    for i, apart in enumerate(planes):
        z = plane ^ apart

        def put(y, x, strips, value):
            sent[i, y, x, strips] = value
            whole[y, z, x, core, strips] = value

        put(half, place, slice(0, 6), own[i])
        put(half, 1 - place, slice(0, 6), by_x[i])
        put(1 - half, place, slice(0, 6), by_y[i])
        put(1 - half, 1 - place, slice(0, 3), across_one[i])
        put(1 - half, 1 - place, slice(3, 6), across_two[i])


def place_other(planes, coords, arrived, _, whole):
    core, plane = coords[0], coords[2]
    for i, apart in enumerate(planes):
        for y in range(2):
            for x in range(2):
                whole[y, plane ^ apart, x, 1 - core] = arrived[i, y, x]


WHOLE = (HALVES, 4, 2, 2, OWN, BLOCK, STRIP)


def run_pack(master):
    return call(
        pack,
        "pack",
        [VMEM],
        [(VMEM, shape_of(1, OWN, BLOCK, STRIP))],
        [],
        math_size(master.shape),
        (master,),
        mib=4,
    )[0]


def run_halves(by_x, by_y):
    shape = shape_of(by_x.shape[0], 3, BLOCK, STRIP)
    return call(
        take_halves, "take_halves", [VMEM] * 2, [(VMEM, shape)] * 2, [], 1, (by_x, by_y), mib=4
    )


def run_both(one, two):
    shape = shape_of(2, OWN, BLOCK, STRIP)
    return call(take_both, "take_both", [VMEM] * 2, [(VMEM, shape)], [], 1, (one, two), mib=4)[0]


def run_place_own(planes, coords, pieces, held):
    count = len(planes)
    return call(
        functools.partial(place_own, len(held), planes),
        "place_own",
        [SMEM] + [VMEM] * (5 + len(held)),
        [(VMEM, shape_of(*WHOLE)), (VMEM, shape_of(count, HALVES, 2, OWN, BLOCK, STRIP))],
        [],
        1,
        (coords, *pieces, *held),
        aliases={6: 0} if held else None,
        mib=4,
    )


def run_place_other(planes, coords, arrived, whole):
    return call(
        functools.partial(place_other, planes),
        "place_other",
        [SMEM] + [VMEM] * 2,
        [(VMEM, shape_of(*WHOLE))],
        [],
        1,
        (coords, arrived, whole),
        aliases={2: 0},
        mib=4,
    )[0]


def neighbour_hop(value):
    return lax.ppermute(value, "dp", OTHER_X), lax.ppermute(value, "tensor", OTHER_Y)


def across_hop(pieces):
    return lax.ppermute(pieces[0], "tensor", OTHER_Y), lax.ppermute(pieces[1], "dp", OTHER_X)


def gather_split(master, coords, prepare):
    own = run_pack(master)
    near = lax.ppermute(own, "dp", NEAR_Z)
    far = lax.ppermute(own, "dp", FAR_Z)
    own_by = neighbour_hop(own)
    own_by, near, far, own, prepared = fence(own_by, near, far, own, prepare())

    other = lax.ppermute(near, "dp", FAR_Z)
    own_across = across_hop(run_halves(*own_by))
    both = run_both(near, far)
    both_by = neighbour_hop(both)
    own_across, both_by, other = fence(own_across, both_by, other)

    other_by = neighbour_hop(other)
    both_across = across_hop(run_halves(*both_by))
    whole, sent = run_place_own((0,), coords, (own, *own_by, *own_across), ())
    own_in = core_hop(sent)
    both_across, other_by, own_in, whole = fence(both_across, other_by, own_in, whole)

    other_across = across_hop(run_halves(*other_by))
    whole, sent = run_place_own((1, 2), coords, (both, *both_by, *both_across), (whole,))
    both_in = core_hop(sent)
    whole = run_place_other((0,), coords, own_in, whole)
    other_across, both_in, whole = fence(other_across, both_in, whole)

    whole, sent = run_place_own((3,), coords, (other, *other_by, *other_across), (whole,))
    other_in = core_hop(sent)
    whole = run_place_other((1, 2), coords, both_in, whole)
    other_in, whole = fence(other_in, whole)
    whole = run_place_other((3,), coords, other_in, whole)
    return whole.reshape(HALVES, STRIPS, BLOCK, STRIP), prepared


def scatter_flat(strips, own):
    if own % 4 == 0:
        mine = lax.psum_scatter(
            strips.reshape(-1, STRIP), EVERY, scatter_dimension=0, tiled=True
        )
        return to_blocks(mine.reshape(-1, BLOCK, STRIP)).astype(F32)
    blocks = to_blocks(strips.reshape(-1, BLOCK, STRIP))
    return lax.psum_scatter(blocks, EVERY, scatter_dimension=0, tiled=True).astype(F32)


def fence(*values):
    return lax.optimization_barrier(values)


OTHER_CORE = [(i, i ^ 1) for i in range(16)]
OTHER_X = [(i, i ^ 2) for i in range(16)]
OTHER_Y = [(0, 1), (1, 0)]


def by_plane(*moves):
    return [(4 * a + i, 4 * b + i) for a, b in moves for i in range(4)]


NEAR_Z = by_plane((0, 1), (1, 0), (2, 3), (3, 2))
FAR_Z = by_plane((0, 2), (1, 3), (2, 0), (3, 1))


def split_sum(coords, kept, arrived, sent_one, sent_two, kept_one, kept_two):
    place, half = coords[1], coords[3]

    @pl.loop(0, 2 * kept.shape[0])
    def _(step):
        plane, i = step // 2, lax.rem(step, 2)
        one, two = pl.ds(0, 3), pl.ds(3, 3)
        sent_one[plane, i] = kept[plane, 1 - half, i, one] + arrived[plane, 1 - half, i, one]
        kept_one[plane, i] = kept[plane, half, i, one] + arrived[plane, half, i, one]
        sent_two[plane, i] = kept[plane, i, 1 - place, two] + arrived[plane, i, 1 - place, two]
        kept_two[plane, i] = kept[plane, i, place, two] + arrived[plane, i, place, two]


def split_again(coords, one, two, one_in, two_in, sent_one, sent_two, kept_one, kept_two):
    place, half = coords[1], coords[3]

    @pl.loop(0, one.shape[0])
    def _(plane):
        sent_one[plane] = one[plane, 1 - place] + one_in[plane, 1 - place]
        kept_one[plane] = one[plane, place] + one_in[plane, place]
        sent_two[plane] = two[plane, 1 - half] + two_in[plane, 1 - half]
        kept_two[plane] = two[plane, half] + two_in[plane, half]


def join_sum(coords, one, two, one_in, two_in, *outs):
    for i, out in enumerate(outs):
        plane = lax.rem(coords[2] + i, 2)
        out[0:3] = one[plane] + one_in[plane]
        out[3:6] = two[plane] + two_in[plane]


def pick_sum(coords, high, high_in, low, low_in, mine, sent):
    @pl.when(coords[2] >= 2)
    def _():
        mine[...] = high[...] + high_in[...]
        sent[...] = low[...] + low_in[...]

    @pl.when(coords[2] < 2)
    def _():
        mine[...] = low[...] + low_in[...]
        sent[...] = high[...] + high_in[...]


def renew_gains(grads, arrived, moments, gains, grads_out, moments_out, gains_out):
    for i in range(2):
        grad = grads[i] + arrived[i]
        moment = DECAY_RATE * moments[i : i + 1] + (1.0 - DECAY_RATE) * grad * grad
        grads_out[i : i + 1] = grad
        moments_out[i : i + 1] = moment
        gains_out[i : i + 1] = gains[i : i + 1] - GAIN_RATE * grad / (jnp.sqrt(moment) + 1e-08)


def sum_of(left, right, out):
    @pl.loop(0, left.shape[0])
    def _(i):
        out[i] = left[i] + right[i]


def run_split(coords, kept, arrived):
    shape = shape_of(kept.shape[0], 2, 3, BLOCK, STRIP)
    outs = call(
        split_sum,
        "split_sum",
        [SMEM, VMEM, VMEM],
        [(VMEM, shape)] * 4,
        [],
        math_size(kept.shape),
        (coords, kept, arrived),
        mib=4,
    )
    return outs[:2], outs[2:]


def run_again(coords, kept, arrived):
    shape = shape_of(kept[0].shape[0], 3, BLOCK, STRIP)
    outs = call(
        split_again,
        "split_again",
        [SMEM] + [VMEM] * 4,
        [(VMEM, shape)] * 4,
        [],
        2 * math_size(kept[0].shape),
        (coords, *kept, *arrived),
        mib=4,
    )
    return outs[:2], outs[2:]


def run_join(coords, kept, arrived):
    return call(
        join_sum,
        "join_sum",
        [SMEM] + [VMEM] * 4,
        [(VMEM, shape_of(OWN, BLOCK, STRIP))] * 2,
        [],
        2 * math_size(kept[0].shape),
        (coords, *kept, *arrived),
        mib=4,
    )


def run_pick(coords, high, high_in, low, low_in):
    return call(
        pick_sum,
        "pick_sum",
        [SMEM] + [VMEM] * 4,
        [(VMEM, shape_of(OWN, BLOCK, STRIP))] * 2,
        [],
        1,
        (coords, high, high_in, low, low_in),
        mib=4,
    )


def run_sum(left, right):
    return call(
        sum_of,
        "sum_of",
        [VMEM] * 2,
        [(VMEM, jax.ShapeDtypeStruct(left.shape, left.dtype))],
        [],
        math_size(left.shape),
        (left, right),
        mib=4,
    )[0]


def run_gains(grads, arrived, moments, gains):
    return call(
        renew_gains,
        "renew_gains",
        [VMEM] * 4,
        [(VMEM, shape_of(2, D, dtype=F32))] * 3,
        [],
        1,
        (grads, arrived, moments, gains),
        mib=4,
    )


def core_hop(sent):
    return lax.ppermute(sent, "dp", OTHER_CORE)


def first_hop(sent):
    return lax.ppermute(sent[0], "tensor", OTHER_Y), lax.ppermute(sent[1], "dp", OTHER_X)


def second_hop(sent):
    return lax.ppermute(sent[0], "dp", OTHER_X), lax.ppermute(sent[1], "tensor", OTHER_Y)


def precise(left, right, left_dim=1, right_dim=0):
    left_high, right_high = left.astype(BF16), right.astype(BF16)
    left_low = (left - left_high.astype(F32)).astype(BF16)
    right_low = (right - right_high.astype(F32)).astype(BF16)
    small = mm(left_high, right_low, left_dim, right_dim) + mm(
        left_low, right_high, left_dim, right_dim
    )
    return mm(left_high, right_high, left_dim, right_dim) + small


def update(mine, arrived, master, stat_left, stat_right, root_left, root_right, *outs):
    grad_out, left_out, right_out, master_out, copy_out = outs
    strip = pl.program_id(0)
    grad = mine[strip].astype(F32) + arrived[strip].astype(F32)
    for i in range(4):
        block = 4 * strip + i
        g = grad[:, i * BLOCK : (i + 1) * BLOCK]
        grad_out[i] = g
        left_out[i] = DECAY_RATE * stat_left[block] + (1.0 - DECAY_RATE) * precise(g, g, 1, 1)
        right_out[i] = DECAY_RATE * stat_right[block] + (1.0 - DECAY_RATE) * precise(g, g, 0, 0)
        direction = precise(root_left[block], precise(g, root_right[block]))
        new = master[block] - STEP_RATE * direction
        master_out[i] = new
        copy_out[i] = new.astype(BF16)


def run_update(sums, blocks):
    count = blocks[0].shape[0]
    tile = pl.BlockSpec((4, BLOCK, BLOCK), lambda i: (i, 0, 0))
    shape = shape_of(count, BLOCK, BLOCK, dtype=F32)
    return call(
        update,
        "update",
        [VMEM] * (len(sums) + len(blocks)),
        [(tile, shape)] * 4 + [(tile, shape_of(count, BLOCK, BLOCK))],
        [],
        12 * 2 * count * BLOCK**3,
        (*sums, *blocks),
        grid=(count // 4,),
        mib=4,
    )


def sum_hops():
    hops = []
    for axis in ("tensor", "dp"):
        size, step = lax.axis_size(axis), 1
        while step < size:
            hops.append((axis, [(i, i ^ step) for i in range(size)]))
            step *= 2
    return hops


def plain_update(grad, master, stat_left, stat_right, root_left, root_right):
    left_new = DECAY_RATE * stat_left + (1.0 - DECAY_RATE) * jnp.einsum(
        "nij,nkj->nik", grad, grad, precision=PRECISE
    )
    right_new = DECAY_RATE * stat_right + (1.0 - DECAY_RATE) * jnp.einsum(
        "nji,njk->nik", grad, grad, precision=PRECISE
    )
    right_side = jnp.einsum("nij,njk->nik", grad, root_right, precision=PRECISE)
    direction = jnp.einsum("nij,njk->nik", root_left, right_side, precision=PRECISE)
    master_new = master - STEP_RATE * direction
    return grad, left_new, right_new, master_new, master_new.astype(BF16)


def body(
    tokens,
    token_mask,
    norm_gains,
    gain_moments,
    cotangent,
    master,
    stat_left,
    stat_right,
    root_left,
    root_right,
):
    rows = tokens.shape[0]
    own_caps = cotangent.shape[0]
    own = master.shape[0]
    split = lax.axis_size("dp") == 16 and lax.axis_size("tensor") == 2
    dp_pos, half = lax.axis_index("dp"), lax.axis_index("tensor")
    coords = jnp.stack([dp_pos % 2, dp_pos // 2 % 2, dp_pos // 4, half]).astype(jnp.int32)

    coords, master = fence(coords, master)
    if split:
        strips, prepared = gather_split(
            master, coords, lambda: run_prepare(coords, token_mask, cotangent)
        )
    else:
        strips, prepared = gather_weights(master), run_prepare(coords, token_mask, cotangent)
    mask, share, out_wide, inverse = prepared
    normed, qkv, attended, after, normed_two, after_pooled = run_forward(
        tokens, norm_gains, mask, share, strips
    )
    hidden_pooled, grad_two, *held = run_mlp(coords, normed_two, out_wide, strips, split)
    hops = sum_hops()
    blocks = (master, stat_left, stat_right, root_left, root_right)
    if not split:
        grad_after, gain_two, grad_att, *held = run_output(
            coords, norm_gains, attended, after, cotangent, share, grad_two, strips, held, split
        )
        grad_mixed, *held = run_backward(coords, mask, normed, qkv, grad_att, held, split)
        input_grad, gain_grads = run_input(
            tokens, norm_gains, grad_mixed, grad_after, gain_two, strips
        )
        pooled = run_pool(after_pooled, hidden_pooled, inverse, strips)
        for hop in hops[:-1]:
            gain_grads = run_sum(gain_grads, lax.ppermute(gain_grads, *hop))
        gain_in = lax.ppermute(gain_grads, *hops[-1])
        gain_results = run_gains(gain_grads, gain_in, gain_moments, norm_gains)
        updated = plain_update(scatter_flat(held[0], own), *blocks)
    else:
        upper_kept, upper_sent, *lower = held
        upper_in = core_hop(upper_sent)
        grad_after, gain_two, grad_att, *lower = run_output(
            coords, norm_gains, attended, after, cotangent, share, grad_two, strips, lower, split
        )
        upper_in, grad_att, lower = fence(upper_in, grad_att, lower)

        upper_sent, upper_kept = run_split(coords, upper_kept, upper_in)
        upper_sent, grad_att, lower = fence(upper_sent, grad_att, lower)
        upper_in = first_hop(upper_sent)
        grad_mixed, *lower = run_backward(coords, mask, normed, qkv, grad_att, lower, split)
        upper_in, grad_mixed, lower = fence(upper_in, grad_mixed, lower)

        lower_in = core_hop(lower[1])
        upper_sent, upper_kept = run_again(coords, upper_kept, upper_in)
        upper_in = second_hop(upper_sent)
        lower_in, upper_sent, grad_mixed = fence(lower_in, upper_sent, grad_mixed)

        lower_sent, lower_kept = run_split(coords, lower[0], lower_in)
        lower_sent, grad_mixed = fence(lower_sent, grad_mixed)
        lower_in = first_hop(lower_sent)
        input_grad, gain_grads = run_input(
            tokens, norm_gains, grad_mixed, grad_after, gain_two, strips
        )
        upper_in, gain_grads = fence(upper_in, gain_grads)

        gain_in = lax.ppermute(gain_grads, *hops[0])
        pooled = run_pool(after_pooled, hidden_pooled, inverse, strips)
        high, high_sent = run_join(coords, upper_kept, upper_in)
        high_in = lax.ppermute(high_sent, "dp", NEAR_Z)
        high_in, lower_in, gain_in, pooled = fence(high_in, lower_in, gain_in, pooled)

        lower_sent, lower_kept = run_again(coords, lower_kept, lower_in)
        lower_in = second_hop(lower_sent)
        gain_grads = run_sum(gain_grads, gain_in)
        gain_in = lax.ppermute(gain_grads, *hops[1])
        lower_in, gain_in = fence(lower_in, gain_in)

        low, low_sent = run_join(coords, lower_kept, lower_in)
        low_in = lax.ppermute(low_sent, "dp", NEAR_Z)
        gain_grads = run_sum(gain_grads, gain_in)
        gain_in = lax.ppermute(gain_grads, *hops[2])
        low_in, gain_in = fence(low_in, gain_in)

        mine, sent = run_pick(coords, high, high_in, low, low_in)
        arrived = lax.ppermute(sent, "dp", FAR_Z)
        gain_grads = run_sum(gain_grads, gain_in)
        gain_in = lax.ppermute(gain_grads, *hops[3])
        gain_grads = run_sum(gain_grads, gain_in)
        gain_in = lax.ppermute(gain_grads, *hops[4])
        gain_results = run_gains(gain_grads, gain_in, gain_moments, norm_gains)
        arrived, gain_results = fence(arrived, gain_results)

        updated = run_update((mine, arrived), blocks)
    return (pooled, input_grad, *gain_results, *updated)


def solution(mesh):
    rows = P(("dp", "tensor"), None)
    blocks = P(("dp", "tensor"), None, None)
    return jax.shard_map(
        body,
        mesh=mesh,
        in_specs=(rows, P("dp", None), P(), P(), rows) + (blocks,) * 5,
        out_specs=(rows, rows, P(), P(), P()) + (blocks,) * 5,
        check_vma=False,
    )
```

```python
import functools

import jax
import jax.numpy as jnp
from jax import lax
from jax.experimental import pallas as pl
from jax.experimental.pallas import tpu as pltpu
from jax.sharding import PartitionSpec as P

D = 768
HEADS = 12
HD = 64
FF = 3072
BLOCK = 96
SLOTS = 16
HALVES = 2
STRIP = 4 * BLOCK
STRIPS = 96
OWN = 6
GROUP = 128
CAPS = GROUP // SLOTS
UPPER = (2, 3)
LOWER = (0, 1)
PAIR = 2 * HD

EPSILON = 1e-06
DECAY_RATE = 0.5
STEP_RATE = 0.25
GAIN_RATE = 0.3
MASKED_SCORE = -1e30
PRECISE = lax.Precision.HIGHEST
F32 = jnp.float32
BF16 = jnp.bfloat16


def mm(left, right, left_dim=1, right_dim=0):
    return lax.dot_general(
        left, right, (((left_dim,), (right_dim,)), ((), ())), preferred_element_type=F32
    )


def weight_of(strips, half, first, rows, width, columns):
    parts = [
        jnp.concatenate([strips[half, first + width * row + column] for row in range(rows)], axis=0)
        for column in columns
    ]
    return jnp.concatenate(parts, axis=1)


def out_weight(strips):
    halves = [weight_of(strips, half, 24, 4, 2, (0, 1)) for half in range(HALVES)]
    return jnp.concatenate(halves, axis=0)


def norm_parts(values):
    center = values - jnp.mean(values, axis=-1, keepdims=True)
    inverse = lax.rsqrt(jnp.mean(center * center, axis=-1, keepdims=True) + EPSILON)
    return center * inverse, inverse


def norm_back(xhat, inverse, gain, grad):
    scaled = grad * gain
    return inverse * (
        scaled
        - jnp.mean(scaled, axis=-1, keepdims=True)
        - xhat * jnp.mean(scaled * xhat, axis=-1, keepdims=True)
    )


def split_pair(values):
    first = lax.broadcasted_iota(jnp.int32, (GROUP, PAIR), 1) < HD
    zero = jnp.zeros_like(values)
    return jnp.concatenate(
        [jnp.where(first, values, zero), jnp.where(first, zero, values)], axis=0
    )


def join_pair(stacked):
    first = lax.broadcasted_iota(jnp.int32, (GROUP, PAIR), 1) < HD
    return jnp.where(first, stacked[:GROUP], stacked[GROUP:])


def caption_of():
    return lax.broadcasted_iota(jnp.int32, (SLOTS, 2 * GROUP), 1) % GROUP // SLOTS


def compact(full, caption):
    kept = full[0:SLOTS]
    for i in range(1, CAPS):
        kept = jnp.where(caption == i, full[i * SLOTS : (i + 1) * SLOTS], kept)
    return kept


def expand(kept, caption):
    zero = jnp.zeros_like(kept)
    return jnp.concatenate(
        [jnp.where(caption == i, kept, zero).astype(BF16) for i in range(CAPS)], axis=0
    )


def softmax_of(scores, bias):
    scores = scores * HD ** (-0.5) + bias
    shifted = jnp.exp(scores - jnp.max(scores, axis=0, keepdims=True))
    return shifted / jnp.sum(shifted, axis=0, keepdims=True)


def pairs_of():
    for half in range(HALVES):
        for start in range(0, STRIP, PAIR):
            yield half, slice(start, start + PAIR), slice(half * STRIP + start, half * STRIP + start + PAIR)


def columns(values, i):
    return values[:, 2 * GROUP * i : 2 * GROUP * (i + 1)]


def key_bias(mask):
    bias = jnp.where(mask > 0, 0.0, MASKED_SCORE)
    return jnp.concatenate([bias] * HEADS, axis=1)


def span_of(i, size=GROUP):
    return pl.ds(pl.multiple_of(i * size, size), size)


def prepare(coords, token_mask, cot, tok, gains, mask, share, out_wide, inverse, normed):
    captions = cot.shape[0]
    first = pl.multiple_of(coords[3] * captions, captions)
    own = token_mask[pl.ds(first, captions), :].astype(F32)
    count = jnp.broadcast_to(jnp.sum(own, axis=1, keepdims=True), (captions, PAIR))
    inverse[...] = 1.0 / count
    key = lax.broadcasted_iota(jnp.int32, (SLOTS, GROUP), 0).astype(F32)
    here = (
        lax.broadcasted_iota(jnp.int32, (CAPS, GROUP), 0)
        == lax.broadcasted_iota(jnp.int32, (CAPS, GROUP), 1) // SLOTS
    )
    slot = lax.broadcasted_iota(jnp.int32, (CAPS, SLOTS, PAIR), 1).astype(F32)
    caption = lax.broadcasted_iota(jnp.int32, (CAPS, SLOTS, PAIR), 0)
    lane = lax.broadcasted_iota(jnp.int32, (CAPS, SLOTS, PAIR), 2)
    for i in range(captions // CAPS):
        span, caps = slice(i * GROUP, (i + 1) * GROUP), slice(i * CAPS, (i + 1) * CAPS)
        number = count[caps]
        by_query = jnp.sum(jnp.where(here, number, 0.0), axis=0, keepdims=True)
        mask[i] = jnp.where(key < by_query, 1.0, 0.0)
        true = slot < number[:, None, :]
        weight = jnp.where(true, 1.0 / number[:, None, :], 0.0)
        share[span, :] = weight.reshape(GROUP, PAIR)
        seen = jnp.where(true & (caption + i * CAPS == lane), 1.0, 0.0)
        out_wide[span, D:] = seen.reshape(GROUP, PAIR).astype(BF16)
        for j in range(0, D, PAIR):
            lanes = slice(j, j + PAIR)
            value = (cot[caps, lanes].astype(F32)[:, None, :] * weight).reshape(GROUP, PAIR)
            out_wide[span, lanes] = value.astype(BF16)
        xhat, _ = norm_parts(tok[span, :].astype(F32))
        normed[span, :] = (xhat * gains[0:1, :]).astype(BF16)


def pool(values, share):
    parts = [
        values[:, i : i + PAIR] * share for i in range(0, values.shape[1], PAIR)
    ]
    weighted = jnp.concatenate(parts, axis=1)
    return jnp.sum(weighted.reshape(-1, SLOTS, values.shape[1]), axis=1)


def attention_forward(
    tok, gains, normed, mask, share, strips, qkv, attended, after, normed_two, after_pooled
):
    rows = tok.shape[0]

    for half in range(HALVES):
        mixed = mm(normed[...], weight_of(strips, half, 0, 8, 3, range(3))).astype(BF16)
        for part in range(3):
            qkv[3 * half + part] = mixed[:, part * STRIP : (part + 1) * STRIP]

    @pl.loop(0, rows // GROUP)
    def _(i):
        span = span_of(i)
        caption = caption_of()
        pairs = list(pairs_of())
        scores = [
            compact(
                mm(qkv[3 * half + 1, span, lanes], split_pair(qkv[3 * half, span, lanes]), 1, 1),
                caption,
            )
            for half, lanes, _ in pairs
        ]
        probs = softmax_of(jnp.concatenate(scores, axis=1), key_bias(mask[i]))
        for pair, (half, lanes, wide) in enumerate(pairs):
            spread = expand(columns(probs, pair), caption)
            mixed = mm(spread, qkv[3 * half + 2, span, lanes], 0, 0)
            attended[span, wide] = join_pair(mixed).astype(BF16)

    after[...] = mm(attended[...], out_weight(strips))

    @pl.loop(0, rows // GROUP)
    def _(i):
        span = span_of(i)
        summed = tok[span, :].astype(F32) + after[span, :]
        after[span, :] = summed
        after_pooled[span_of(i, CAPS), :] = pool(summed, share[span, :])
        xhat, _ = norm_parts(summed)
        normed_two[span, :] = (xhat * gains[1:2, :]).astype(BF16)


GELU_A = 0.7978845608028654
GELU_B = 0.044715


def gelu_both(v):
    square = v * v
    inner = jnp.tanh(GELU_A * v * (1.0 + GELU_B * square))
    half_up = 0.5 * (1.0 + inner)
    slope = half_up + (0.5 * GELU_A) * v * (1.0 - inner * inner) * (1.0 + (3.0 * GELU_B) * square)
    return v * half_up, slope


class Emitter:
    def __init__(self, targets, runs, coords):
        self.core = coords[0]
        self.whole = targets[0] if len(targets) == 1 else None
        self.batches = [] if self.whole is not None else list(zip(runs, targets[0::2], targets[1::2]))

    def store(self, pieces, here=True):
        if self.whole is not None:

            @pl.when(here)
            def _():
                for value, half, strip in pieces:
                    self.whole[half, strip] = value

            return
        for core in range(2):

            @pl.when((self.core == core) & here)
            def _():
                for value, half, strip in pieces:
                    plane, place = strip // (4 * OWN), strip // (2 * OWN) % 2
                    for run, kept, sent in self.batches:
                        if plane in run:
                            target = kept if strip // OWN % 2 == core else sent
                            target[plane - run[0], half, place, strip % OWN] = value


def strips_of(grad, rows, columns):
    return [
        (i, j, grad[i * BLOCK : (i + 1) * BLOCK, j * STRIP : (j + 1) * STRIP])
        for i in range(rows)
        for j in range(columns)
    ]


def mlp_both(coords, normed_two, out_wide, strips, *rest):
    hidden_pooled, grad_normed_two, *targets, hidden, grad_up = rest
    step = pl.program_id(0)
    rows = normed_two.shape[0]
    emit = Emitter(targets, (UPPER, LOWER), coords)
    half = step // 2
    column = lax.rem(step, 2)

    @pl.when(step == 0)
    def _():
        grad_normed_two[...] = jnp.zeros_like(grad_normed_two)

    up_weight = weight_of(strips, half, 32 + 2 * column, 8, 4, (0, 1))
    down_weight = weight_of(strips, half, 64 + 16 * column, 8, 2, (0, 1))
    chunk = 256
    for i in range(rows // chunk):
        span = slice(i * chunk, (i + 1) * chunk)
        act, slope = gelu_both(mm(normed_two[span, :], up_weight))
        hidden[span, :] = act.astype(BF16)
        grad = (mm(out_wide[span, :D], down_weight, 1, 1) * slope).astype(BF16)
        grad_up[span, :] = grad
        grad_normed_two[span, :] += mm(grad, up_weight, 1, 1)

    both = mm(hidden[...], out_wide[...], 0, 0)
    hidden_pooled[step] = both[:, D:]
    down_strips = strips_of(both[:, :D].astype(BF16), 8, 2)
    up_strips = strips_of(mm(normed_two[...], grad_up[...], 0, 0).astype(BF16), 8, 2)
    for i in range(2):
        pieces = [(value, half, 64 + 16 * i + 2 * row + part) for row, part, value in down_strips]
        pieces += [(value, half, 32 + 4 * row + 2 * i + part) for row, part, value in up_strips]
        emit.store(pieces, column == i)


def pool_out(after_pooled, hidden_pooled, inverse, strips, pooled):
    captions = pooled.shape[0]
    pooled[...] = after_pooled[...]
    for step in range(4):
        value = hidden_pooled[step]
        high = value.astype(BF16)
        low = (value - high.astype(F32)).astype(BF16)
        weight = weight_of(strips, step // 2, 64 + 16 * (step % 2), 8, 2, (0, 1))
        both = mm(jnp.concatenate([high, low], axis=1), weight, 0, 0)
        total = both[:captions] + both[PAIR : PAIR + captions]
        pooled[...] += total * jnp.concatenate([inverse[...]] * (D // PAIR), axis=1)


def output_backward(
    held, coords, gains, attended, after, cot, share, grad_normed_two, strips, *rest
):
    grad_after, gain_part, grad_att, *targets, after_low = rest[held:]
    rows = after.shape[0]
    emit = Emitter(targets, (LOWER,), coords)
    gain_part[...] = jnp.zeros_like(gain_part)

    @pl.loop(0, rows // GROUP)
    def _(i):
        span = span_of(i)
        xhat, inverse = norm_parts(after[span, :])
        grad = grad_normed_two[span, :]
        gain_part[...] += jnp.sum(grad * xhat, axis=0, keepdims=True)
        weight = share[span, :].reshape(CAPS, SLOTS, PAIR)
        parts = [
            (cot[span_of(i, CAPS), j : j + PAIR].astype(F32)[:, None, :] * weight)
            for j in range(0, D, PAIR)
        ]
        grad_out = jnp.concatenate([part.reshape(GROUP, PAIR) for part in parts], axis=1)
        value = grad_out + norm_back(xhat, inverse, gains[1:2, :], grad)
        grad_after[span, :] = value
        after_low[span, :] = value.astype(BF16)

    grad_att[...] = mm(after_low[...], out_weight(strips), 1, 1).astype(BF16)
    grad_w = mm(attended[...], after_low[...], 0, 0).astype(BF16)
    emit.store(
        [
            (value, row // 4, 24 + 2 * (row % 4) + part)
            for row, part, value in strips_of(grad_w, 8, 2)
        ]
    )


def attention_backward(held, coords, mask, normed, qkv, grad_att, *rest):
    grad_mixed, *targets = rest[held:]
    rows = normed.shape[0]
    emit = Emitter(targets, (LOWER,), coords)

    @pl.loop(0, rows // GROUP)
    def _(i):
        span = span_of(i)
        caption = caption_of()
        scale = HD ** (-0.5)
        pairs = list(pairs_of())
        scores = [
            compact(
                mm(qkv[3 * half + 1, span, lanes], split_pair(qkv[3 * half, span, lanes]), 1, 1),
                caption,
            )
            for half, lanes, _ in pairs
        ]
        grad_probs = [
            compact(
                mm(qkv[3 * half + 2, span, lanes], split_pair(grad_att[span, wide]), 1, 1), caption
            )
            for half, lanes, wide in pairs
        ]
        probs = softmax_of(jnp.concatenate(scores, axis=1), key_bias(mask[i]))
        grad_probs = jnp.concatenate(grad_probs, axis=1)
        inner = jnp.sum(probs * grad_probs, axis=0, keepdims=True)
        grad_scores = probs * (grad_probs - inner)
        for pair, (half, lanes, wide) in enumerate(pairs):
            spread = expand(columns(grad_scores, pair), caption)
            back = mm(spread, qkv[3 * half + 1, span, lanes], 0, 0)
            grad_mixed[3 * half, span, lanes] = (join_pair(back) * scale).astype(BF16)
            back = mm(spread, split_pair(qkv[3 * half, span, lanes]))
            grad_mixed[3 * half + 1, span, lanes] = (back * scale).astype(BF16)
            spread = expand(columns(probs, pair), caption)
            grad_mixed[3 * half + 2, span, lanes] = mm(
                spread, split_pair(grad_att[span, wide])
            ).astype(BF16)

    for half in range(HALVES):
        grads = jnp.concatenate([grad_mixed[3 * half + part] for part in range(3)], axis=1)
        grad_w = mm(normed[...], grads, 0, 0).astype(BF16)
        emit.store([(value, half, 3 * row + part) for row, part, value in strips_of(grad_w, 8, 3)])


def input_backward(tok, gains, grad_mixed, grad_after, gain_two, strips, input_grad, gain_part):
    rows = tok.shape[0]
    grads = jnp.concatenate([grad_mixed[part] for part in range(6)], axis=1)
    halves = [weight_of(strips, half, 0, 8, 3, range(3)) for half in range(HALVES)]
    input_grad[...] = mm(grads, jnp.concatenate(halves, axis=1), 1, 1)
    gain_part[0] = jnp.zeros_like(gain_two)
    gain_part[1] = gain_two[...]

    @pl.loop(0, rows // GROUP)
    def _(i):
        span = span_of(i)
        xhat, inverse = norm_parts(tok[span, :].astype(F32))
        grad = input_grad[span, :]
        gain_part[0] += jnp.sum(grad * xhat, axis=0, keepdims=True)
        input_grad[span, :] = grad_after[span, :] + norm_back(xhat, inverse, gains[0:1, :], grad)


def shape_of(*shape, dtype=BF16):
    return jax.ShapeDtypeStruct(shape, dtype)


VMEM = pl.BlockSpec(memory_space=pltpu.VMEM)
SMEM = pl.BlockSpec(memory_space=pltpu.SMEM)


def call(kernel, name, in_specs, outs, scratch, flops, args, grid=(1,), aliases=None, mib=10):
    moved = sum(math_size(a.shape) * a.dtype.itemsize for a in args)
    moved += sum(math_size(s.shape) * s.dtype.itemsize for _, s in outs)
    return pl.pallas_call(
        kernel,
        grid=grid,
        in_specs=in_specs,
        out_specs=[spec for spec, _ in outs],
        out_shape=[shape for _, shape in outs],
        scratch_shapes=scratch,
        input_output_aliases=aliases or {},
        compiler_params=pltpu.CompilerParams(
            dimension_semantics=("arbitrary",) * len(grid), vmem_limit_bytes=mib << 20
        ),
        cost_estimate=pl.CostEstimate(flops=1, bytes_accessed=1, transcendentals=0),
        name=name,
    )(*args)


def math_size(shape):
    size = 1
    for extent in shape:
        size *= extent
    return size


UNIT = 2 * 768 * 768 * 768


def run_prepare(coords, token_mask, cot, tok, gains):
    captions = cot.shape[0]
    rows = captions * SLOTS
    return call(
        prepare,
        "prepare",
        [SMEM] + [VMEM] * 4,
        [
            (VMEM, shape_of(rows // GROUP, SLOTS, GROUP, dtype=F32)),
            (VMEM, shape_of(rows, PAIR, dtype=F32)),
            (VMEM, shape_of(rows, D + PAIR)),
            (VMEM, shape_of(captions, PAIR, dtype=F32)),
            (VMEM, shape_of(rows, D)),
        ],
        [],
        1,
        (coords, token_mask, cot, tok, gains),
        mib=6,
    )


def run_forward(tok, gains, normed, mask, share, strips):
    rows = tok.shape[0]
    return call(
        attention_forward,
        "attention_forward",
        [VMEM] * 6,
        [
            (VMEM, shape_of(6, rows, STRIP)),
            (VMEM, shape_of(rows, D)),
            (VMEM, shape_of(rows, D, dtype=F32)),
            (VMEM, shape_of(rows, D)),
            (VMEM, shape_of(rows // SLOTS, D, dtype=F32)),
        ],
        [],
        5 * UNIT,
        (tok, gains, normed, mask, share, strips),
        mib=3,
    )


def targets_of(runs, split):
    if split:
        shapes = [shape_of(len(run), HALVES, 2, OWN, BLOCK, STRIP) for run in runs for _ in range(2)]
    else:
        shapes = [shape_of(HALVES, STRIPS, BLOCK, STRIP)]
    return [(VMEM, shape) for shape in shapes]


def run_mlp(coords, normed_two, out_wide, strips, split):
    rows = normed_two.shape[0]
    return call(
        mlp_both,
        "mlp_both",
        [SMEM] + [VMEM] * 3,
        [(VMEM, shape_of(4, D, PAIR, dtype=F32)), (VMEM, shape_of(rows, D, dtype=F32))]
        + targets_of((UPPER, LOWER), split),
        [pltpu.VMEM((rows, D), BF16), pltpu.VMEM((rows, D), BF16)],
        20 * UNIT,
        (coords, normed_two, out_wide, strips),
        grid=(4,),
        mib=6 if split else 44,
    )


def run_pool(after_pooled, hidden_pooled, inverse, strips):
    return call(
        pool_out,
        "pool_out",
        [VMEM] * 4,
        [(VMEM, jax.ShapeDtypeStruct(after_pooled.shape, F32))],
        [],
        UNIT // 2,
        (after_pooled, hidden_pooled, inverse, strips),
        mib=6,
    )[0]


def run_output(coords, gains, attended, after, cot, share, grad_two, strips, held, split):
    rows = after.shape[0]
    return call(
        functools.partial(output_backward, len(held)),
        "output_backward",
        [SMEM] + [VMEM] * (7 + len(held)),
        [
            (VMEM, shape_of(rows, D, dtype=F32)),
            (VMEM, shape_of(1, D, dtype=F32)),
            (VMEM, shape_of(rows, D)),
        ]
        + targets_of((LOWER,), split),
        [pltpu.VMEM((rows, D), BF16)],
        2 * UNIT,
        (coords, gains, attended, after, cot, share, grad_two, strips, *held),
        aliases={8 + i: 3 + i for i in range(len(held))},
        mib=6 if split else 56,
    )


def run_backward(coords, mask, normed, qkv, grad_att, held, split):
    rows = normed.shape[0]
    return call(
        functools.partial(attention_backward, len(held)),
        "attention_backward",
        [SMEM, VMEM, VMEM, VMEM, VMEM] + [VMEM] * len(held),
        [(VMEM, shape_of(6, rows, STRIP))] + targets_of((LOWER,), split),
        [],
        7 * UNIT,
        (coords, mask, normed, qkv, grad_att, *held),
        aliases={5 + i: 1 + i for i in range(len(held))},
        mib=6 if split else 56,
    )


def run_input(tok, gains, grad_mixed, grad_after, gain_two, strips):
    rows = tok.shape[0]
    return call(
        input_backward,
        "input_backward",
        [VMEM] * 6,
        [(VMEM, shape_of(rows, D, dtype=F32)), (VMEM, shape_of(2, 1, D, dtype=F32))],
        [],
        3 * UNIT,
        (tok, gains, grad_mixed, grad_after, gain_two, strips),
        mib=5,
    )


def to_strips(blocks):
    count = blocks.shape[0] // 4
    return blocks.reshape(count, 4, BLOCK, BLOCK).transpose(0, 2, 1, 3).reshape(count, BLOCK, STRIP)


def to_blocks(strips):
    count = strips.shape[0]
    return strips.reshape(count, BLOCK, 4, BLOCK).transpose(0, 2, 1, 3).reshape(-1, BLOCK, BLOCK)


EVERY = ("tensor", "dp")


def gather_weights(master):
    low = master.astype(BF16)
    own = low.shape[0]
    if own % 4 == 0:
        strips = to_strips(low).reshape(-1, STRIP)
        strips = lax.all_gather(strips, EVERY, axis=0, tiled=True)
        return strips.reshape(HALVES, STRIPS, BLOCK, STRIP)
    blocks = lax.all_gather(low, EVERY, axis=0, tiled=True)
    return to_strips(blocks).reshape(HALVES, STRIPS, BLOCK, STRIP)


def pack(master, out):
    for strip in range(master.shape[0] // 4):
        parts = [master[4 * strip + i].astype(BF16) for i in range(4)]
        out[0, strip] = jnp.concatenate(parts, axis=1)


def take_halves(by_x, by_y, from_x, from_y):
    for plane in range(by_x.shape[0]):
        from_x[plane] = by_x[plane, 0:3]
        from_y[plane] = by_y[plane, 3:6]


def take_both(one, two, out):
    out[0] = one[0]
    out[1] = two[0]


def place_own(held, planes, coords, own, by_x, by_y, across_one, across_two, *rest):
    whole, sent = rest[held:]
    core, place, plane, half = coords[0], coords[1], coords[2], coords[3]
    for i, apart in enumerate(planes):
        z = plane ^ apart

        def put(y, x, strips, value):
            sent[i, y, x, strips] = value
            whole[y, z, x, core, strips] = value

        put(half, place, slice(0, 6), own[i])
        put(half, 1 - place, slice(0, 6), by_x[i])
        put(1 - half, place, slice(0, 6), by_y[i])
        put(1 - half, 1 - place, slice(0, 3), across_one[i])
        put(1 - half, 1 - place, slice(3, 6), across_two[i])


def place_other(planes, coords, arrived, _, whole):
    core, plane = coords[0], coords[2]
    for i, apart in enumerate(planes):
        for y in range(2):
            for x in range(2):
                whole[y, plane ^ apart, x, 1 - core] = arrived[i, y, x]


WHOLE = (HALVES, 4, 2, 2, OWN, BLOCK, STRIP)


def run_pack(master):
    return call(
        pack,
        "pack",
        [VMEM],
        [(VMEM, shape_of(1, OWN, BLOCK, STRIP))],
        [],
        math_size(master.shape),
        (master,),
        mib=4,
    )[0]


def run_halves(by_x, by_y):
    shape = shape_of(by_x.shape[0], 3, BLOCK, STRIP)
    return call(
        take_halves, "take_halves", [VMEM] * 2, [(VMEM, shape)] * 2, [], 1, (by_x, by_y), mib=4
    )


def run_both(one, two):
    shape = shape_of(2, OWN, BLOCK, STRIP)
    return call(take_both, "take_both", [VMEM] * 2, [(VMEM, shape)], [], 1, (one, two), mib=4)[0]


def run_place_own(planes, coords, pieces, held):
    count = len(planes)
    return call(
        functools.partial(place_own, len(held), planes),
        "place_own",
        [SMEM] + [VMEM] * (5 + len(held)),
        [(VMEM, shape_of(*WHOLE)), (VMEM, shape_of(count, HALVES, 2, OWN, BLOCK, STRIP))],
        [],
        1,
        (coords, *pieces, *held),
        aliases={6: 0} if held else None,
        mib=4,
    )


def run_place_other(planes, coords, arrived, whole):
    return call(
        functools.partial(place_other, planes),
        "place_other",
        [SMEM] + [VMEM] * 2,
        [(VMEM, shape_of(*WHOLE))],
        [],
        1,
        (coords, arrived, whole),
        aliases={2: 0},
        mib=4,
    )[0]


def neighbour_hop(value):
    return lax.ppermute(value, "dp", OTHER_X), lax.ppermute(value, "tensor", OTHER_Y)


def across_hop(pieces):
    return lax.ppermute(pieces[0], "tensor", OTHER_Y), lax.ppermute(pieces[1], "dp", OTHER_X)


def gather_split(master, coords, prepare):
    own = run_pack(master)
    near = lax.ppermute(own, "dp", NEAR_Z)
    far = lax.ppermute(own, "dp", FAR_Z)
    own_by = neighbour_hop(own)
    own_by, near, far, own, prepared = fence(own_by, near, far, own, prepare())

    other = lax.ppermute(near, "dp", FAR_Z)
    own_across = across_hop(run_halves(*own_by))
    both = run_both(near, far)
    both_by = neighbour_hop(both)
    own_across, both_by, other = fence(own_across, both_by, other)

    other_by = neighbour_hop(other)
    both_across = across_hop(run_halves(*both_by))
    whole, sent = run_place_own((0,), coords, (own, *own_by, *own_across), ())
    own_in = core_hop(sent)
    both_across, other_by, own_in, whole = fence(both_across, other_by, own_in, whole)

    other_across = across_hop(run_halves(*other_by))
    whole, sent = run_place_own((1, 2), coords, (both, *both_by, *both_across), (whole,))
    both_in = core_hop(sent)
    whole = run_place_other((0,), coords, own_in, whole)
    other_across, both_in, whole = fence(other_across, both_in, whole)

    whole, sent = run_place_own((3,), coords, (other, *other_by, *other_across), (whole,))
    other_in = core_hop(sent)
    whole = run_place_other((1, 2), coords, both_in, whole)
    other_in, whole = fence(other_in, whole)
    whole = run_place_other((3,), coords, other_in, whole)
    return whole.reshape(HALVES, STRIPS, BLOCK, STRIP), prepared


def scatter_flat(strips, own):
    if own % 4 == 0:
        mine = lax.psum_scatter(
            strips.reshape(-1, STRIP), EVERY, scatter_dimension=0, tiled=True
        )
        return to_blocks(mine.reshape(-1, BLOCK, STRIP)).astype(F32)
    blocks = to_blocks(strips.reshape(-1, BLOCK, STRIP))
    return lax.psum_scatter(blocks, EVERY, scatter_dimension=0, tiled=True).astype(F32)


def fence(*values):
    return lax.optimization_barrier(values)


OTHER_CORE = [(i, i ^ 1) for i in range(16)]
OTHER_X = [(i, i ^ 2) for i in range(16)]
OTHER_Y = [(0, 1), (1, 0)]


def by_plane(*moves):
    return [(4 * a + i, 4 * b + i) for a, b in moves for i in range(4)]


NEAR_Z = by_plane((0, 1), (1, 0), (2, 3), (3, 2))
FAR_Z = by_plane((0, 2), (1, 3), (2, 0), (3, 1))


def split_sum(coords, kept, arrived, sent_one, sent_two, kept_one, kept_two):
    place, half = coords[1], coords[3]

    @pl.loop(0, 2 * kept.shape[0])
    def _(step):
        plane, i = step // 2, lax.rem(step, 2)
        one, two = pl.ds(0, 3), pl.ds(3, 3)
        sent_one[plane, i] = kept[plane, 1 - half, i, one] + arrived[plane, 1 - half, i, one]
        kept_one[plane, i] = kept[plane, half, i, one] + arrived[plane, half, i, one]
        sent_two[plane, i] = kept[plane, i, 1 - place, two] + arrived[plane, i, 1 - place, two]
        kept_two[plane, i] = kept[plane, i, place, two] + arrived[plane, i, place, two]


def split_again(coords, one, two, one_in, two_in, sent_one, sent_two, kept_one, kept_two):
    place, half = coords[1], coords[3]

    @pl.loop(0, one.shape[0])
    def _(plane):
        sent_one[plane] = one[plane, 1 - place] + one_in[plane, 1 - place]
        kept_one[plane] = one[plane, place] + one_in[plane, place]
        sent_two[plane] = two[plane, 1 - half] + two_in[plane, 1 - half]
        kept_two[plane] = two[plane, half] + two_in[plane, half]


def join_sum(coords, one, two, one_in, two_in, *outs):
    for i, out in enumerate(outs):
        plane = lax.rem(coords[2] + i, 2)
        out[0:3] = one[plane] + one_in[plane]
        out[3:6] = two[plane] + two_in[plane]


def pick_sum(coords, high, high_in, low, low_in, mine, sent):
    @pl.when(coords[2] >= 2)
    def _():
        mine[...] = high[...] + high_in[...]
        sent[...] = low[...] + low_in[...]

    @pl.when(coords[2] < 2)
    def _():
        mine[...] = low[...] + low_in[...]
        sent[...] = high[...] + high_in[...]


def renew_gains(grads, arrived, moments, gains, grads_out, moments_out, gains_out):
    for i in range(2):
        grad = grads[i] + arrived[i]
        moment = DECAY_RATE * moments[i : i + 1] + (1.0 - DECAY_RATE) * grad * grad
        grads_out[i : i + 1] = grad
        moments_out[i : i + 1] = moment
        gains_out[i : i + 1] = gains[i : i + 1] - GAIN_RATE * grad / (jnp.sqrt(moment) + 1e-08)


def sum_of(left, right, out):
    @pl.loop(0, left.shape[0])
    def _(i):
        out[i] = left[i] + right[i]


def run_split(coords, kept, arrived):
    shape = shape_of(kept.shape[0], 2, 3, BLOCK, STRIP)
    outs = call(
        split_sum,
        "split_sum",
        [SMEM, VMEM, VMEM],
        [(VMEM, shape)] * 4,
        [],
        math_size(kept.shape),
        (coords, kept, arrived),
        mib=4,
    )
    return outs[:2], outs[2:]


def run_again(coords, kept, arrived):
    shape = shape_of(kept[0].shape[0], 3, BLOCK, STRIP)
    outs = call(
        split_again,
        "split_again",
        [SMEM] + [VMEM] * 4,
        [(VMEM, shape)] * 4,
        [],
        2 * math_size(kept[0].shape),
        (coords, *kept, *arrived),
        mib=4,
    )
    return outs[:2], outs[2:]


def run_join(coords, kept, arrived):
    return call(
        join_sum,
        "join_sum",
        [SMEM] + [VMEM] * 4,
        [(VMEM, shape_of(OWN, BLOCK, STRIP))] * 2,
        [],
        2 * math_size(kept[0].shape),
        (coords, *kept, *arrived),
        mib=4,
    )


def run_pick(coords, high, high_in, low, low_in):
    return call(
        pick_sum,
        "pick_sum",
        [SMEM] + [VMEM] * 4,
        [(VMEM, shape_of(OWN, BLOCK, STRIP))] * 2,
        [],
        1,
        (coords, high, high_in, low, low_in),
        mib=4,
    )


def run_sum(left, right):
    return call(
        sum_of,
        "sum_of",
        [VMEM] * 2,
        [(VMEM, jax.ShapeDtypeStruct(left.shape, left.dtype))],
        [],
        math_size(left.shape),
        (left, right),
        mib=4,
    )[0]


def run_gains(grads, arrived, moments, gains):
    return call(
        renew_gains,
        "renew_gains",
        [VMEM] * 4,
        [(VMEM, shape_of(2, D, dtype=F32))] * 3,
        [],
        1,
        (grads, arrived, moments, gains),
        mib=4,
    )


def core_hop(sent):
    return lax.ppermute(sent, "dp", OTHER_CORE)


def first_hop(sent):
    return lax.ppermute(sent[0], "tensor", OTHER_Y), lax.ppermute(sent[1], "dp", OTHER_X)


def second_hop(sent):
    return lax.ppermute(sent[0], "dp", OTHER_X), lax.ppermute(sent[1], "tensor", OTHER_Y)


def precise(left, right, left_dim=1, right_dim=0):
    left_high, right_high = left.astype(BF16), right.astype(BF16)
    left_low = (left - left_high.astype(F32)).astype(BF16)
    right_low = (right - right_high.astype(F32)).astype(BF16)
    small = mm(left_high, right_low, left_dim, right_dim) + mm(
        left_low, right_high, left_dim, right_dim
    )
    return mm(left_high, right_high, left_dim, right_dim) + small


def update(mine, arrived, master, stat_left, stat_right, root_left, root_right, *outs):
    grad_out, left_out, right_out, master_out, copy_out = outs
    strip = pl.program_id(0)
    grad = mine[strip].astype(F32) + arrived[strip].astype(F32)
    blocks = [4 * strip + i for i in range(4)]
    grads = [grad[:, i * BLOCK : (i + 1) * BLOCK] for i in range(4)]
    sides = [precise(g, root_right[block]) for g, block in zip(grads, blocks)]
    lefts = [precise(g, g, 1, 1) for g in grads]
    rights = [precise(g, g, 0, 0) for g in grads]
    directions = [precise(root_left[block], side) for side, block in zip(sides, blocks)]
    for i, block in enumerate(blocks):
        grad_out[i] = grads[i]
        left_out[i] = DECAY_RATE * stat_left[block] + (1.0 - DECAY_RATE) * lefts[i]
        right_out[i] = DECAY_RATE * stat_right[block] + (1.0 - DECAY_RATE) * rights[i]
        new = master[block] - STEP_RATE * directions[i]
        master_out[i] = new
        copy_out[i] = new.astype(BF16)


def run_update(sums, blocks):
    count = blocks[0].shape[0]
    tile = pl.BlockSpec((4, BLOCK, BLOCK), lambda i: (i, 0, 0))
    shape = shape_of(count, BLOCK, BLOCK, dtype=F32)
    return call(
        update,
        "update",
        [VMEM] * (len(sums) + len(blocks)),
        [(tile, shape)] * 4 + [(tile, shape_of(count, BLOCK, BLOCK))],
        [],
        12 * 2 * count * BLOCK**3,
        (*sums, *blocks),
        grid=(count // 4,),
        mib=4,
    )


def sum_hops():
    hops = []
    for axis in ("tensor", "dp"):
        size, step = lax.axis_size(axis), 1
        while step < size:
            hops.append((axis, [(i, i ^ step) for i in range(size)]))
            step *= 2
    return hops


def plain_update(grad, master, stat_left, stat_right, root_left, root_right):
    left_new = DECAY_RATE * stat_left + (1.0 - DECAY_RATE) * jnp.einsum(
        "nij,nkj->nik", grad, grad, precision=PRECISE
    )
    right_new = DECAY_RATE * stat_right + (1.0 - DECAY_RATE) * jnp.einsum(
        "nji,njk->nik", grad, grad, precision=PRECISE
    )
    right_side = jnp.einsum("nij,njk->nik", grad, root_right, precision=PRECISE)
    direction = jnp.einsum("nij,njk->nik", root_left, right_side, precision=PRECISE)
    master_new = master - STEP_RATE * direction
    return grad, left_new, right_new, master_new, master_new.astype(BF16)


def body(
    tokens,
    token_mask,
    norm_gains,
    gain_moments,
    cotangent,
    master,
    stat_left,
    stat_right,
    root_left,
    root_right,
):
    rows = tokens.shape[0]
    own_caps = cotangent.shape[0]
    own = master.shape[0]
    split = lax.axis_size("dp") == 16 and lax.axis_size("tensor") == 2
    dp_pos, half = lax.axis_index("dp"), lax.axis_index("tensor")
    coords = jnp.stack([dp_pos % 2, dp_pos // 2 % 2, dp_pos // 4, half]).astype(jnp.int32)

    coords, master = fence(coords, master)
    first = functools.partial(run_prepare, coords, token_mask, cotangent, tokens, norm_gains)
    if split:
        strips, prepared = gather_split(master, coords, first)
    else:
        strips, prepared = gather_weights(master), first()
    mask, share, out_wide, inverse, normed = prepared
    qkv, attended, after, normed_two, after_pooled = run_forward(
        tokens, norm_gains, normed, mask, share, strips
    )
    hidden_pooled, grad_two, *held = run_mlp(coords, normed_two, out_wide, strips, split)
    hops = sum_hops()
    blocks = (master, stat_left, stat_right, root_left, root_right)
    if not split:
        grad_after, gain_two, grad_att, *held = run_output(
            coords, norm_gains, attended, after, cotangent, share, grad_two, strips, held, split
        )
        grad_mixed, *held = run_backward(coords, mask, normed, qkv, grad_att, held, split)
        input_grad, gain_grads = run_input(
            tokens, norm_gains, grad_mixed, grad_after, gain_two, strips
        )
        pooled = run_pool(after_pooled, hidden_pooled, inverse, strips)
        for hop in hops[:-1]:
            gain_grads = run_sum(gain_grads, lax.ppermute(gain_grads, *hop))
        gain_in = lax.ppermute(gain_grads, *hops[-1])
        gain_results = run_gains(gain_grads, gain_in, gain_moments, norm_gains)
        updated = plain_update(scatter_flat(held[0], own), *blocks)
    else:
        upper_kept, upper_sent, *lower = held
        upper_in = core_hop(upper_sent)
        grad_after, gain_two, grad_att, *lower = run_output(
            coords, norm_gains, attended, after, cotangent, share, grad_two, strips, lower, split
        )
        upper_in, grad_att, lower = fence(upper_in, grad_att, lower)

        upper_sent, upper_kept = run_split(coords, upper_kept, upper_in)
        upper_sent, grad_att, lower = fence(upper_sent, grad_att, lower)
        upper_in = first_hop(upper_sent)
        grad_mixed, *lower = run_backward(coords, mask, normed, qkv, grad_att, lower, split)
        upper_in, grad_mixed, lower = fence(upper_in, grad_mixed, lower)

        lower_in = core_hop(lower[1])
        upper_sent, upper_kept = run_again(coords, upper_kept, upper_in)
        upper_in = second_hop(upper_sent)
        lower_in, upper_sent, grad_mixed = fence(lower_in, upper_sent, grad_mixed)

        lower_sent, lower_kept = run_split(coords, lower[0], lower_in)
        lower_sent, grad_mixed = fence(lower_sent, grad_mixed)
        lower_in = first_hop(lower_sent)
        input_grad, gain_grads = run_input(
            tokens, norm_gains, grad_mixed, grad_after, gain_two, strips
        )
        upper_in, gain_grads = fence(upper_in, gain_grads)

        gain_in = lax.ppermute(gain_grads, *hops[0])
        pooled = run_pool(after_pooled, hidden_pooled, inverse, strips)
        high, high_sent = run_join(coords, upper_kept, upper_in)
        high_in = lax.ppermute(high_sent, "dp", NEAR_Z)
        high_in, lower_in, gain_in, pooled = fence(high_in, lower_in, gain_in, pooled)

        lower_sent, lower_kept = run_again(coords, lower_kept, lower_in)
        lower_in = second_hop(lower_sent)
        gain_grads = run_sum(gain_grads, gain_in)
        gain_in = lax.ppermute(gain_grads, *hops[1])
        lower_in, gain_in = fence(lower_in, gain_in)

        low, low_sent = run_join(coords, lower_kept, lower_in)
        low_in = lax.ppermute(low_sent, "dp", NEAR_Z)
        gain_grads = run_sum(gain_grads, gain_in)
        gain_in = lax.ppermute(gain_grads, *hops[2])
        low_in, gain_in = fence(low_in, gain_in)

        mine, sent = run_pick(coords, high, high_in, low, low_in)
        arrived = lax.ppermute(sent, "dp", FAR_Z)
        gain_grads = run_sum(gain_grads, gain_in)
        gain_in = lax.ppermute(gain_grads, *hops[3])
        gain_grads = run_sum(gain_grads, gain_in)
        gain_in = lax.ppermute(gain_grads, *hops[4])
        gain_results = run_gains(gain_grads, gain_in, gain_moments, norm_gains)
        arrived, gain_results = fence(arrived, gain_results)

        updated = run_update((mine, arrived), blocks)
    return (pooled, input_grad, *gain_results, *updated)


def solution(mesh):
    rows = P(("dp", "tensor"), None)
    blocks = P(("dp", "tensor"), None, None)
    return jax.shard_map(
        body,
        mesh=mesh,
        in_specs=(rows, P("dp", None), P(), P(), rows) + (blocks,) * 5,
        out_specs=(rows, rows, P(), P(), P()) + (blocks,) * 5,
        check_vma=False,
    )
```

```python
import functools

import jax
import jax.numpy as jnp
from jax import lax
from jax.experimental import pallas as pl
from jax.experimental.pallas import tpu as pltpu
from jax.sharding import PartitionSpec as P

D = 768
HEADS = 12
HD = 64
FF = 3072
BLOCK = 96
SLOTS = 16
HALVES = 2
STRIP = 4 * BLOCK
STRIPS = 96
OWN = 6
GROUP = 128
CAPS = GROUP // SLOTS
UPPER = (2, 3)
LOWER = (0, 1)
PAIR = 2 * HD

EPSILON = 1e-06
DECAY_RATE = 0.5
STEP_RATE = 0.25
GAIN_RATE = 0.3
MASKED_SCORE = -1e30
PRECISE = lax.Precision.HIGHEST
F32 = jnp.float32
BF16 = jnp.bfloat16


def mm(left, right, left_dim=1, right_dim=0):
    return lax.dot_general(
        left, right, (((left_dim,), (right_dim,)), ((), ())), preferred_element_type=F32
    )


def weight_of(strips, half, first, rows, width, columns):
    parts = [
        jnp.concatenate([strips[half, first + width * row + column] for row in range(rows)], axis=0)
        for column in columns
    ]
    return jnp.concatenate(parts, axis=1)


def out_weight(strips):
    halves = [weight_of(strips, half, 24, 4, 2, (0, 1)) for half in range(HALVES)]
    return jnp.concatenate(halves, axis=0)


def norm_parts(values):
    center = values - jnp.mean(values, axis=-1, keepdims=True)
    inverse = lax.rsqrt(jnp.mean(center * center, axis=-1, keepdims=True) + EPSILON)
    return center * inverse, inverse


def norm_back(xhat, inverse, gain, grad):
    scaled = grad * gain
    return inverse * (
        scaled
        - jnp.mean(scaled, axis=-1, keepdims=True)
        - xhat * jnp.mean(scaled * xhat, axis=-1, keepdims=True)
    )


def split_pair(values):
    first = lax.broadcasted_iota(jnp.int32, (GROUP, PAIR), 1) < HD
    zero = jnp.zeros_like(values)
    return jnp.concatenate(
        [jnp.where(first, values, zero), jnp.where(first, zero, values)], axis=0
    )


def join_pair(stacked):
    first = lax.broadcasted_iota(jnp.int32, (GROUP, PAIR), 1) < HD
    return jnp.where(first, stacked[:GROUP], stacked[GROUP:])


def caption_of():
    return lax.broadcasted_iota(jnp.int32, (SLOTS, 2 * GROUP), 1) % GROUP // SLOTS


def compact(full, caption):
    kept = full[0:SLOTS]
    for i in range(1, CAPS):
        kept = jnp.where(caption == i, full[i * SLOTS : (i + 1) * SLOTS], kept)
    return kept


def expand(kept, caption):
    zero = jnp.zeros_like(kept)
    return jnp.concatenate(
        [jnp.where(caption == i, kept, zero).astype(BF16) for i in range(CAPS)], axis=0
    )


def softmax_of(scores, bias):
    scores = scores * HD ** (-0.5) + bias
    shifted = jnp.exp(scores - jnp.max(scores, axis=0, keepdims=True))
    return shifted / jnp.sum(shifted, axis=0, keepdims=True)


def pairs_of():
    for half in range(HALVES):
        for start in range(0, STRIP, PAIR):
            yield half, slice(start, start + PAIR), slice(half * STRIP + start, half * STRIP + start + PAIR)


def columns(values, i):
    return values[:, 2 * GROUP * i : 2 * GROUP * (i + 1)]


def key_bias(mask):
    bias = jnp.where(mask > 0, 0.0, MASKED_SCORE)
    return jnp.concatenate([bias] * HEADS, axis=1)


def span_of(i, size=GROUP):
    return pl.ds(pl.multiple_of(i * size, size), size)


def prepare(coords, token_mask, cot, tok, gains, mask, share, out_wide, inverse, normed):
    captions = cot.shape[0]
    first = pl.multiple_of(coords[3] * captions, captions)
    own = token_mask[pl.ds(first, captions), :].astype(F32)
    count = jnp.broadcast_to(jnp.sum(own, axis=1, keepdims=True), (captions, PAIR))
    inverse[...] = 1.0 / count
    key = lax.broadcasted_iota(jnp.int32, (SLOTS, GROUP), 0).astype(F32)
    here = (
        lax.broadcasted_iota(jnp.int32, (CAPS, GROUP), 0)
        == lax.broadcasted_iota(jnp.int32, (CAPS, GROUP), 1) // SLOTS
    )
    slot = lax.broadcasted_iota(jnp.int32, (CAPS, SLOTS, PAIR), 1).astype(F32)
    caption = lax.broadcasted_iota(jnp.int32, (CAPS, SLOTS, PAIR), 0)
    lane = lax.broadcasted_iota(jnp.int32, (CAPS, SLOTS, PAIR), 2)
    for i in range(captions // CAPS):
        span, caps = slice(i * GROUP, (i + 1) * GROUP), slice(i * CAPS, (i + 1) * CAPS)
        number = count[caps]
        by_query = jnp.sum(jnp.where(here, number, 0.0), axis=0, keepdims=True)
        mask[i] = jnp.where(key < by_query, 1.0, 0.0)
        true = slot < number[:, None, :]
        weight = jnp.where(true, 1.0 / number[:, None, :], 0.0)
        share[span, :] = weight.reshape(GROUP, PAIR)
        seen = jnp.where(true & (caption + i * CAPS == lane), 1.0, 0.0)
        out_wide[span, D:] = seen.reshape(GROUP, PAIR).astype(BF16)
        for j in range(0, D, PAIR):
            lanes = slice(j, j + PAIR)
            value = (cot[caps, lanes].astype(F32)[:, None, :] * weight).reshape(GROUP, PAIR)
            out_wide[span, lanes] = value.astype(BF16)
        xhat, _ = norm_parts(tok[span, :].astype(F32))
        normed[span, :] = (xhat * gains[0:1, :]).astype(BF16)


def pool(values, share):
    parts = [
        values[:, i : i + PAIR] * share for i in range(0, values.shape[1], PAIR)
    ]
    weighted = jnp.concatenate(parts, axis=1)
    return jnp.sum(weighted.reshape(-1, SLOTS, values.shape[1]), axis=1)


def attention_forward(
    tok, gains, normed, mask, share, strips, qkv, attended, after, normed_two, after_pooled
):
    rows = tok.shape[0]

    for half in range(HALVES):
        mixed = mm(normed[...], weight_of(strips, half, 0, 8, 3, range(3))).astype(BF16)
        for part in range(3):
            qkv[3 * half + part] = mixed[:, part * STRIP : (part + 1) * STRIP]

    @pl.loop(0, rows // GROUP)
    def _(i):
        span = span_of(i)
        caption = caption_of()
        pairs = list(pairs_of())
        scores = [
            compact(
                mm(qkv[3 * half + 1, span, lanes], split_pair(qkv[3 * half, span, lanes]), 1, 1),
                caption,
            )
            for half, lanes, _ in pairs
        ]
        probs = softmax_of(jnp.concatenate(scores, axis=1), key_bias(mask[i]))
        for pair, (half, lanes, wide) in enumerate(pairs):
            spread = expand(columns(probs, pair), caption)
            mixed = mm(spread, qkv[3 * half + 2, span, lanes], 0, 0)
            attended[span, wide] = join_pair(mixed).astype(BF16)

    after[...] = mm(attended[...], out_weight(strips))

    @pl.loop(0, rows // GROUP)
    def _(i):
        span = span_of(i)
        summed = tok[span, :].astype(F32) + after[span, :]
        after[span, :] = summed
        after_pooled[span_of(i, CAPS), :] = pool(summed, share[span, :])
        xhat, _ = norm_parts(summed)
        normed_two[span, :] = (xhat * gains[1:2, :]).astype(BF16)


GELU_A = 0.7978845608028654
GELU_B = 0.044715


def gelu_both(v):
    square = v * v
    inner = jnp.tanh(GELU_A * v * (1.0 + GELU_B * square))
    half_up = 0.5 * (1.0 + inner)
    slope = half_up + (0.5 * GELU_A) * v * (1.0 - inner * inner) * (1.0 + (3.0 * GELU_B) * square)
    return v * half_up, slope


class Emitter:
    def __init__(self, targets, runs, coords):
        self.core = coords[0]
        self.whole = targets[0] if len(targets) == 1 else None
        self.batches = [] if self.whole is not None else list(zip(runs, targets[0::2], targets[1::2]))

    def store(self, pieces, here=True):
        if self.whole is not None:

            @pl.when(here)
            def _():
                for value, half, strip in pieces:
                    self.whole[half, strip] = value

            return
        for core in range(2):

            @pl.when((self.core == core) & here)
            def _():
                for value, half, strip in pieces:
                    plane, place = strip // (4 * OWN), strip // (2 * OWN) % 2
                    for run, kept, sent in self.batches:
                        if plane in run:
                            target = kept if strip // OWN % 2 == core else sent
                            target[plane - run[0], half, place, strip % OWN] = value


def strips_of(grad, rows, columns):
    return [
        (i, j, grad[i * BLOCK : (i + 1) * BLOCK, j * STRIP : (j + 1) * STRIP])
        for i in range(rows)
        for j in range(columns)
    ]


def mlp_both(coords, normed_two, out_wide, strips, *rest):
    hidden_pooled, grad_normed_two, *targets, hidden, grad_up = rest
    step = pl.program_id(0)
    rows = normed_two.shape[0]
    emit = Emitter(targets, (UPPER, LOWER), coords)
    half = step // 2
    column = lax.rem(step, 2)

    @pl.when(step == 0)
    def _():
        grad_normed_two[...] = jnp.zeros_like(grad_normed_two)

    up_weight = weight_of(strips, half, 32 + 2 * column, 8, 4, (0, 1))
    down_weight = weight_of(strips, half, 64 + 16 * column, 8, 2, (0, 1))
    chunk = 256
    for i in range(rows // chunk):
        span = slice(i * chunk, (i + 1) * chunk)
        act, slope = gelu_both(mm(normed_two[span, :], up_weight))
        hidden[span, :] = act.astype(BF16)
        grad = (mm(out_wide[span, :D], down_weight, 1, 1) * slope).astype(BF16)
        grad_up[span, :] = grad
        grad_normed_two[span, :] += mm(grad, up_weight, 1, 1)

    both = mm(hidden[...], out_wide[...], 0, 0)
    hidden_pooled[step] = both[:, D:]
    down_strips = strips_of(both[:, :D].astype(BF16), 8, 2)
    up_strips = strips_of(mm(normed_two[...], grad_up[...], 0, 0).astype(BF16), 8, 2)
    for i in range(2):
        pieces = [(value, half, 64 + 16 * i + 2 * row + part) for row, part, value in down_strips]
        pieces += [(value, half, 32 + 4 * row + 2 * i + part) for row, part, value in up_strips]
        emit.store(pieces, column == i)


def pool_out(after_pooled, hidden_pooled, inverse, strips, pooled):
    captions = pooled.shape[0]
    pooled[...] = after_pooled[...]
    for step in range(4):
        value = hidden_pooled[step]
        high = value.astype(BF16)
        low = (value - high.astype(F32)).astype(BF16)
        weight = weight_of(strips, step // 2, 64 + 16 * (step % 2), 8, 2, (0, 1))
        both = mm(jnp.concatenate([high, low], axis=1), weight, 0, 0)
        total = both[:captions] + both[PAIR : PAIR + captions]
        pooled[...] += total * jnp.concatenate([inverse[...]] * (D // PAIR), axis=1)


def output_backward(
    held, coords, gains, attended, after, cot, share, grad_normed_two, strips, *rest
):
    grad_after, gain_part, grad_att, *targets, after_low = rest[held:]
    rows = after.shape[0]
    emit = Emitter(targets, (LOWER,), coords)
    gain_part[...] = jnp.zeros_like(gain_part)

    @pl.loop(0, rows // GROUP)
    def _(i):
        span = span_of(i)
        xhat, inverse = norm_parts(after[span, :])
        grad = grad_normed_two[span, :]
        gain_part[...] += jnp.sum(grad * xhat, axis=0, keepdims=True)
        weight = share[span, :].reshape(CAPS, SLOTS, PAIR)
        parts = [
            (cot[span_of(i, CAPS), j : j + PAIR].astype(F32)[:, None, :] * weight)
            for j in range(0, D, PAIR)
        ]
        grad_out = jnp.concatenate([part.reshape(GROUP, PAIR) for part in parts], axis=1)
        value = grad_out + norm_back(xhat, inverse, gains[1:2, :], grad)
        grad_after[span, :] = value
        after_low[span, :] = value.astype(BF16)

    grad_att[...] = mm(after_low[...], out_weight(strips), 1, 1).astype(BF16)
    grad_w = mm(attended[...], after_low[...], 0, 0).astype(BF16)
    emit.store(
        [
            (value, row // 4, 24 + 2 * (row % 4) + part)
            for row, part, value in strips_of(grad_w, 8, 2)
        ]
    )


def attention_backward(held, coords, mask, normed, qkv, grad_att, *rest):
    grad_mixed, *targets = rest[held:]
    rows = normed.shape[0]
    emit = Emitter(targets, (LOWER,), coords)

    @pl.loop(0, rows // GROUP)
    def _(i):
        span = span_of(i)
        caption = caption_of()
        scale = HD ** (-0.5)
        pairs = list(pairs_of())
        scores = [
            compact(
                mm(qkv[3 * half + 1, span, lanes], split_pair(qkv[3 * half, span, lanes]), 1, 1),
                caption,
            )
            for half, lanes, _ in pairs
        ]
        grad_probs = [
            compact(
                mm(qkv[3 * half + 2, span, lanes], split_pair(grad_att[span, wide]), 1, 1), caption
            )
            for half, lanes, wide in pairs
        ]
        probs = softmax_of(jnp.concatenate(scores, axis=1), key_bias(mask[i]))
        grad_probs = jnp.concatenate(grad_probs, axis=1)
        inner = jnp.sum(probs * grad_probs, axis=0, keepdims=True)
        grad_scores = probs * (grad_probs - inner)
        for pair, (half, lanes, wide) in enumerate(pairs):
            spread = expand(columns(grad_scores, pair), caption)
            back = mm(spread, qkv[3 * half + 1, span, lanes], 0, 0)
            grad_mixed[3 * half, span, lanes] = (join_pair(back) * scale).astype(BF16)
            back = mm(spread, split_pair(qkv[3 * half, span, lanes]))
            grad_mixed[3 * half + 1, span, lanes] = (back * scale).astype(BF16)
            spread = expand(columns(probs, pair), caption)
            grad_mixed[3 * half + 2, span, lanes] = mm(
                spread, split_pair(grad_att[span, wide])
            ).astype(BF16)

    for half in range(HALVES):
        grads = jnp.concatenate([grad_mixed[3 * half + part] for part in range(3)], axis=1)
        grad_w = mm(normed[...], grads, 0, 0).astype(BF16)
        emit.store([(value, half, 3 * row + part) for row, part, value in strips_of(grad_w, 8, 3)])


def input_backward(tok, gains, grad_mixed, grad_after, gain_two, strips, input_grad, gain_part):
    rows = tok.shape[0]
    grads = jnp.concatenate([grad_mixed[part] for part in range(6)], axis=1)
    halves = [weight_of(strips, half, 0, 8, 3, range(3)) for half in range(HALVES)]
    input_grad[...] = mm(grads, jnp.concatenate(halves, axis=1), 1, 1)
    gain_part[0] = jnp.zeros_like(gain_two)
    gain_part[1] = gain_two[...]

    @pl.loop(0, rows // GROUP)
    def _(i):
        span = span_of(i)
        xhat, inverse = norm_parts(tok[span, :].astype(F32))
        grad = input_grad[span, :]
        gain_part[0] += jnp.sum(grad * xhat, axis=0, keepdims=True)
        input_grad[span, :] = grad_after[span, :] + norm_back(xhat, inverse, gains[0:1, :], grad)


def shape_of(*shape, dtype=BF16):
    return jax.ShapeDtypeStruct(shape, dtype)


VMEM = pl.BlockSpec(memory_space=pltpu.VMEM)
SMEM = pl.BlockSpec(memory_space=pltpu.SMEM)


def call(kernel, name, in_specs, outs, scratch, flops, args, grid=(1,), aliases=None, mib=10):
    moved = sum(math_size(a.shape) * a.dtype.itemsize for a in args)
    moved += sum(math_size(s.shape) * s.dtype.itemsize for _, s in outs)
    return pl.pallas_call(
        kernel,
        grid=grid,
        in_specs=in_specs,
        out_specs=[spec for spec, _ in outs],
        out_shape=[shape for _, shape in outs],
        scratch_shapes=scratch,
        input_output_aliases=aliases or {},
        compiler_params=pltpu.CompilerParams(
            dimension_semantics=("arbitrary",) * len(grid), vmem_limit_bytes=mib << 20
        ),
        cost_estimate=pl.CostEstimate(flops=1, bytes_accessed=1, transcendentals=0),
        name=name,
    )(*args)


def math_size(shape):
    size = 1
    for extent in shape:
        size *= extent
    return size


UNIT = 2 * 768 * 768 * 768


def run_prepare(coords, token_mask, cot, tok, gains):
    captions = cot.shape[0]
    rows = captions * SLOTS
    return call(
        prepare,
        "prepare",
        [SMEM] + [VMEM] * 4,
        [
            (VMEM, shape_of(rows // GROUP, SLOTS, GROUP, dtype=F32)),
            (VMEM, shape_of(rows, PAIR, dtype=F32)),
            (VMEM, shape_of(rows, D + PAIR)),
            (VMEM, shape_of(captions, PAIR, dtype=F32)),
            (VMEM, shape_of(rows, D)),
        ],
        [],
        1,
        (coords, token_mask, cot, tok, gains),
        mib=6,
    )


def run_forward(tok, gains, normed, mask, share, strips):
    rows = tok.shape[0]
    return call(
        attention_forward,
        "attention_forward",
        [VMEM] * 6,
        [
            (VMEM, shape_of(6, rows, STRIP)),
            (VMEM, shape_of(rows, D)),
            (VMEM, shape_of(rows, D, dtype=F32)),
            (VMEM, shape_of(rows, D)),
            (VMEM, shape_of(rows // SLOTS, D, dtype=F32)),
        ],
        [],
        5 * UNIT,
        (tok, gains, normed, mask, share, strips),
        mib=3,
    )


def targets_of(runs, split):
    if split:
        shapes = [shape_of(len(run), HALVES, 2, OWN, BLOCK, STRIP) for run in runs for _ in range(2)]
    else:
        shapes = [shape_of(HALVES, STRIPS, BLOCK, STRIP)]
    return [(VMEM, shape) for shape in shapes]


def run_mlp(coords, normed_two, out_wide, strips, split):
    rows = normed_two.shape[0]
    return call(
        mlp_both,
        "mlp_both",
        [SMEM] + [VMEM] * 3,
        [(VMEM, shape_of(4, D, PAIR, dtype=F32)), (VMEM, shape_of(rows, D, dtype=F32))]
        + targets_of((UPPER, LOWER), split),
        [pltpu.VMEM((rows, D), BF16), pltpu.VMEM((rows, D), BF16)],
        20 * UNIT,
        (coords, normed_two, out_wide, strips),
        grid=(4,),
        mib=6 if split else 44,
    )


def run_pool(after_pooled, hidden_pooled, inverse, strips):
    return call(
        pool_out,
        "pool_out",
        [VMEM] * 4,
        [(VMEM, jax.ShapeDtypeStruct(after_pooled.shape, F32))],
        [],
        UNIT // 2,
        (after_pooled, hidden_pooled, inverse, strips),
        mib=6,
    )[0]


def run_output(coords, gains, attended, after, cot, share, grad_two, strips, held, split):
    rows = after.shape[0]
    return call(
        functools.partial(output_backward, len(held)),
        "output_backward",
        [SMEM] + [VMEM] * (7 + len(held)),
        [
            (VMEM, shape_of(rows, D, dtype=F32)),
            (VMEM, shape_of(1, D, dtype=F32)),
            (VMEM, shape_of(rows, D)),
        ]
        + targets_of((LOWER,), split),
        [pltpu.VMEM((rows, D), BF16)],
        2 * UNIT,
        (coords, gains, attended, after, cot, share, grad_two, strips, *held),
        aliases={8 + i: 3 + i for i in range(len(held))},
        mib=6 if split else 56,
    )


def run_backward(coords, mask, normed, qkv, grad_att, held, split):
    rows = normed.shape[0]
    return call(
        functools.partial(attention_backward, len(held)),
        "attention_backward",
        [SMEM, VMEM, VMEM, VMEM, VMEM] + [VMEM] * len(held),
        [(VMEM, shape_of(6, rows, STRIP))] + targets_of((LOWER,), split),
        [],
        7 * UNIT,
        (coords, mask, normed, qkv, grad_att, *held),
        aliases={5 + i: 1 + i for i in range(len(held))},
        mib=6 if split else 56,
    )


def run_input(tok, gains, grad_mixed, grad_after, gain_two, strips):
    rows = tok.shape[0]
    return call(
        input_backward,
        "input_backward",
        [VMEM] * 6,
        [(VMEM, shape_of(rows, D, dtype=F32)), (VMEM, shape_of(2, 1, D, dtype=F32))],
        [],
        3 * UNIT,
        (tok, gains, grad_mixed, grad_after, gain_two, strips),
        mib=5,
    )


def to_strips(blocks):
    count = blocks.shape[0] // 4
    return blocks.reshape(count, 4, BLOCK, BLOCK).transpose(0, 2, 1, 3).reshape(count, BLOCK, STRIP)


def to_blocks(strips):
    count = strips.shape[0]
    return strips.reshape(count, BLOCK, 4, BLOCK).transpose(0, 2, 1, 3).reshape(-1, BLOCK, BLOCK)


EVERY = ("tensor", "dp")


def gather_weights(master):
    low = master.astype(BF16)
    own = low.shape[0]
    if own % 4 == 0:
        strips = to_strips(low).reshape(-1, STRIP)
        strips = lax.all_gather(strips, EVERY, axis=0, tiled=True)
        return strips.reshape(HALVES, STRIPS, BLOCK, STRIP)
    blocks = lax.all_gather(low, EVERY, axis=0, tiled=True)
    return to_strips(blocks).reshape(HALVES, STRIPS, BLOCK, STRIP)


def pack(master, out):
    for strip in range(master.shape[0] // 4):
        parts = [master[4 * strip + i].astype(BF16) for i in range(4)]
        out[0, strip] = jnp.concatenate(parts, axis=1)


def take_halves(by_x, by_y, from_x, from_y):
    for plane in range(by_x.shape[0]):
        from_x[plane] = by_x[plane, 0:3]
        from_y[plane] = by_y[plane, 3:6]


def take_both(one, two, out):
    out[0] = one[0]
    out[1] = two[0]


def place_own(held, planes, coords, own, by_x, by_y, across_one, across_two, *rest):
    whole, sent = rest[held:]
    core, place, plane, half = coords[0], coords[1], coords[2], coords[3]
    for i, apart in enumerate(planes):
        z = plane ^ apart

        def put(y, x, strips, value):
            sent[i, y, x, strips] = value
            whole[y, z, x, core, strips] = value

        put(half, place, slice(0, 6), own[i])
        put(half, 1 - place, slice(0, 6), by_x[i])
        put(1 - half, place, slice(0, 6), by_y[i])
        put(1 - half, 1 - place, slice(0, 3), across_one[i])
        put(1 - half, 1 - place, slice(3, 6), across_two[i])


def place_other(planes, coords, arrived, _, whole):
    core, plane = coords[0], coords[2]
    for i, apart in enumerate(planes):
        for y in range(2):
            for x in range(2):
                whole[y, plane ^ apart, x, 1 - core] = arrived[i, y, x]


WHOLE = (HALVES, 4, 2, 2, OWN, BLOCK, STRIP)


def run_pack(master):
    return call(
        pack,
        "pack",
        [VMEM],
        [(VMEM, shape_of(1, OWN, BLOCK, STRIP))],
        [],
        math_size(master.shape),
        (master,),
        mib=4,
    )[0]


def run_halves(by_x, by_y):
    shape = shape_of(by_x.shape[0], 3, BLOCK, STRIP)
    return call(
        take_halves, "take_halves", [VMEM] * 2, [(VMEM, shape)] * 2, [], 1, (by_x, by_y), mib=4
    )


def run_both(one, two):
    shape = shape_of(2, OWN, BLOCK, STRIP)
    return call(take_both, "take_both", [VMEM] * 2, [(VMEM, shape)], [], 1, (one, two), mib=4)[0]


def run_place_own(planes, coords, pieces, held):
    count = len(planes)
    return call(
        functools.partial(place_own, len(held), planes),
        "place_own",
        [SMEM] + [VMEM] * (5 + len(held)),
        [(VMEM, shape_of(*WHOLE)), (VMEM, shape_of(count, HALVES, 2, OWN, BLOCK, STRIP))],
        [],
        1,
        (coords, *pieces, *held),
        aliases={6: 0} if held else None,
        mib=4,
    )


def run_place_other(planes, coords, arrived, whole):
    return call(
        functools.partial(place_other, planes),
        "place_other",
        [SMEM] + [VMEM] * 2,
        [(VMEM, shape_of(*WHOLE))],
        [],
        1,
        (coords, arrived, whole),
        aliases={2: 0},
        mib=4,
    )[0]


def neighbour_hop(value):
    return lax.ppermute(value, "dp", OTHER_X), lax.ppermute(value, "tensor", OTHER_Y)


def across_hop(pieces):
    return lax.ppermute(pieces[0], "tensor", OTHER_Y), lax.ppermute(pieces[1], "dp", OTHER_X)


def gather_split(master, coords, prepare):
    own = run_pack(master)
    near = lax.ppermute(own, "dp", NEAR_Z)
    far = lax.ppermute(own, "dp", FAR_Z)
    own_by = neighbour_hop(own)
    own_by, prepared = fence(own_by, prepare())
    own_across = across_hop(run_halves(*own_by))
    near, far, own_across, own_by, own, prepared = fence(near, far, own_across, own_by, own, prepared)

    both = run_both(near, far)
    both_by = neighbour_hop(both)
    other = lax.ppermute(far, "dp", NEAR_Z)
    other_by = neighbour_hop(other)
    both_across = across_hop(run_halves(*both_by))
    whole, sent = run_place_own((0,), coords, (own, *own_by, *own_across), ())
    own_in = core_hop(sent)
    both_across, other_by, own_in, whole = fence(both_across, other_by, own_in, whole)

    other_across = across_hop(run_halves(*other_by))
    whole, sent = run_place_own((1, 2), coords, (both, *both_by, *both_across), (whole,))
    both_in = core_hop(sent)
    whole = run_place_other((0,), coords, own_in, whole)
    other_across, both_in, whole = fence(other_across, both_in, whole)

    whole, sent = run_place_own((3,), coords, (other, *other_by, *other_across), (whole,))
    other_in = core_hop(sent)
    whole = run_place_other((1, 2), coords, both_in, whole)
    other_in, whole = fence(other_in, whole)
    whole = run_place_other((3,), coords, other_in, whole)
    return whole.reshape(HALVES, STRIPS, BLOCK, STRIP), prepared


def scatter_flat(strips, own):
    if own % 4 == 0:
        mine = lax.psum_scatter(
            strips.reshape(-1, STRIP), EVERY, scatter_dimension=0, tiled=True
        )
        return to_blocks(mine.reshape(-1, BLOCK, STRIP)).astype(F32)
    blocks = to_blocks(strips.reshape(-1, BLOCK, STRIP))
    return lax.psum_scatter(blocks, EVERY, scatter_dimension=0, tiled=True).astype(F32)


def fence(*values):
    return lax.optimization_barrier(values)


OTHER_CORE = [(i, i ^ 1) for i in range(16)]
OTHER_X = [(i, i ^ 2) for i in range(16)]
OTHER_Y = [(0, 1), (1, 0)]


def by_plane(*moves):
    return [(4 * a + i, 4 * b + i) for a, b in moves for i in range(4)]


NEAR_Z = by_plane((0, 1), (1, 0), (2, 3), (3, 2))
FAR_Z = by_plane((0, 2), (1, 3), (2, 0), (3, 1))


def split_sum(coords, kept, arrived, sent_one, sent_two, kept_one, kept_two):
    place, half = coords[1], coords[3]

    @pl.loop(0, 2 * kept.shape[0])
    def _(step):
        plane, i = step // 2, lax.rem(step, 2)
        one, two = pl.ds(0, 3), pl.ds(3, 3)
        sent_one[plane, i] = kept[plane, 1 - half, i, one] + arrived[plane, 1 - half, i, one]
        kept_one[plane, i] = kept[plane, half, i, one] + arrived[plane, half, i, one]
        sent_two[plane, i] = kept[plane, i, 1 - place, two] + arrived[plane, i, 1 - place, two]
        kept_two[plane, i] = kept[plane, i, place, two] + arrived[plane, i, place, two]


def split_again(coords, one, two, one_in, two_in, sent_one, sent_two, kept_one, kept_two):
    place, half = coords[1], coords[3]

    @pl.loop(0, one.shape[0])
    def _(plane):
        sent_one[plane] = one[plane, 1 - place] + one_in[plane, 1 - place]
        kept_one[plane] = one[plane, place] + one_in[plane, place]
        sent_two[plane] = two[plane, 1 - half] + two_in[plane, 1 - half]
        kept_two[plane] = two[plane, half] + two_in[plane, half]


def join_sum(coords, one, two, one_in, two_in, *outs):
    for i, out in enumerate(outs):
        plane = lax.rem(coords[2] + i, 2)
        out[0:3] = one[plane] + one_in[plane]
        out[3:6] = two[plane] + two_in[plane]


def pick_sum(coords, high, high_in, low, low_in, mine, sent):
    @pl.when(coords[2] >= 2)
    def _():
        mine[...] = high[...] + high_in[...]
        sent[...] = low[...] + low_in[...]

    @pl.when(coords[2] < 2)
    def _():
        mine[...] = low[...] + low_in[...]
        sent[...] = high[...] + high_in[...]


def renew_gains(grads, arrived, moments, gains, grads_out, moments_out, gains_out):
    for i in range(2):
        grad = grads[i] + arrived[i]
        moment = DECAY_RATE * moments[i : i + 1] + (1.0 - DECAY_RATE) * grad * grad
        grads_out[i : i + 1] = grad
        moments_out[i : i + 1] = moment
        gains_out[i : i + 1] = gains[i : i + 1] - GAIN_RATE * grad / (jnp.sqrt(moment) + 1e-08)


def sum_of(left, right, out):
    @pl.loop(0, left.shape[0])
    def _(i):
        out[i] = left[i] + right[i]


def run_split(coords, kept, arrived):
    shape = shape_of(kept.shape[0], 2, 3, BLOCK, STRIP)
    outs = call(
        split_sum,
        "split_sum",
        [SMEM, VMEM, VMEM],
        [(VMEM, shape)] * 4,
        [],
        math_size(kept.shape),
        (coords, kept, arrived),
        mib=4,
    )
    return outs[:2], outs[2:]


def run_again(coords, kept, arrived):
    shape = shape_of(kept[0].shape[0], 3, BLOCK, STRIP)
    outs = call(
        split_again,
        "split_again",
        [SMEM] + [VMEM] * 4,
        [(VMEM, shape)] * 4,
        [],
        2 * math_size(kept[0].shape),
        (coords, *kept, *arrived),
        mib=4,
    )
    return outs[:2], outs[2:]


def run_join(coords, kept, arrived):
    return call(
        join_sum,
        "join_sum",
        [SMEM] + [VMEM] * 4,
        [(VMEM, shape_of(OWN, BLOCK, STRIP))] * 2,
        [],
        2 * math_size(kept[0].shape),
        (coords, *kept, *arrived),
        mib=4,
    )


def run_pick(coords, high, high_in, low, low_in):
    return call(
        pick_sum,
        "pick_sum",
        [SMEM] + [VMEM] * 4,
        [(VMEM, shape_of(OWN, BLOCK, STRIP))] * 2,
        [],
        1,
        (coords, high, high_in, low, low_in),
        mib=4,
    )


def run_sum(left, right):
    return call(
        sum_of,
        "sum_of",
        [VMEM] * 2,
        [(VMEM, jax.ShapeDtypeStruct(left.shape, left.dtype))],
        [],
        math_size(left.shape),
        (left, right),
        mib=4,
    )[0]


def run_gains(grads, arrived, moments, gains):
    return call(
        renew_gains,
        "renew_gains",
        [VMEM] * 4,
        [(VMEM, shape_of(2, D, dtype=F32))] * 3,
        [],
        1,
        (grads, arrived, moments, gains),
        mib=4,
    )


def core_hop(sent):
    return lax.ppermute(sent, "dp", OTHER_CORE)


def first_hop(sent):
    return lax.ppermute(sent[0], "tensor", OTHER_Y), lax.ppermute(sent[1], "dp", OTHER_X)


def second_hop(sent):
    return lax.ppermute(sent[0], "dp", OTHER_X), lax.ppermute(sent[1], "tensor", OTHER_Y)


def precise(left, right, left_dim=1, right_dim=0):
    left_high, right_high = left.astype(BF16), right.astype(BF16)
    left_low = (left - left_high.astype(F32)).astype(BF16)
    right_low = (right - right_high.astype(F32)).astype(BF16)
    small = mm(left_high, right_low, left_dim, right_dim) + mm(
        left_low, right_high, left_dim, right_dim
    )
    return mm(left_high, right_high, left_dim, right_dim) + small


def update(mine, arrived, master, stat_left, stat_right, root_left, root_right, *outs):
    grad_out, left_out, right_out, master_out, copy_out = outs
    strip = pl.program_id(0)
    grad = mine[strip].astype(F32) + arrived[strip].astype(F32)
    blocks = [4 * strip + i for i in range(4)]
    grads = [grad[:, i * BLOCK : (i + 1) * BLOCK] for i in range(4)]
    sides = [precise(g, root_right[block]) for g, block in zip(grads, blocks)]
    lefts = [precise(g, g, 1, 1) for g in grads]
    rights = [precise(g, g, 0, 0) for g in grads]
    directions = [precise(root_left[block], side) for side, block in zip(sides, blocks)]
    for i, block in enumerate(blocks):
        grad_out[i] = grads[i]
        left_out[i] = DECAY_RATE * stat_left[block] + (1.0 - DECAY_RATE) * lefts[i]
        right_out[i] = DECAY_RATE * stat_right[block] + (1.0 - DECAY_RATE) * rights[i]
        new = master[block] - STEP_RATE * directions[i]
        master_out[i] = new
        copy_out[i] = new.astype(BF16)


def run_update(sums, blocks):
    count = blocks[0].shape[0]
    tile = pl.BlockSpec((4, BLOCK, BLOCK), lambda i: (i, 0, 0))
    shape = shape_of(count, BLOCK, BLOCK, dtype=F32)
    return call(
        update,
        "update",
        [VMEM] * (len(sums) + len(blocks)),
        [(tile, shape)] * 4 + [(tile, shape_of(count, BLOCK, BLOCK))],
        [],
        12 * 2 * count * BLOCK**3,
        (*sums, *blocks),
        grid=(count // 4,),
        mib=4,
    )


def sum_hops():
    hops = []
    for axis in ("tensor", "dp"):
        size, step = lax.axis_size(axis), 1
        while step < size:
            hops.append((axis, [(i, i ^ step) for i in range(size)]))
            step *= 2
    return hops


def plain_update(grad, master, stat_left, stat_right, root_left, root_right):
    left_new = DECAY_RATE * stat_left + (1.0 - DECAY_RATE) * jnp.einsum(
        "nij,nkj->nik", grad, grad, precision=PRECISE
    )
    right_new = DECAY_RATE * stat_right + (1.0 - DECAY_RATE) * jnp.einsum(
        "nji,njk->nik", grad, grad, precision=PRECISE
    )
    right_side = jnp.einsum("nij,njk->nik", grad, root_right, precision=PRECISE)
    direction = jnp.einsum("nij,njk->nik", root_left, right_side, precision=PRECISE)
    master_new = master - STEP_RATE * direction
    return grad, left_new, right_new, master_new, master_new.astype(BF16)


def body(
    tokens,
    token_mask,
    norm_gains,
    gain_moments,
    cotangent,
    master,
    stat_left,
    stat_right,
    root_left,
    root_right,
):
    rows = tokens.shape[0]
    own_caps = cotangent.shape[0]
    own = master.shape[0]
    split = lax.axis_size("dp") == 16 and lax.axis_size("tensor") == 2
    dp_pos, half = lax.axis_index("dp"), lax.axis_index("tensor")
    coords = jnp.stack([dp_pos % 2, dp_pos // 2 % 2, dp_pos // 4, half]).astype(jnp.int32)

    coords, master = fence(coords, master)
    first = functools.partial(run_prepare, coords, token_mask, cotangent, tokens, norm_gains)
    if split:
        strips, prepared = gather_split(master, coords, first)
    else:
        strips, prepared = gather_weights(master), first()
    mask, share, out_wide, inverse, normed = prepared
    qkv, attended, after, normed_two, after_pooled = run_forward(
        tokens, norm_gains, normed, mask, share, strips
    )
    hidden_pooled, grad_two, *held = run_mlp(coords, normed_two, out_wide, strips, split)
    hops = sum_hops()
    blocks = (master, stat_left, stat_right, root_left, root_right)
    if not split:
        grad_after, gain_two, grad_att, *held = run_output(
            coords, norm_gains, attended, after, cotangent, share, grad_two, strips, held, split
        )
        grad_mixed, *held = run_backward(coords, mask, normed, qkv, grad_att, held, split)
        input_grad, gain_grads = run_input(
            tokens, norm_gains, grad_mixed, grad_after, gain_two, strips
        )
        pooled = run_pool(after_pooled, hidden_pooled, inverse, strips)
        for hop in hops[:-1]:
            gain_grads = run_sum(gain_grads, lax.ppermute(gain_grads, *hop))
        gain_in = lax.ppermute(gain_grads, *hops[-1])
        gain_results = run_gains(gain_grads, gain_in, gain_moments, norm_gains)
        updated = plain_update(scatter_flat(held[0], own), *blocks)
    else:
        upper_kept, upper_sent, *lower = held
        upper_in = core_hop(upper_sent)
        grad_after, gain_two, grad_att, *lower = run_output(
            coords, norm_gains, attended, after, cotangent, share, grad_two, strips, lower, split
        )
        upper_in, grad_att, lower = fence(upper_in, grad_att, lower)

        upper_sent, upper_kept = run_split(coords, upper_kept, upper_in)
        upper_sent, grad_att, lower = fence(upper_sent, grad_att, lower)
        upper_in = first_hop(upper_sent)
        grad_mixed, *lower = run_backward(coords, mask, normed, qkv, grad_att, lower, split)
        upper_in, grad_mixed, lower = fence(upper_in, grad_mixed, lower)

        lower_in = core_hop(lower[1])
        upper_sent, upper_kept = run_again(coords, upper_kept, upper_in)
        upper_in = second_hop(upper_sent)

        lower_sent, lower_kept = run_split(coords, lower[0], lower_in)
        lower_in = first_hop(lower_sent)
        input_grad, gain_grads = run_input(
            tokens, norm_gains, grad_mixed, grad_after, gain_two, strips
        )

        gain_in = lax.ppermute(gain_grads, *hops[0])
        pooled = run_pool(after_pooled, hidden_pooled, inverse, strips)
        high, high_sent = run_join(coords, upper_kept, upper_in)
        high_in = lax.ppermute(high_sent, "dp", NEAR_Z)
        high_in, lower_in, gain_in, pooled = fence(high_in, lower_in, gain_in, pooled)

        lower_sent, lower_kept = run_again(coords, lower_kept, lower_in)
        lower_in = second_hop(lower_sent)
        gain_grads = run_sum(gain_grads, gain_in)
        gain_in = lax.ppermute(gain_grads, *hops[1])
        lower_in, gain_in = fence(lower_in, gain_in)

        low, low_sent = run_join(coords, lower_kept, lower_in)
        low_in = lax.ppermute(low_sent, "dp", NEAR_Z)
        gain_grads = run_sum(gain_grads, gain_in)
        gain_in = lax.ppermute(gain_grads, *hops[2])
        low_in, gain_in = fence(low_in, gain_in)

        mine, sent = run_pick(coords, high, high_in, low, low_in)
        arrived = lax.ppermute(sent, "dp", FAR_Z)
        gain_grads = run_sum(gain_grads, gain_in)
        gain_in = lax.ppermute(gain_grads, *hops[3])
        gain_grads = run_sum(gain_grads, gain_in)
        gain_in = lax.ppermute(gain_grads, *hops[4])
        gain_results = run_gains(gain_grads, gain_in, gain_moments, norm_gains)
        arrived, gain_results = fence(arrived, gain_results)

        updated = run_update((mine, arrived), blocks)
    return (pooled, input_grad, *gain_results, *updated)


def solution(mesh):
    rows = P(("dp", "tensor"), None)
    blocks = P(("dp", "tensor"), None, None)
    return jax.shard_map(
        body,
        mesh=mesh,
        in_specs=(rows, P("dp", None), P(), P(), rows) + (blocks,) * 5,
        out_specs=(rows, rows, P(), P(), P()) + (blocks,) * 5,
        check_vma=False,
    )
```

```python
import functools

import jax
import jax.numpy as jnp
from jax import lax
from jax.experimental import pallas as pl
from jax.experimental.pallas import tpu as pltpu
from jax.sharding import PartitionSpec as P

D = 768
HEADS = 12
HD = 64
FF = 3072
BLOCK = 96
SLOTS = 16
HALVES = 2
STRIP = 4 * BLOCK
STRIPS = 96
OWN = 6
GROUP = 128
CAPS = GROUP // SLOTS
UPPER = (2, 3)
LOWER = (0, 1)
PAIR = 2 * HD

EPSILON = 1e-06
DECAY_RATE = 0.5
STEP_RATE = 0.25
GAIN_RATE = 0.3
MASKED_SCORE = -1e30
PRECISE = lax.Precision.HIGHEST
F32 = jnp.float32
BF16 = jnp.bfloat16


def mm(left, right, left_dim=1, right_dim=0):
    return lax.dot_general(
        left, right, (((left_dim,), (right_dim,)), ((), ())), preferred_element_type=F32
    )


def weight_of(strips, half, first, rows, width, columns):
    parts = [
        jnp.concatenate([strips[half, first + width * row + column] for row in range(rows)], axis=0)
        for column in columns
    ]
    return jnp.concatenate(parts, axis=1)


def out_weight(strips):
    halves = [weight_of(strips, half, 24, 4, 2, (0, 1)) for half in range(HALVES)]
    return jnp.concatenate(halves, axis=0)


def norm_parts(values):
    center = values - jnp.mean(values, axis=-1, keepdims=True)
    inverse = lax.rsqrt(jnp.mean(center * center, axis=-1, keepdims=True) + EPSILON)
    return center * inverse, inverse


def norm_back(xhat, inverse, gain, grad):
    scaled = grad * gain
    return inverse * (
        scaled
        - jnp.mean(scaled, axis=-1, keepdims=True)
        - xhat * jnp.mean(scaled * xhat, axis=-1, keepdims=True)
    )


def split_pair(values):
    first = lax.broadcasted_iota(jnp.int32, (GROUP, PAIR), 1) < HD
    zero = jnp.zeros_like(values)
    return jnp.concatenate(
        [jnp.where(first, values, zero), jnp.where(first, zero, values)], axis=0
    )


def join_pair(stacked):
    first = lax.broadcasted_iota(jnp.int32, (GROUP, PAIR), 1) < HD
    return jnp.where(first, stacked[:GROUP], stacked[GROUP:])


def caption_of():
    return lax.broadcasted_iota(jnp.int32, (SLOTS, 2 * GROUP), 1) % GROUP // SLOTS


def compact(full, caption):
    kept = full[0:SLOTS]
    for i in range(1, CAPS):
        kept = jnp.where(caption == i, full[i * SLOTS : (i + 1) * SLOTS], kept)
    return kept


def expand(kept, caption):
    zero = jnp.zeros_like(kept)
    return jnp.concatenate(
        [jnp.where(caption == i, kept, zero).astype(BF16) for i in range(CAPS)], axis=0
    )


def softmax_of(scores, bias):
    scores = scores * HD ** (-0.5) + bias
    shifted = jnp.exp(scores - jnp.max(scores, axis=0, keepdims=True))
    return shifted / jnp.sum(shifted, axis=0, keepdims=True)


def pairs_of():
    for half in range(HALVES):
        for start in range(0, STRIP, PAIR):
            yield half, slice(start, start + PAIR), slice(half * STRIP + start, half * STRIP + start + PAIR)


def columns(values, i):
    return values[:, 2 * GROUP * i : 2 * GROUP * (i + 1)]


def key_bias(mask):
    bias = jnp.where(mask > 0, 0.0, MASKED_SCORE)
    return jnp.concatenate([bias] * HEADS, axis=1)


def span_of(i, size=GROUP):
    return pl.ds(pl.multiple_of(i * size, size), size)


def prepare(coords, token_mask, cot, tok, gains, mask, share, out_wide, inverse, normed):
    captions = cot.shape[0]
    first = pl.multiple_of(coords[3] * captions, captions)
    own = token_mask[pl.ds(first, captions), :].astype(F32)
    count = jnp.broadcast_to(jnp.sum(own, axis=1, keepdims=True), (captions, PAIR))
    inverse[...] = 1.0 / count
    key = lax.broadcasted_iota(jnp.int32, (SLOTS, GROUP), 0).astype(F32)
    here = (
        lax.broadcasted_iota(jnp.int32, (CAPS, GROUP), 0)
        == lax.broadcasted_iota(jnp.int32, (CAPS, GROUP), 1) // SLOTS
    )
    slot = lax.broadcasted_iota(jnp.int32, (CAPS, SLOTS, PAIR), 1).astype(F32)
    caption = lax.broadcasted_iota(jnp.int32, (CAPS, SLOTS, PAIR), 0)
    lane = lax.broadcasted_iota(jnp.int32, (CAPS, SLOTS, PAIR), 2)
    for i in range(captions // CAPS):
        span, caps = slice(i * GROUP, (i + 1) * GROUP), slice(i * CAPS, (i + 1) * CAPS)
        number = count[caps]
        by_query = jnp.sum(jnp.where(here, number, 0.0), axis=0, keepdims=True)
        mask[i] = jnp.where(key < by_query, 1.0, 0.0)
        true = slot < number[:, None, :]
        weight = jnp.where(true, 1.0 / number[:, None, :], 0.0)
        share[span, :] = weight.reshape(GROUP, PAIR)
        seen = jnp.where(true & (caption + i * CAPS == lane), 1.0, 0.0)
        out_wide[span, D:] = seen.reshape(GROUP, PAIR).astype(BF16)
        for j in range(0, D, PAIR):
            lanes = slice(j, j + PAIR)
            value = (cot[caps, lanes].astype(F32)[:, None, :] * weight).reshape(GROUP, PAIR)
            out_wide[span, lanes] = value.astype(BF16)
        xhat, _ = norm_parts(tok[span, :].astype(F32))
        normed[span, :] = (xhat * gains[0:1, :]).astype(BF16)


def pool(values, share):
    parts = [
        values[:, i : i + PAIR] * share for i in range(0, values.shape[1], PAIR)
    ]
    weighted = jnp.concatenate(parts, axis=1)
    return jnp.sum(weighted.reshape(-1, SLOTS, values.shape[1]), axis=1)


def attention_forward(
    tok, gains, normed, mask, share, strips, qkv, attended, after, normed_two, after_pooled
):
    rows = tok.shape[0]

    for half in range(HALVES):
        mixed = mm(normed[...], weight_of(strips, half, 0, 8, 3, range(3))).astype(BF16)
        for part in range(3):
            qkv[3 * half + part] = mixed[:, part * STRIP : (part + 1) * STRIP]

    @pl.loop(0, rows // GROUP)
    def _(i):
        span = span_of(i)
        caption = caption_of()
        pairs = list(pairs_of())
        scores = [
            compact(
                mm(qkv[3 * half + 1, span, lanes], split_pair(qkv[3 * half, span, lanes]), 1, 1),
                caption,
            )
            for half, lanes, _ in pairs
        ]
        probs = softmax_of(jnp.concatenate(scores, axis=1), key_bias(mask[i]))
        for pair, (half, lanes, wide) in enumerate(pairs):
            spread = expand(columns(probs, pair), caption)
            mixed = mm(spread, qkv[3 * half + 2, span, lanes], 0, 0)
            attended[span, wide] = join_pair(mixed).astype(BF16)

    after[...] = mm(attended[...], out_weight(strips))

    @pl.loop(0, rows // GROUP)
    def _(i):
        span = span_of(i)
        summed = tok[span, :].astype(F32) + after[span, :]
        after[span, :] = summed
        after_pooled[span_of(i, CAPS), :] = pool(summed, share[span, :])
        xhat, _ = norm_parts(summed)
        normed_two[span, :] = (xhat * gains[1:2, :]).astype(BF16)


GELU_A = 0.7978845608028654
GELU_B = 0.044715


def gelu_both(v):
    square = v * v
    inner = jnp.tanh(GELU_A * v * (1.0 + GELU_B * square))
    half_up = 0.5 * (1.0 + inner)
    slope = half_up + (0.5 * GELU_A) * v * (1.0 - inner * inner) * (1.0 + (3.0 * GELU_B) * square)
    return v * half_up, slope


class Emitter:
    def __init__(self, targets, runs, coords):
        self.core = coords[0]
        self.whole = targets[0] if len(targets) == 1 else None
        self.batches = [] if self.whole is not None else list(zip(runs, targets[0::2], targets[1::2]))

    def store(self, pieces, here=True):
        if self.whole is not None:

            @pl.when(here)
            def _():
                for value, half, strip in pieces:
                    self.whole[half, strip] = value

            return
        for core in range(2):

            @pl.when((self.core == core) & here)
            def _():
                for value, half, strip in pieces:
                    plane, place = strip // (4 * OWN), strip // (2 * OWN) % 2
                    for run, kept, sent in self.batches:
                        if plane in run:
                            target = kept if strip // OWN % 2 == core else sent
                            target[plane - run[0], half, place, strip % OWN] = value


def strips_of(grad, rows, columns):
    return [
        (i, j, grad[i * BLOCK : (i + 1) * BLOCK, j * STRIP : (j + 1) * STRIP])
        for i in range(rows)
        for j in range(columns)
    ]


def mlp_both(coords, normed_two, out_wide, strips, *rest):
    hidden_pooled, grad_normed_two, *targets, hidden, grad_up = rest
    step = pl.program_id(0)
    rows = normed_two.shape[0]
    emit = Emitter(targets, (UPPER, LOWER), coords)
    half = step // 2
    column = lax.rem(step, 2)

    @pl.when(step == 0)
    def _():
        grad_normed_two[...] = jnp.zeros_like(grad_normed_two)

    up_weight = weight_of(strips, half, 32 + 2 * column, 8, 4, (0, 1))
    down_weight = weight_of(strips, half, 64 + 16 * column, 8, 2, (0, 1))
    chunk = 256
    for i in range(rows // chunk):
        span = slice(i * chunk, (i + 1) * chunk)
        act, slope = gelu_both(mm(normed_two[span, :], up_weight))
        hidden[span, :] = act.astype(BF16)
        grad = (mm(out_wide[span, :D], down_weight, 1, 1) * slope).astype(BF16)
        grad_up[span, :] = grad
        grad_normed_two[span, :] += mm(grad, up_weight, 1, 1)

    both = mm(hidden[...], out_wide[...], 0, 0)
    hidden_pooled[step] = both[:, D:]
    down_strips = strips_of(both[:, :D].astype(BF16), 8, 2)
    up_strips = strips_of(mm(normed_two[...], grad_up[...], 0, 0).astype(BF16), 8, 2)
    for i in range(2):
        pieces = [(value, half, 64 + 16 * i + 2 * row + part) for row, part, value in down_strips]
        pieces += [(value, half, 32 + 4 * row + 2 * i + part) for row, part, value in up_strips]
        emit.store(pieces, column == i)


def pool_out(after_pooled, hidden_pooled, inverse, strips, pooled):
    captions = pooled.shape[0]
    pooled[...] = after_pooled[...]
    for step in range(4):
        value = hidden_pooled[step]
        high = value.astype(BF16)
        low = (value - high.astype(F32)).astype(BF16)
        weight = weight_of(strips, step // 2, 64 + 16 * (step % 2), 8, 2, (0, 1))
        both = mm(jnp.concatenate([high, low], axis=1), weight, 0, 0)
        total = both[:captions] + both[PAIR : PAIR + captions]
        pooled[...] += total * jnp.concatenate([inverse[...]] * (D // PAIR), axis=1)


def output_backward(
    held, coords, gains, attended, after, cot, share, grad_normed_two, strips, *rest
):
    grad_after, gain_part, grad_att, *targets, after_low = rest[held:]
    rows = after.shape[0]
    emit = Emitter(targets, (LOWER,), coords)
    gain_part[...] = jnp.zeros_like(gain_part)

    @pl.loop(0, rows // GROUP)
    def _(i):
        span = span_of(i)
        xhat, inverse = norm_parts(after[span, :])
        grad = grad_normed_two[span, :]
        gain_part[...] += jnp.sum(grad * xhat, axis=0, keepdims=True)
        weight = share[span, :].reshape(CAPS, SLOTS, PAIR)
        parts = [
            (cot[span_of(i, CAPS), j : j + PAIR].astype(F32)[:, None, :] * weight)
            for j in range(0, D, PAIR)
        ]
        grad_out = jnp.concatenate([part.reshape(GROUP, PAIR) for part in parts], axis=1)
        value = grad_out + norm_back(xhat, inverse, gains[1:2, :], grad)
        grad_after[span, :] = value
        after_low[span, :] = value.astype(BF16)

    grad_att[...] = mm(after_low[...], out_weight(strips), 1, 1).astype(BF16)
    grad_w = mm(attended[...], after_low[...], 0, 0).astype(BF16)
    emit.store(
        [
            (value, row // 4, 24 + 2 * (row % 4) + part)
            for row, part, value in strips_of(grad_w, 8, 2)
        ]
    )


def attention_backward(held, coords, mask, normed, qkv, grad_att, *rest):
    grad_mixed, *targets = rest[held:]
    rows = normed.shape[0]
    emit = Emitter(targets, (LOWER,), coords)

    @pl.loop(0, rows // GROUP)
    def _(i):
        span = span_of(i)
        caption = caption_of()
        scale = HD ** (-0.5)
        pairs = list(pairs_of())
        scores = [
            compact(
                mm(qkv[3 * half + 1, span, lanes], split_pair(qkv[3 * half, span, lanes]), 1, 1),
                caption,
            )
            for half, lanes, _ in pairs
        ]
        grad_probs = [
            compact(
                mm(qkv[3 * half + 2, span, lanes], split_pair(grad_att[span, wide]), 1, 1), caption
            )
            for half, lanes, wide in pairs
        ]
        probs = softmax_of(jnp.concatenate(scores, axis=1), key_bias(mask[i]))
        grad_probs = jnp.concatenate(grad_probs, axis=1)
        inner = jnp.sum(probs * grad_probs, axis=0, keepdims=True)
        grad_scores = probs * (grad_probs - inner)
        for pair, (half, lanes, wide) in enumerate(pairs):
            spread = expand(columns(grad_scores, pair), caption)
            back = mm(spread, qkv[3 * half + 1, span, lanes], 0, 0)
            grad_mixed[3 * half, span, lanes] = (join_pair(back) * scale).astype(BF16)
            back = mm(spread, split_pair(qkv[3 * half, span, lanes]))
            grad_mixed[3 * half + 1, span, lanes] = (back * scale).astype(BF16)
            spread = expand(columns(probs, pair), caption)
            grad_mixed[3 * half + 2, span, lanes] = mm(
                spread, split_pair(grad_att[span, wide])
            ).astype(BF16)

    for half in range(HALVES):
        grads = jnp.concatenate([grad_mixed[3 * half + part] for part in range(3)], axis=1)
        grad_w = mm(normed[...], grads, 0, 0).astype(BF16)
        emit.store([(value, half, 3 * row + part) for row, part, value in strips_of(grad_w, 8, 3)])


def input_backward(tok, gains, grad_mixed, grad_after, gain_two, strips, input_grad, gain_part):
    rows = tok.shape[0]
    grads = jnp.concatenate([grad_mixed[part] for part in range(6)], axis=1)
    halves = [weight_of(strips, half, 0, 8, 3, range(3)) for half in range(HALVES)]
    input_grad[...] = mm(grads, jnp.concatenate(halves, axis=1), 1, 1)
    gain_part[0] = jnp.zeros_like(gain_two)
    gain_part[1] = gain_two[...]

    @pl.loop(0, rows // GROUP)
    def _(i):
        span = span_of(i)
        xhat, inverse = norm_parts(tok[span, :].astype(F32))
        grad = input_grad[span, :]
        gain_part[0] += jnp.sum(grad * xhat, axis=0, keepdims=True)
        input_grad[span, :] = grad_after[span, :] + norm_back(xhat, inverse, gains[0:1, :], grad)


def shape_of(*shape, dtype=BF16):
    return jax.ShapeDtypeStruct(shape, dtype)


VMEM = pl.BlockSpec(memory_space=pltpu.VMEM)
SMEM = pl.BlockSpec(memory_space=pltpu.SMEM)


def call(kernel, name, in_specs, outs, scratch, flops, args, grid=(1,), aliases=None, mib=10):
    moved = sum(math_size(a.shape) * a.dtype.itemsize for a in args)
    moved += sum(math_size(s.shape) * s.dtype.itemsize for _, s in outs)
    return pl.pallas_call(
        kernel,
        grid=grid,
        in_specs=in_specs,
        out_specs=[spec for spec, _ in outs],
        out_shape=[shape for _, shape in outs],
        scratch_shapes=scratch,
        input_output_aliases=aliases or {},
        compiler_params=pltpu.CompilerParams(
            dimension_semantics=("arbitrary",) * len(grid), vmem_limit_bytes=mib << 20
        ),
        cost_estimate=pl.CostEstimate(flops=1, bytes_accessed=1, transcendentals=0),
        name=name,
    )(*args)


def math_size(shape):
    size = 1
    for extent in shape:
        size *= extent
    return size


UNIT = 2 * 768 * 768 * 768


def run_prepare(coords, token_mask, cot, tok, gains):
    captions = cot.shape[0]
    rows = captions * SLOTS
    return call(
        prepare,
        "prepare",
        [SMEM] + [VMEM] * 4,
        [
            (VMEM, shape_of(rows // GROUP, SLOTS, GROUP, dtype=F32)),
            (VMEM, shape_of(rows, PAIR, dtype=F32)),
            (VMEM, shape_of(rows, D + PAIR)),
            (VMEM, shape_of(captions, PAIR, dtype=F32)),
            (VMEM, shape_of(rows, D)),
        ],
        [],
        1,
        (coords, token_mask, cot, tok, gains),
        mib=6,
    )


def run_forward(tok, gains, normed, mask, share, strips):
    rows = tok.shape[0]
    return call(
        attention_forward,
        "attention_forward",
        [VMEM] * 6,
        [
            (VMEM, shape_of(6, rows, STRIP)),
            (VMEM, shape_of(rows, D)),
            (VMEM, shape_of(rows, D, dtype=F32)),
            (VMEM, shape_of(rows, D)),
            (VMEM, shape_of(rows // SLOTS, D, dtype=F32)),
        ],
        [],
        5 * UNIT,
        (tok, gains, normed, mask, share, strips),
        mib=3,
    )


def targets_of(runs, split):
    if split:
        shapes = [shape_of(len(run), HALVES, 2, OWN, BLOCK, STRIP) for run in runs for _ in range(2)]
    else:
        shapes = [shape_of(HALVES, STRIPS, BLOCK, STRIP)]
    return [(VMEM, shape) for shape in shapes]


def run_mlp(coords, normed_two, out_wide, strips, split):
    rows = normed_two.shape[0]
    return call(
        mlp_both,
        "mlp_both",
        [SMEM] + [VMEM] * 3,
        [(VMEM, shape_of(4, D, PAIR, dtype=F32)), (VMEM, shape_of(rows, D, dtype=F32))]
        + targets_of((UPPER, LOWER), split),
        [pltpu.VMEM((rows, D), BF16), pltpu.VMEM((rows, D), BF16)],
        20 * UNIT,
        (coords, normed_two, out_wide, strips),
        grid=(4,),
        mib=6 if split else 44,
    )


def run_pool(after_pooled, hidden_pooled, inverse, strips):
    return call(
        pool_out,
        "pool_out",
        [VMEM] * 4,
        [(VMEM, jax.ShapeDtypeStruct(after_pooled.shape, F32))],
        [],
        UNIT // 2,
        (after_pooled, hidden_pooled, inverse, strips),
        mib=6,
    )[0]


def run_output(coords, gains, attended, after, cot, share, grad_two, strips, held, split):
    rows = after.shape[0]
    return call(
        functools.partial(output_backward, len(held)),
        "output_backward",
        [SMEM] + [VMEM] * (7 + len(held)),
        [
            (VMEM, shape_of(rows, D, dtype=F32)),
            (VMEM, shape_of(1, D, dtype=F32)),
            (VMEM, shape_of(rows, D)),
        ]
        + targets_of((LOWER,), split),
        [pltpu.VMEM((rows, D), BF16)],
        2 * UNIT,
        (coords, gains, attended, after, cot, share, grad_two, strips, *held),
        aliases={8 + i: 3 + i for i in range(len(held))},
        mib=6 if split else 56,
    )


def run_backward(coords, mask, normed, qkv, grad_att, held, split):
    rows = normed.shape[0]
    return call(
        functools.partial(attention_backward, len(held)),
        "attention_backward",
        [SMEM, VMEM, VMEM, VMEM, VMEM] + [VMEM] * len(held),
        [(VMEM, shape_of(6, rows, STRIP))] + targets_of((LOWER,), split),
        [],
        7 * UNIT,
        (coords, mask, normed, qkv, grad_att, *held),
        aliases={5 + i: 1 + i for i in range(len(held))},
        mib=6 if split else 56,
    )


def run_input(tok, gains, grad_mixed, grad_after, gain_two, strips):
    rows = tok.shape[0]
    return call(
        input_backward,
        "input_backward",
        [VMEM] * 6,
        [(VMEM, shape_of(rows, D, dtype=F32)), (VMEM, shape_of(2, 1, D, dtype=F32))],
        [],
        3 * UNIT,
        (tok, gains, grad_mixed, grad_after, gain_two, strips),
        mib=5,
    )


def to_strips(blocks):
    count = blocks.shape[0] // 4
    return blocks.reshape(count, 4, BLOCK, BLOCK).transpose(0, 2, 1, 3).reshape(count, BLOCK, STRIP)


def to_blocks(strips):
    count = strips.shape[0]
    return strips.reshape(count, BLOCK, 4, BLOCK).transpose(0, 2, 1, 3).reshape(-1, BLOCK, BLOCK)


EVERY = ("tensor", "dp")


def gather_weights(master):
    low = master.astype(BF16)
    own = low.shape[0]
    if own % 4 == 0:
        strips = to_strips(low).reshape(-1, STRIP)
        strips = lax.all_gather(strips, EVERY, axis=0, tiled=True)
        return strips.reshape(HALVES, STRIPS, BLOCK, STRIP)
    blocks = lax.all_gather(low, EVERY, axis=0, tiled=True)
    return to_strips(blocks).reshape(HALVES, STRIPS, BLOCK, STRIP)


def pack(master, out):
    for strip in range(master.shape[0] // 4):
        parts = [master[4 * strip + i].astype(BF16) for i in range(4)]
        out[0, strip] = jnp.concatenate(parts, axis=1)


def take_halves(by_x, by_y, from_x, from_y):
    for plane in range(by_x.shape[0]):
        from_x[plane] = by_x[plane, 0:3]
        from_y[plane] = by_y[plane, 3:6]


def take_both(one, two, out):
    out[0] = one[0]
    out[1] = two[0]


def place_own(held, planes, coords, own, by_x, by_y, across_one, across_two, *rest):
    whole, sent = rest[held:]
    core, place, plane, half = coords[0], coords[1], coords[2], coords[3]
    for i, apart in enumerate(planes):
        z = plane ^ apart

        def put(y, x, strips, value):
            sent[i, y, x, strips] = value
            whole[y, z, x, core, strips] = value

        put(half, place, slice(0, 6), own[i])
        put(half, 1 - place, slice(0, 6), by_x[i])
        put(1 - half, place, slice(0, 6), by_y[i])
        put(1 - half, 1 - place, slice(0, 3), across_one[i])
        put(1 - half, 1 - place, slice(3, 6), across_two[i])


def place_most(apart, coords, own, by_x, by_y, _, whole, sent):
    core, place, plane, half = coords[0], coords[1], coords[2], coords[3]
    for i, (y, x, value) in enumerate(
        ((half, place, own), (half, 1 - place, by_x), (1 - half, place, by_y))
    ):
        sent[i] = value[0]
        whole[y, plane ^ apart, x, core] = value[0]


def place_last(apart, coords, most_in, one_in, two_in, one, two, _, whole):
    core, place, plane, half = coords[0], coords[1], coords[2], coords[3]
    z = plane ^ apart
    for i, (y, x) in enumerate(((half, place), (half, 1 - place), (1 - half, place))):
        whole[y, z, x, 1 - core] = most_in[i]
    for strips, mine, other in ((pl.ds(0, 3), one, one_in), (pl.ds(3, 3), two, two_in)):
        whole[1 - half, z, 1 - place, core, strips] = mine[0]
        whole[1 - half, z, 1 - place, 1 - core, strips] = other[0]


def place_other(planes, coords, arrived, _, whole):
    core, plane = coords[0], coords[2]
    for i, apart in enumerate(planes):
        for y in range(2):
            for x in range(2):
                whole[y, plane ^ apart, x, 1 - core] = arrived[i, y, x]


WHOLE = (HALVES, 4, 2, 2, OWN, BLOCK, STRIP)


def run_pack(master):
    return call(
        pack,
        "pack",
        [VMEM],
        [(VMEM, shape_of(1, OWN, BLOCK, STRIP))],
        [],
        math_size(master.shape),
        (master,),
        mib=4,
    )[0]


def run_halves(by_x, by_y):
    shape = shape_of(by_x.shape[0], 3, BLOCK, STRIP)
    return call(
        take_halves, "take_halves", [VMEM] * 2, [(VMEM, shape)] * 2, [], 1, (by_x, by_y), mib=4
    )


def run_both(one, two):
    shape = shape_of(2, OWN, BLOCK, STRIP)
    return call(take_both, "take_both", [VMEM] * 2, [(VMEM, shape)], [], 1, (one, two), mib=4)[0]


def run_place_own(planes, coords, pieces, held):
    count = len(planes)
    return call(
        functools.partial(place_own, len(held), planes),
        "place_own",
        [SMEM] + [VMEM] * (5 + len(held)),
        [(VMEM, shape_of(*WHOLE)), (VMEM, shape_of(count, HALVES, 2, OWN, BLOCK, STRIP))],
        [],
        1,
        (coords, *pieces, *held),
        aliases={6: 0} if held else None,
        mib=4,
    )


def run_place_most(apart, coords, pieces, whole):
    return call(
        functools.partial(place_most, apart),
        "place_most",
        [SMEM] + [VMEM] * 4,
        [(VMEM, shape_of(*WHOLE)), (VMEM, shape_of(3, OWN, BLOCK, STRIP))],
        [],
        1,
        (coords, *pieces, whole),
        aliases={4: 0},
        mib=4,
    )


def run_place_last(apart, coords, pieces, whole):
    return call(
        functools.partial(place_last, apart),
        "place_last",
        [SMEM] + [VMEM] * 6,
        [(VMEM, shape_of(*WHOLE))],
        [],
        1,
        (coords, *pieces, whole),
        aliases={6: 0},
        mib=4,
    )[0]


def run_place_other(planes, coords, arrived, whole):
    return call(
        functools.partial(place_other, planes),
        "place_other",
        [SMEM] + [VMEM] * 2,
        [(VMEM, shape_of(*WHOLE))],
        [],
        1,
        (coords, arrived, whole),
        aliases={2: 0},
        mib=4,
    )[0]


def neighbour_hop(value):
    return lax.ppermute(value, "dp", OTHER_X), lax.ppermute(value, "tensor", OTHER_Y)


def across_hop(pieces):
    return lax.ppermute(pieces[0], "tensor", OTHER_Y), lax.ppermute(pieces[1], "dp", OTHER_X)


def gather_split(master, coords, prepare):
    own = run_pack(master)
    near = lax.ppermute(own, "dp", NEAR_Z)
    far = lax.ppermute(own, "dp", FAR_Z)
    own_by = neighbour_hop(own)
    own_by, prepared = fence(own_by, prepare())
    own_across = across_hop(run_halves(*own_by))
    near, far, own_across, own_by, own, prepared = fence(near, far, own_across, own_by, own, prepared)

    both = run_both(near, far)
    both_by = neighbour_hop(both)
    other = lax.ppermute(far, "dp", NEAR_Z)
    other_by = neighbour_hop(other)
    both_across = across_hop(run_halves(*both_by))
    whole, sent = run_place_own((0,), coords, (own, *own_by, *own_across), ())
    own_in = core_hop(sent)
    both_across, other_by, own_in, whole = fence(both_across, other_by, own_in, whole)

    other_across = across_hop(run_halves(*other_by))
    whole, sent = run_place_own((1, 2), coords, (both, *both_by, *both_across), (whole,))
    both_in = core_hop(sent)
    whole, sent = run_place_most(3, coords, (other, *other_by), whole)
    other_in = core_hop(sent)
    whole = run_place_other((0,), coords, own_in, whole)
    other_across, both_in, other_in, whole = fence(other_across, both_in, other_in, whole)

    across_in = core_hop(other_across[0]), core_hop(other_across[1])
    whole = run_place_other((1, 2), coords, both_in, whole)
    across_in, whole = fence(across_in, whole)
    whole = run_place_last(3, coords, (other_in, *across_in, *other_across), whole)
    return whole.reshape(HALVES, STRIPS, BLOCK, STRIP), prepared


def scatter_flat(strips, own):
    if own % 4 == 0:
        mine = lax.psum_scatter(
            strips.reshape(-1, STRIP), EVERY, scatter_dimension=0, tiled=True
        )
        return to_blocks(mine.reshape(-1, BLOCK, STRIP)).astype(F32)
    blocks = to_blocks(strips.reshape(-1, BLOCK, STRIP))
    return lax.psum_scatter(blocks, EVERY, scatter_dimension=0, tiled=True).astype(F32)


def fence(*values):
    return lax.optimization_barrier(values)


OTHER_CORE = [(i, i ^ 1) for i in range(16)]
OTHER_X = [(i, i ^ 2) for i in range(16)]
OTHER_Y = [(0, 1), (1, 0)]


def by_plane(*moves):
    return [(4 * a + i, 4 * b + i) for a, b in moves for i in range(4)]


NEAR_Z = by_plane((0, 1), (1, 0), (2, 3), (3, 2))
FAR_Z = by_plane((0, 2), (1, 3), (2, 0), (3, 1))


def split_sum(coords, kept, arrived, sent_one, sent_two, kept_one, kept_two):
    place, half = coords[1], coords[3]

    @pl.loop(0, 2 * kept.shape[0])
    def _(step):
        plane, i = step // 2, lax.rem(step, 2)
        one, two = pl.ds(0, 3), pl.ds(3, 3)
        sent_one[plane, i] = kept[plane, 1 - half, i, one] + arrived[plane, 1 - half, i, one]
        kept_one[plane, i] = kept[plane, half, i, one] + arrived[plane, half, i, one]
        sent_two[plane, i] = kept[plane, i, 1 - place, two] + arrived[plane, i, 1 - place, two]
        kept_two[plane, i] = kept[plane, i, place, two] + arrived[plane, i, place, two]


def split_again(coords, one, two, one_in, two_in, sent_one, sent_two, kept_one, kept_two):
    place, half = coords[1], coords[3]

    @pl.loop(0, one.shape[0])
    def _(plane):
        sent_one[plane] = one[plane, 1 - place] + one_in[plane, 1 - place]
        kept_one[plane] = one[plane, place] + one_in[plane, place]
        sent_two[plane] = two[plane, 1 - half] + two_in[plane, 1 - half]
        kept_two[plane] = two[plane, half] + two_in[plane, half]


def join_sum(coords, one, two, one_in, two_in, *outs):
    for i, out in enumerate(outs):
        plane = lax.rem(coords[2] + i, 2)
        out[0:3] = one[plane] + one_in[plane]
        out[3:6] = two[plane] + two_in[plane]


def pick_sum(coords, high, high_in, low, low_in, mine, sent):
    @pl.when(coords[2] >= 2)
    def _():
        mine[...] = high[...] + high_in[...]
        sent[...] = low[...] + low_in[...]

    @pl.when(coords[2] < 2)
    def _():
        mine[...] = low[...] + low_in[...]
        sent[...] = high[...] + high_in[...]


def renew_gains(grads, arrived, moments, gains, grads_out, moments_out, gains_out):
    for i in range(2):
        grad = grads[i] + arrived[i]
        moment = DECAY_RATE * moments[i : i + 1] + (1.0 - DECAY_RATE) * grad * grad
        grads_out[i : i + 1] = grad
        moments_out[i : i + 1] = moment
        gains_out[i : i + 1] = gains[i : i + 1] - GAIN_RATE * grad / (jnp.sqrt(moment) + 1e-08)


def sum_of(left, right, out):
    @pl.loop(0, left.shape[0])
    def _(i):
        out[i] = left[i] + right[i]


def run_split(coords, kept, arrived):
    shape = shape_of(kept.shape[0], 2, 3, BLOCK, STRIP)
    outs = call(
        split_sum,
        "split_sum",
        [SMEM, VMEM, VMEM],
        [(VMEM, shape)] * 4,
        [],
        math_size(kept.shape),
        (coords, kept, arrived),
        mib=4,
    )
    return outs[:2], outs[2:]


def run_again(coords, kept, arrived):
    shape = shape_of(kept[0].shape[0], 3, BLOCK, STRIP)
    outs = call(
        split_again,
        "split_again",
        [SMEM] + [VMEM] * 4,
        [(VMEM, shape)] * 4,
        [],
        2 * math_size(kept[0].shape),
        (coords, *kept, *arrived),
        mib=4,
    )
    return outs[:2], outs[2:]


def run_join(coords, kept, arrived):
    return call(
        join_sum,
        "join_sum",
        [SMEM] + [VMEM] * 4,
        [(VMEM, shape_of(OWN, BLOCK, STRIP))] * 2,
        [],
        2 * math_size(kept[0].shape),
        (coords, *kept, *arrived),
        mib=4,
    )


def run_pick(coords, high, high_in, low, low_in):
    return call(
        pick_sum,
        "pick_sum",
        [SMEM] + [VMEM] * 4,
        [(VMEM, shape_of(OWN, BLOCK, STRIP))] * 2,
        [],
        1,
        (coords, high, high_in, low, low_in),
        mib=4,
    )


def run_sum(left, right):
    return call(
        sum_of,
        "sum_of",
        [VMEM] * 2,
        [(VMEM, jax.ShapeDtypeStruct(left.shape, left.dtype))],
        [],
        math_size(left.shape),
        (left, right),
        mib=4,
    )[0]


def run_gains(grads, arrived, moments, gains):
    return call(
        renew_gains,
        "renew_gains",
        [VMEM] * 4,
        [(VMEM, shape_of(2, D, dtype=F32))] * 3,
        [],
        1,
        (grads, arrived, moments, gains),
        mib=4,
    )


def core_hop(sent):
    return lax.ppermute(sent, "dp", OTHER_CORE)


def first_hop(sent):
    return lax.ppermute(sent[0], "tensor", OTHER_Y), lax.ppermute(sent[1], "dp", OTHER_X)


def second_hop(sent):
    return lax.ppermute(sent[0], "dp", OTHER_X), lax.ppermute(sent[1], "tensor", OTHER_Y)


def precise(left, right, left_dim=1, right_dim=0):
    left_high, right_high = left.astype(BF16), right.astype(BF16)
    left_low = (left - left_high.astype(F32)).astype(BF16)
    right_low = (right - right_high.astype(F32)).astype(BF16)
    small = mm(left_high, right_low, left_dim, right_dim) + mm(
        left_low, right_high, left_dim, right_dim
    )
    return mm(left_high, right_high, left_dim, right_dim) + small


def update(mine, arrived, master, stat_left, stat_right, root_left, root_right, *outs):
    grad_out, left_out, right_out, master_out, copy_out = outs
    count = grad_out.shape[0]
    first = pl.program_id(0) * count
    grads = []
    for i in range(count // 4):
        strip = first // 4 + i
        grad = mine[strip].astype(F32) + arrived[strip].astype(F32)
        grads += [grad[:, j * BLOCK : (j + 1) * BLOCK] for j in range(4)]
    blocks = [first + i for i in range(count)]
    sides = [precise(g, root_right[block]) for g, block in zip(grads, blocks)]
    lefts = [precise(g, g, 1, 1) for g in grads]
    rights = [precise(g, g, 0, 0) for g in grads]
    directions = [precise(root_left[block], side) for side, block in zip(sides, blocks)]
    for i, block in enumerate(blocks):
        grad_out[i] = grads[i]
        left_out[i] = DECAY_RATE * stat_left[block] + (1.0 - DECAY_RATE) * lefts[i]
        right_out[i] = DECAY_RATE * stat_right[block] + (1.0 - DECAY_RATE) * rights[i]
        new = master[block] - STEP_RATE * directions[i]
        master_out[i] = new
        copy_out[i] = new.astype(BF16)


def run_update(sums, blocks):
    count = blocks[0].shape[0]
    step = 8 if count % 8 == 0 else 4
    tile = pl.BlockSpec((step, BLOCK, BLOCK), lambda i: (i, 0, 0))
    shape = shape_of(count, BLOCK, BLOCK, dtype=F32)
    return call(
        update,
        "update",
        [VMEM] * (len(sums) + len(blocks)),
        [(tile, shape)] * 4 + [(tile, shape_of(count, BLOCK, BLOCK))],
        [],
        12 * 2 * count * BLOCK**3,
        (*sums, *blocks),
        grid=(count // step,),
        mib=8,
    )


def sum_hops():
    hops = []
    for axis in ("tensor", "dp"):
        size, step = lax.axis_size(axis), 1
        while step < size:
            hops.append((axis, [(i, i ^ step) for i in range(size)]))
            step *= 2
    return hops


def plain_update(grad, master, stat_left, stat_right, root_left, root_right):
    left_new = DECAY_RATE * stat_left + (1.0 - DECAY_RATE) * jnp.einsum(
        "nij,nkj->nik", grad, grad, precision=PRECISE
    )
    right_new = DECAY_RATE * stat_right + (1.0 - DECAY_RATE) * jnp.einsum(
        "nji,njk->nik", grad, grad, precision=PRECISE
    )
    right_side = jnp.einsum("nij,njk->nik", grad, root_right, precision=PRECISE)
    direction = jnp.einsum("nij,njk->nik", root_left, right_side, precision=PRECISE)
    master_new = master - STEP_RATE * direction
    return grad, left_new, right_new, master_new, master_new.astype(BF16)


def body(
    tokens,
    token_mask,
    norm_gains,
    gain_moments,
    cotangent,
    master,
    stat_left,
    stat_right,
    root_left,
    root_right,
):
    rows = tokens.shape[0]
    own_caps = cotangent.shape[0]
    own = master.shape[0]
    split = lax.axis_size("dp") == 16 and lax.axis_size("tensor") == 2
    dp_pos, half = lax.axis_index("dp"), lax.axis_index("tensor")
    coords = jnp.stack([dp_pos % 2, dp_pos // 2 % 2, dp_pos // 4, half]).astype(jnp.int32)

    coords, master = fence(coords, master)
    first = functools.partial(run_prepare, coords, token_mask, cotangent, tokens, norm_gains)
    if split:
        strips, prepared = gather_split(master, coords, first)
    else:
        strips, prepared = gather_weights(master), first()
    mask, share, out_wide, inverse, normed = prepared
    qkv, attended, after, normed_two, after_pooled = run_forward(
        tokens, norm_gains, normed, mask, share, strips
    )
    hidden_pooled, grad_two, *held = run_mlp(coords, normed_two, out_wide, strips, split)
    hops = sum_hops()
    blocks = (master, stat_left, stat_right, root_left, root_right)
    if not split:
        grad_after, gain_two, grad_att, *held = run_output(
            coords, norm_gains, attended, after, cotangent, share, grad_two, strips, held, split
        )
        grad_mixed, *held = run_backward(coords, mask, normed, qkv, grad_att, held, split)
        input_grad, gain_grads = run_input(
            tokens, norm_gains, grad_mixed, grad_after, gain_two, strips
        )
        pooled = run_pool(after_pooled, hidden_pooled, inverse, strips)
        for hop in hops[:-1]:
            gain_grads = run_sum(gain_grads, lax.ppermute(gain_grads, *hop))
        gain_in = lax.ppermute(gain_grads, *hops[-1])
        gain_results = run_gains(gain_grads, gain_in, gain_moments, norm_gains)
        updated = plain_update(scatter_flat(held[0], own), *blocks)
    else:
        upper_kept, upper_sent, *lower = held
        upper_in = core_hop(upper_sent)
        grad_after, gain_two, grad_att, *lower = run_output(
            coords, norm_gains, attended, after, cotangent, share, grad_two, strips, lower, split
        )
        upper_in, grad_att, lower = fence(upper_in, grad_att, lower)

        upper_sent, upper_kept = run_split(coords, upper_kept, upper_in)
        upper_sent, grad_att, lower = fence(upper_sent, grad_att, lower)
        upper_in = first_hop(upper_sent)
        grad_mixed, *lower = run_backward(coords, mask, normed, qkv, grad_att, lower, split)
        upper_in, grad_mixed, lower = fence(upper_in, grad_mixed, lower)

        lower_in = core_hop(lower[1])
        upper_sent, upper_kept = run_again(coords, upper_kept, upper_in)
        upper_in = second_hop(upper_sent)

        lower_sent, lower_kept = run_split(coords, lower[0], lower_in)
        lower_in = first_hop(lower_sent)
        input_grad, gain_grads = run_input(
            tokens, norm_gains, grad_mixed, grad_after, gain_two, strips
        )

        gain_in = lax.ppermute(gain_grads, *hops[0])
        pooled = run_pool(after_pooled, hidden_pooled, inverse, strips)
        high, high_sent = run_join(coords, upper_kept, upper_in)
        high_in = lax.ppermute(high_sent, "dp", NEAR_Z)
        high_in, lower_in, gain_in, pooled = fence(high_in, lower_in, gain_in, pooled)

        lower_sent, lower_kept = run_again(coords, lower_kept, lower_in)
        lower_in = second_hop(lower_sent)
        gain_grads = run_sum(gain_grads, gain_in)
        gain_in = lax.ppermute(gain_grads, *hops[1])
        lower_in, gain_in = fence(lower_in, gain_in)

        low, low_sent = run_join(coords, lower_kept, lower_in)
        low_in = lax.ppermute(low_sent, "dp", NEAR_Z)
        gain_grads = run_sum(gain_grads, gain_in)
        gain_in = lax.ppermute(gain_grads, *hops[2])
        low_in, gain_in = fence(low_in, gain_in)

        mine, sent = run_pick(coords, high, high_in, low, low_in)
        arrived = lax.ppermute(sent, "dp", FAR_Z)
        gain_grads = run_sum(gain_grads, gain_in)
        gain_in = lax.ppermute(gain_grads, *hops[3])
        gain_grads = run_sum(gain_grads, gain_in)
        gain_in = lax.ppermute(gain_grads, *hops[4])
        gain_results = run_gains(gain_grads, gain_in, gain_moments, norm_gains)
        arrived, gain_results = fence(arrived, gain_results)

        updated = run_update((mine, arrived), blocks)
    return (pooled, input_grad, *gain_results, *updated)


def solution(mesh):
    rows = P(("dp", "tensor"), None)
    blocks = P(("dp", "tensor"), None, None)
    return jax.shard_map(
        body,
        mesh=mesh,
        in_specs=(rows, P("dp", None), P(), P(), rows) + (blocks,) * 5,
        out_specs=(rows, rows, P(), P(), P()) + (blocks,) * 5,
        check_vma=False,
    )
```

```python
import functools

import jax
import jax.numpy as jnp
from jax import lax
from jax.experimental import pallas as pl
from jax.experimental.pallas import tpu as pltpu
from jax.sharding import PartitionSpec as P

D = 768
HEADS = 12
HD = 64
FF = 3072
BLOCK = 96
SLOTS = 16
HALVES = 2
STRIP = 4 * BLOCK
STRIPS = 96
OWN = 6
GROUP = 128
CAPS = GROUP // SLOTS
UPPER = (2, 3)
LOWER = (0, 1)
PAIR = 2 * HD

EPSILON = 1e-06
DECAY_RATE = 0.5
STEP_RATE = 0.25
GAIN_RATE = 0.3
MASKED_SCORE = -1e30
PRECISE = lax.Precision.HIGHEST
F32 = jnp.float32
BF16 = jnp.bfloat16


def mm(left, right, left_dim=1, right_dim=0):
    return lax.dot_general(
        left, right, (((left_dim,), (right_dim,)), ((), ())), preferred_element_type=F32
    )


def weight_of(strips, half, first, rows, width, columns):
    parts = [
        jnp.concatenate([strips[half, first + width * row + column] for row in range(rows)], axis=0)
        for column in columns
    ]
    return jnp.concatenate(parts, axis=1)


def out_weight(strips):
    halves = [weight_of(strips, half, 24, 4, 2, (0, 1)) for half in range(HALVES)]
    return jnp.concatenate(halves, axis=0)


def norm_parts(values):
    center = values - jnp.mean(values, axis=-1, keepdims=True)
    inverse = lax.rsqrt(jnp.mean(center * center, axis=-1, keepdims=True) + EPSILON)
    return center * inverse, inverse


def norm_back(xhat, inverse, gain, grad):
    scaled = grad * gain
    return inverse * (
        scaled
        - jnp.mean(scaled, axis=-1, keepdims=True)
        - xhat * jnp.mean(scaled * xhat, axis=-1, keepdims=True)
    )


def split_pair(values):
    first = lax.broadcasted_iota(jnp.int32, (GROUP, PAIR), 1) < HD
    zero = jnp.zeros_like(values)
    return jnp.concatenate(
        [jnp.where(first, values, zero), jnp.where(first, zero, values)], axis=0
    )


def join_pair(stacked):
    first = lax.broadcasted_iota(jnp.int32, (GROUP, PAIR), 1) < HD
    return jnp.where(first, stacked[:GROUP], stacked[GROUP:])


def caption_of():
    return lax.broadcasted_iota(jnp.int32, (SLOTS, 2 * GROUP), 1) % GROUP // SLOTS


def compact(full, caption):
    kept = full[0:SLOTS]
    for i in range(1, CAPS):
        kept = jnp.where(caption == i, full[i * SLOTS : (i + 1) * SLOTS], kept)
    return kept


def expand(kept, caption):
    zero = jnp.zeros_like(kept)
    return jnp.concatenate(
        [jnp.where(caption == i, kept, zero).astype(BF16) for i in range(CAPS)], axis=0
    )


def softmax_of(scores, bias):
    scores = scores * HD ** (-0.5) + bias
    shifted = jnp.exp(scores - jnp.max(scores, axis=0, keepdims=True))
    return shifted / jnp.sum(shifted, axis=0, keepdims=True)


def pairs_of():
    for half in range(HALVES):
        for start in range(0, STRIP, PAIR):
            yield half, slice(start, start + PAIR), slice(half * STRIP + start, half * STRIP + start + PAIR)


def columns(values, i):
    return values[:, 2 * GROUP * i : 2 * GROUP * (i + 1)]


def key_bias(mask):
    bias = jnp.where(mask > 0, 0.0, MASKED_SCORE)
    return jnp.concatenate([bias] * HEADS, axis=1)


def span_of(i, size=GROUP):
    return pl.ds(pl.multiple_of(i * size, size), size)


def prepare(coords, token_mask, cot, tok, gains, mask, share, out_wide, inverse, normed):
    captions = cot.shape[0]
    first = pl.multiple_of(coords[3] * captions, captions)
    own = token_mask[pl.ds(first, captions), :].astype(F32)
    count = jnp.broadcast_to(jnp.sum(own, axis=1, keepdims=True), (captions, PAIR))
    inverse[...] = 1.0 / count
    key = lax.broadcasted_iota(jnp.int32, (SLOTS, GROUP), 0).astype(F32)
    here = (
        lax.broadcasted_iota(jnp.int32, (CAPS, GROUP), 0)
        == lax.broadcasted_iota(jnp.int32, (CAPS, GROUP), 1) // SLOTS
    )
    slot = lax.broadcasted_iota(jnp.int32, (CAPS, SLOTS, PAIR), 1).astype(F32)
    caption = lax.broadcasted_iota(jnp.int32, (CAPS, SLOTS, PAIR), 0)
    lane = lax.broadcasted_iota(jnp.int32, (CAPS, SLOTS, PAIR), 2)
    for i in range(captions // CAPS):
        span, caps = slice(i * GROUP, (i + 1) * GROUP), slice(i * CAPS, (i + 1) * CAPS)
        number = count[caps]
        by_query = jnp.sum(jnp.where(here, number, 0.0), axis=0, keepdims=True)
        mask[i] = jnp.where(key < by_query, 1.0, 0.0)
        true = slot < number[:, None, :]
        weight = jnp.where(true, 1.0 / number[:, None, :], 0.0)
        share[span, :] = weight.reshape(GROUP, PAIR)
        seen = jnp.where(true & (caption + i * CAPS == lane), 1.0, 0.0)
        out_wide[span, D:] = seen.reshape(GROUP, PAIR).astype(BF16)
        for j in range(0, D, PAIR):
            lanes = slice(j, j + PAIR)
            value = (cot[caps, lanes].astype(F32)[:, None, :] * weight).reshape(GROUP, PAIR)
            out_wide[span, lanes] = value.astype(BF16)
        xhat, _ = norm_parts(tok[span, :].astype(F32))
        normed[span, :] = (xhat * gains[0:1, :]).astype(BF16)


def pool(values, share):
    parts = [
        values[:, i : i + PAIR] * share for i in range(0, values.shape[1], PAIR)
    ]
    weighted = jnp.concatenate(parts, axis=1)
    return jnp.sum(weighted.reshape(-1, SLOTS, values.shape[1]), axis=1)


def attention_forward(
    tok, gains, normed, mask, share, strips, qkv, attended, after, normed_two, after_pooled
):
    rows = tok.shape[0]

    for half in range(HALVES):
        mixed = mm(normed[...], weight_of(strips, half, 0, 8, 3, range(3))).astype(BF16)
        for part in range(3):
            qkv[3 * half + part] = mixed[:, part * STRIP : (part + 1) * STRIP]

    @pl.loop(0, rows // GROUP)
    def _(i):
        span = span_of(i)
        caption = caption_of()
        pairs = list(pairs_of())
        scores = [
            compact(
                mm(qkv[3 * half + 1, span, lanes], split_pair(qkv[3 * half, span, lanes]), 1, 1),
                caption,
            )
            for half, lanes, _ in pairs
        ]
        probs = softmax_of(jnp.concatenate(scores, axis=1), key_bias(mask[i]))
        for pair, (half, lanes, wide) in enumerate(pairs):
            spread = expand(columns(probs, pair), caption)
            mixed = mm(spread, qkv[3 * half + 2, span, lanes], 0, 0)
            attended[span, wide] = join_pair(mixed).astype(BF16)

    after[...] = mm(attended[...], out_weight(strips))

    @pl.loop(0, rows // GROUP)
    def _(i):
        span = span_of(i)
        summed = tok[span, :].astype(F32) + after[span, :]
        after[span, :] = summed
        after_pooled[span_of(i, CAPS), :] = pool(summed, share[span, :])
        xhat, _ = norm_parts(summed)
        normed_two[span, :] = (xhat * gains[1:2, :]).astype(BF16)


GELU_A = 0.7978845608028654
GELU_B = 0.044715


def gelu_both(v):
    square = v * v
    inner = jnp.tanh(GELU_A * v * (1.0 + GELU_B * square))
    half_up = 0.5 * (1.0 + inner)
    slope = half_up + (0.5 * GELU_A) * v * (1.0 - inner * inner) * (1.0 + (3.0 * GELU_B) * square)
    return v * half_up, slope


class Emitter:
    def __init__(self, targets, runs, coords):
        self.core = coords[0]
        self.whole = targets[0] if len(targets) == 1 else None
        self.batches = [] if self.whole is not None else list(zip(runs, targets[0::2], targets[1::2]))

    def store(self, pieces, here=True):
        if self.whole is not None:

            @pl.when(here)
            def _():
                for value, half, strip in pieces:
                    self.whole[half, strip] = value

            return
        for core in range(2):

            @pl.when((self.core == core) & here)
            def _():
                for value, half, strip in pieces:
                    plane, place = strip // (4 * OWN), strip // (2 * OWN) % 2
                    for run, kept, sent in self.batches:
                        if plane in run:
                            target = kept if strip // OWN % 2 == core else sent
                            target[plane - run[0], half, place, strip % OWN] = value


def strips_of(grad, rows, columns):
    return [
        (i, j, grad[i * BLOCK : (i + 1) * BLOCK, j * STRIP : (j + 1) * STRIP])
        for i in range(rows)
        for j in range(columns)
    ]


def mlp_both(coords, normed_two, out_wide, strips, *rest):
    hidden_pooled, grad_normed_two, *targets, hidden, grad_up = rest
    step = pl.program_id(0)
    rows = normed_two.shape[0]
    emit = Emitter(targets, (UPPER, LOWER), coords)
    half = step // 2
    column = lax.rem(step, 2)

    @pl.when(step == 0)
    def _():
        grad_normed_two[...] = jnp.zeros_like(grad_normed_two)

    up_weight = weight_of(strips, half, 32 + 2 * column, 8, 4, (0, 1))
    down_weight = weight_of(strips, half, 64 + 16 * column, 8, 2, (0, 1))
    chunk = 256
    for i in range(rows // chunk):
        span = slice(i * chunk, (i + 1) * chunk)
        act, slope = gelu_both(mm(normed_two[span, :], up_weight))
        hidden[span, :] = act.astype(BF16)
        grad = (mm(out_wide[span, :D], down_weight, 1, 1) * slope).astype(BF16)
        grad_up[span, :] = grad
        grad_normed_two[span, :] += mm(grad, up_weight, 1, 1)

    both = mm(hidden[...], out_wide[...], 0, 0)
    hidden_pooled[step] = both[:, D:]
    down_strips = strips_of(both[:, :D].astype(BF16), 8, 2)
    up_strips = strips_of(mm(normed_two[...], grad_up[...], 0, 0).astype(BF16), 8, 2)
    for i in range(2):
        pieces = [(value, half, 64 + 16 * i + 2 * row + part) for row, part, value in down_strips]
        pieces += [(value, half, 32 + 4 * row + 2 * i + part) for row, part, value in up_strips]
        emit.store(pieces, column == i)


def pool_out(after_pooled, hidden_pooled, inverse, strips, pooled):
    captions = pooled.shape[0]
    pooled[...] = after_pooled[...]
    for step in range(4):
        value = hidden_pooled[step]
        high = value.astype(BF16)
        low = (value - high.astype(F32)).astype(BF16)
        weight = weight_of(strips, step // 2, 64 + 16 * (step % 2), 8, 2, (0, 1))
        both = mm(jnp.concatenate([high, low], axis=1), weight, 0, 0)
        total = both[:captions] + both[PAIR : PAIR + captions]
        pooled[...] += total * jnp.concatenate([inverse[...]] * (D // PAIR), axis=1)


def output_backward(
    held, coords, gains, attended, after, cot, share, grad_normed_two, strips, *rest
):
    grad_after, gain_part, grad_att, *targets, after_low = rest[held:]
    rows = after.shape[0]
    emit = Emitter(targets, (LOWER,), coords)
    gain_part[...] = jnp.zeros_like(gain_part)

    @pl.loop(0, rows // GROUP)
    def _(i):
        span = span_of(i)
        xhat, inverse = norm_parts(after[span, :])
        grad = grad_normed_two[span, :]
        gain_part[...] += jnp.sum(grad * xhat, axis=0, keepdims=True)
        weight = share[span, :].reshape(CAPS, SLOTS, PAIR)
        parts = [
            (cot[span_of(i, CAPS), j : j + PAIR].astype(F32)[:, None, :] * weight)
            for j in range(0, D, PAIR)
        ]
        grad_out = jnp.concatenate([part.reshape(GROUP, PAIR) for part in parts], axis=1)
        value = grad_out + norm_back(xhat, inverse, gains[1:2, :], grad)
        grad_after[span, :] = value
        after_low[span, :] = value.astype(BF16)

    grad_att[...] = mm(after_low[...], out_weight(strips), 1, 1).astype(BF16)
    grad_w = mm(attended[...], after_low[...], 0, 0).astype(BF16)
    emit.store(
        [
            (value, row // 4, 24 + 2 * (row % 4) + part)
            for row, part, value in strips_of(grad_w, 8, 2)
        ]
    )


def attention_backward(held, coords, mask, normed, qkv, grad_att, *rest):
    grad_mixed, *targets = rest[held:]
    rows = normed.shape[0]
    emit = Emitter(targets, (LOWER,), coords)

    @pl.loop(0, rows // GROUP)
    def _(i):
        span = span_of(i)
        caption = caption_of()
        scale = HD ** (-0.5)
        pairs = list(pairs_of())
        scores = [
            compact(
                mm(qkv[3 * half + 1, span, lanes], split_pair(qkv[3 * half, span, lanes]), 1, 1),
                caption,
            )
            for half, lanes, _ in pairs
        ]
        grad_probs = [
            compact(
                mm(qkv[3 * half + 2, span, lanes], split_pair(grad_att[span, wide]), 1, 1), caption
            )
            for half, lanes, wide in pairs
        ]
        probs = softmax_of(jnp.concatenate(scores, axis=1), key_bias(mask[i]))
        grad_probs = jnp.concatenate(grad_probs, axis=1)
        inner = jnp.sum(probs * grad_probs, axis=0, keepdims=True)
        grad_scores = probs * (grad_probs - inner)
        for pair, (half, lanes, wide) in enumerate(pairs):
            spread = expand(columns(grad_scores, pair), caption)
            back = mm(spread, qkv[3 * half + 1, span, lanes], 0, 0)
            grad_mixed[3 * half, span, lanes] = (join_pair(back) * scale).astype(BF16)
            back = mm(spread, split_pair(qkv[3 * half, span, lanes]))
            grad_mixed[3 * half + 1, span, lanes] = (back * scale).astype(BF16)
            spread = expand(columns(probs, pair), caption)
            grad_mixed[3 * half + 2, span, lanes] = mm(
                spread, split_pair(grad_att[span, wide])
            ).astype(BF16)

    for half in range(HALVES):
        grads = jnp.concatenate([grad_mixed[3 * half + part] for part in range(3)], axis=1)
        grad_w = mm(normed[...], grads, 0, 0).astype(BF16)
        emit.store([(value, half, 3 * row + part) for row, part, value in strips_of(grad_w, 8, 3)])


def input_backward(tok, gains, grad_mixed, grad_after, gain_two, strips, input_grad, gain_part):
    rows = tok.shape[0]
    grads = jnp.concatenate([grad_mixed[part] for part in range(6)], axis=1)
    halves = [weight_of(strips, half, 0, 8, 3, range(3)) for half in range(HALVES)]
    input_grad[...] = mm(grads, jnp.concatenate(halves, axis=1), 1, 1)
    gain_part[0] = jnp.zeros_like(gain_two)
    gain_part[1] = gain_two[...]

    @pl.loop(0, rows // GROUP)
    def _(i):
        span = span_of(i)
        xhat, inverse = norm_parts(tok[span, :].astype(F32))
        grad = input_grad[span, :]
        gain_part[0] += jnp.sum(grad * xhat, axis=0, keepdims=True)
        input_grad[span, :] = grad_after[span, :] + norm_back(xhat, inverse, gains[0:1, :], grad)


def shape_of(*shape, dtype=BF16):
    return jax.ShapeDtypeStruct(shape, dtype)


VMEM = pl.BlockSpec(memory_space=pltpu.VMEM)
SMEM = pl.BlockSpec(memory_space=pltpu.SMEM)


def call(kernel, name, in_specs, outs, scratch, flops, args, grid=(1,), aliases=None, mib=10):
    moved = sum(math_size(a.shape) * a.dtype.itemsize for a in args)
    moved += sum(math_size(s.shape) * s.dtype.itemsize for _, s in outs)
    return pl.pallas_call(
        kernel,
        grid=grid,
        in_specs=in_specs,
        out_specs=[spec for spec, _ in outs],
        out_shape=[shape for _, shape in outs],
        scratch_shapes=scratch,
        input_output_aliases=aliases or {},
        compiler_params=pltpu.CompilerParams(
            dimension_semantics=("arbitrary",) * len(grid), vmem_limit_bytes=mib << 20
        ),
        cost_estimate=pl.CostEstimate(flops=1, bytes_accessed=1, transcendentals=0),
        name=name,
    )(*args)


def math_size(shape):
    size = 1
    for extent in shape:
        size *= extent
    return size


UNIT = 2 * 768 * 768 * 768


def run_prepare(coords, token_mask, cot, tok, gains):
    captions = cot.shape[0]
    rows = captions * SLOTS
    return call(
        prepare,
        "prepare",
        [SMEM] + [VMEM] * 4,
        [
            (VMEM, shape_of(rows // GROUP, SLOTS, GROUP, dtype=F32)),
            (VMEM, shape_of(rows, PAIR, dtype=F32)),
            (VMEM, shape_of(rows, D + PAIR)),
            (VMEM, shape_of(captions, PAIR, dtype=F32)),
            (VMEM, shape_of(rows, D)),
        ],
        [],
        1,
        (coords, token_mask, cot, tok, gains),
        mib=6,
    )


def run_forward(tok, gains, normed, mask, share, strips):
    rows = tok.shape[0]
    return call(
        attention_forward,
        "attention_forward",
        [VMEM] * 6,
        [
            (VMEM, shape_of(6, rows, STRIP)),
            (VMEM, shape_of(rows, D)),
            (VMEM, shape_of(rows, D, dtype=F32)),
            (VMEM, shape_of(rows, D)),
            (VMEM, shape_of(rows // SLOTS, D, dtype=F32)),
        ],
        [],
        5 * UNIT,
        (tok, gains, normed, mask, share, strips),
        mib=3,
    )


def targets_of(runs, split):
    if split:
        shapes = [shape_of(len(run), HALVES, 2, OWN, BLOCK, STRIP) for run in runs for _ in range(2)]
    else:
        shapes = [shape_of(HALVES, STRIPS, BLOCK, STRIP)]
    return [(VMEM, shape) for shape in shapes]


def run_mlp(coords, normed_two, out_wide, strips, split):
    rows = normed_two.shape[0]
    return call(
        mlp_both,
        "mlp_both",
        [SMEM] + [VMEM] * 3,
        [(VMEM, shape_of(4, D, PAIR, dtype=F32)), (VMEM, shape_of(rows, D, dtype=F32))]
        + targets_of((UPPER, LOWER), split),
        [pltpu.VMEM((rows, D), BF16), pltpu.VMEM((rows, D), BF16)],
        20 * UNIT,
        (coords, normed_two, out_wide, strips),
        grid=(4,),
        mib=6 if split else 44,
    )


def run_pool(after_pooled, hidden_pooled, inverse, strips):
    return call(
        pool_out,
        "pool_out",
        [VMEM] * 4,
        [(VMEM, jax.ShapeDtypeStruct(after_pooled.shape, F32))],
        [],
        UNIT // 2,
        (after_pooled, hidden_pooled, inverse, strips),
        mib=6,
    )[0]


def run_output(coords, gains, attended, after, cot, share, grad_two, strips, held, split):
    rows = after.shape[0]
    return call(
        functools.partial(output_backward, len(held)),
        "output_backward",
        [SMEM] + [VMEM] * (7 + len(held)),
        [
            (VMEM, shape_of(rows, D, dtype=F32)),
            (VMEM, shape_of(1, D, dtype=F32)),
            (VMEM, shape_of(rows, D)),
        ]
        + targets_of((LOWER,), split),
        [pltpu.VMEM((rows, D), BF16)],
        2 * UNIT,
        (coords, gains, attended, after, cot, share, grad_two, strips, *held),
        aliases={8 + i: 3 + i for i in range(len(held))},
        mib=6 if split else 56,
    )


def run_backward(coords, mask, normed, qkv, grad_att, held, split):
    rows = normed.shape[0]
    return call(
        functools.partial(attention_backward, len(held)),
        "attention_backward",
        [SMEM, VMEM, VMEM, VMEM, VMEM] + [VMEM] * len(held),
        [(VMEM, shape_of(6, rows, STRIP))] + targets_of((LOWER,), split),
        [],
        7 * UNIT,
        (coords, mask, normed, qkv, grad_att, *held),
        aliases={5 + i: 1 + i for i in range(len(held))},
        mib=6 if split else 56,
    )


def run_input(tok, gains, grad_mixed, grad_after, gain_two, strips):
    rows = tok.shape[0]
    return call(
        input_backward,
        "input_backward",
        [VMEM] * 6,
        [(VMEM, shape_of(rows, D, dtype=F32)), (VMEM, shape_of(2, 1, D, dtype=F32))],
        [],
        3 * UNIT,
        (tok, gains, grad_mixed, grad_after, gain_two, strips),
        mib=5,
    )


def to_strips(blocks):
    count = blocks.shape[0] // 4
    return blocks.reshape(count, 4, BLOCK, BLOCK).transpose(0, 2, 1, 3).reshape(count, BLOCK, STRIP)


def to_blocks(strips):
    count = strips.shape[0]
    return strips.reshape(count, BLOCK, 4, BLOCK).transpose(0, 2, 1, 3).reshape(-1, BLOCK, BLOCK)


EVERY = ("tensor", "dp")


def gather_weights(master):
    low = master.astype(BF16)
    own = low.shape[0]
    if own % 4 == 0:
        strips = to_strips(low).reshape(-1, STRIP)
        strips = lax.all_gather(strips, EVERY, axis=0, tiled=True)
        return strips.reshape(HALVES, STRIPS, BLOCK, STRIP)
    blocks = lax.all_gather(low, EVERY, axis=0, tiled=True)
    return to_strips(blocks).reshape(HALVES, STRIPS, BLOCK, STRIP)


def pack(master, out):
    for strip in range(master.shape[0] // 4):
        parts = [master[4 * strip + i].astype(BF16) for i in range(4)]
        out[0, strip] = jnp.concatenate(parts, axis=1)


def take_halves(by_x, by_y, from_x, from_y):
    for plane in range(by_x.shape[0]):
        from_x[plane] = by_x[plane, 0:3]
        from_y[plane] = by_y[plane, 3:6]


def take_both(one, two, out):
    out[0] = one[0]
    out[1] = two[0]


def place_own(held, planes, coords, own, by_x, by_y, across_one, across_two, *rest):
    whole, sent = rest[held:]
    core, place, plane, half = coords[0], coords[1], coords[2], coords[3]
    for i, apart in enumerate(planes):
        z = plane ^ apart

        def put(y, x, strips, value):
            sent[i, y, x, strips] = value
            whole[y, z, x, core, strips] = value

        put(half, place, slice(0, 6), own[i])
        put(half, 1 - place, slice(0, 6), by_x[i])
        put(1 - half, place, slice(0, 6), by_y[i])
        put(1 - half, 1 - place, slice(0, 3), across_one[i])
        put(1 - half, 1 - place, slice(3, 6), across_two[i])


def place_most(apart, coords, own, by_x, by_y, _, whole, sent):
    core, place, plane, half = coords[0], coords[1], coords[2], coords[3]
    for i, (y, x, value) in enumerate(
        ((half, place, own), (half, 1 - place, by_x), (1 - half, place, by_y))
    ):
        sent[i] = value[0]
        whole[y, plane ^ apart, x, core] = value[0]


def place_last(apart, coords, most_in, one_in, two_in, one, two, _, whole):
    core, place, plane, half = coords[0], coords[1], coords[2], coords[3]
    z = plane ^ apart
    for i, (y, x) in enumerate(((half, place), (half, 1 - place), (1 - half, place))):
        whole[y, z, x, 1 - core] = most_in[i]
    for strips, mine, other in ((pl.ds(0, 3), one, one_in), (pl.ds(3, 3), two, two_in)):
        whole[1 - half, z, 1 - place, core, strips] = mine[0]
        whole[1 - half, z, 1 - place, 1 - core, strips] = other[0]


def place_other(planes, coords, arrived, _, whole):
    core, plane = coords[0], coords[2]
    for i, apart in enumerate(planes):
        for y in range(2):
            for x in range(2):
                whole[y, plane ^ apart, x, 1 - core] = arrived[i, y, x]


WHOLE = (HALVES, 4, 2, 2, OWN, BLOCK, STRIP)


def run_pack(master):
    return call(
        pack,
        "pack",
        [VMEM],
        [(VMEM, shape_of(1, OWN, BLOCK, STRIP))],
        [],
        math_size(master.shape),
        (master,),
        mib=4,
    )[0]


def run_halves(by_x, by_y):
    shape = shape_of(by_x.shape[0], 3, BLOCK, STRIP)
    return call(
        take_halves, "take_halves", [VMEM] * 2, [(VMEM, shape)] * 2, [], 1, (by_x, by_y), mib=4
    )


def run_both(one, two):
    shape = shape_of(2, OWN, BLOCK, STRIP)
    return call(take_both, "take_both", [VMEM] * 2, [(VMEM, shape)], [], 1, (one, two), mib=4)[0]


def run_place_own(planes, coords, pieces, held):
    count = len(planes)
    return call(
        functools.partial(place_own, len(held), planes),
        "place_own",
        [SMEM] + [VMEM] * (5 + len(held)),
        [(VMEM, shape_of(*WHOLE)), (VMEM, shape_of(count, HALVES, 2, OWN, BLOCK, STRIP))],
        [],
        1,
        (coords, *pieces, *held),
        aliases={6: 0} if held else None,
        mib=4,
    )


def run_place_most(apart, coords, pieces, whole):
    return call(
        functools.partial(place_most, apart),
        "place_most",
        [SMEM] + [VMEM] * 4,
        [(VMEM, shape_of(*WHOLE)), (VMEM, shape_of(3, OWN, BLOCK, STRIP))],
        [],
        1,
        (coords, *pieces, whole),
        aliases={4: 0},
        mib=4,
    )


def run_place_last(apart, coords, pieces, whole):
    return call(
        functools.partial(place_last, apart),
        "place_last",
        [SMEM] + [VMEM] * 6,
        [(VMEM, shape_of(*WHOLE))],
        [],
        1,
        (coords, *pieces, whole),
        aliases={6: 0},
        mib=4,
    )[0]


def run_place_other(planes, coords, arrived, whole):
    return call(
        functools.partial(place_other, planes),
        "place_other",
        [SMEM] + [VMEM] * 2,
        [(VMEM, shape_of(*WHOLE))],
        [],
        1,
        (coords, arrived, whole),
        aliases={2: 0},
        mib=4,
    )[0]


def neighbour_hop(value):
    return lax.ppermute(value, "dp", OTHER_X), lax.ppermute(value, "tensor", OTHER_Y)


def across_hop(pieces):
    return lax.ppermute(pieces[0], "tensor", OTHER_Y), lax.ppermute(pieces[1], "dp", OTHER_X)


def gather_split(master, coords, prepare):
    own = run_pack(master)
    near = lax.ppermute(own, "dp", NEAR_Z)
    far = lax.ppermute(own, "dp", FAR_Z)
    own_by = neighbour_hop(own)
    own_by, prepared = fence(own_by, prepare())
    own_across = across_hop(run_halves(*own_by))
    near, far, own_across, own_by, own, prepared = fence(near, far, own_across, own_by, own, prepared)

    both = run_both(near, far)
    both_by = neighbour_hop(both)
    other = lax.ppermute(far, "dp", NEAR_Z)
    other_by = neighbour_hop(other)
    both_across = across_hop(run_halves(*both_by))
    whole, sent = run_place_own((0,), coords, (own, *own_by, *own_across), ())
    own_in = core_hop(sent)
    both_across, other_by, own_in, whole = fence(both_across, other_by, own_in, whole)

    other_across = across_hop(run_halves(*other_by))
    whole, sent = run_place_own((1, 2), coords, (both, *both_by, *both_across), (whole,))
    both_in = core_hop(sent)
    whole, sent = run_place_most(3, coords, (other, *other_by), whole)
    other_in = core_hop(sent)
    whole = run_place_other((0,), coords, own_in, whole)
    other_across, both_in, other_in, whole = fence(other_across, both_in, other_in, whole)

    across_in = core_hop(other_across[0]), core_hop(other_across[1])
    whole = run_place_other((1, 2), coords, both_in, whole)
    across_in, whole = fence(across_in, whole)
    whole = run_place_last(3, coords, (other_in, *across_in, *other_across), whole)
    return whole.reshape(HALVES, STRIPS, BLOCK, STRIP), prepared


def scatter_flat(strips, own):
    if own % 4 == 0:
        mine = lax.psum_scatter(
            strips.reshape(-1, STRIP), EVERY, scatter_dimension=0, tiled=True
        )
        return to_blocks(mine.reshape(-1, BLOCK, STRIP)).astype(F32)
    blocks = to_blocks(strips.reshape(-1, BLOCK, STRIP))
    return lax.psum_scatter(blocks, EVERY, scatter_dimension=0, tiled=True).astype(F32)


def fence(*values):
    return lax.optimization_barrier(values)


OTHER_CORE = [(i, i ^ 1) for i in range(16)]
OTHER_X = [(i, i ^ 2) for i in range(16)]
OTHER_Y = [(0, 1), (1, 0)]


def by_plane(*moves):
    return [(4 * a + i, 4 * b + i) for a, b in moves for i in range(4)]


NEAR_Z = by_plane((0, 1), (1, 0), (2, 3), (3, 2))
FAR_Z = by_plane((0, 2), (1, 3), (2, 0), (3, 1))


def split_sum(coords, kept, arrived, sent_one, sent_two, kept_one, kept_two):
    place, half = coords[1], coords[3]

    @pl.loop(0, 2 * kept.shape[0])
    def _(step):
        plane, i = step // 2, lax.rem(step, 2)
        one, two = pl.ds(0, 3), pl.ds(3, 3)
        sent_one[plane, i] = kept[plane, 1 - half, i, one] + arrived[plane, 1 - half, i, one]
        kept_one[plane, i] = kept[plane, half, i, one] + arrived[plane, half, i, one]
        sent_two[plane, i] = kept[plane, i, 1 - place, two] + arrived[plane, i, 1 - place, two]
        kept_two[plane, i] = kept[plane, i, place, two] + arrived[plane, i, place, two]


def split_again(coords, one, two, one_in, two_in, sent_one, sent_two, kept_one, kept_two):
    place, half = coords[1], coords[3]

    @pl.loop(0, one.shape[0])
    def _(plane):
        sent_one[plane] = one[plane, 1 - place] + one_in[plane, 1 - place]
        kept_one[plane] = one[plane, place] + one_in[plane, place]
        sent_two[plane] = two[plane, 1 - half] + two_in[plane, 1 - half]
        kept_two[plane] = two[plane, half] + two_in[plane, half]


def join_sum(coords, one, two, one_in, two_in, *outs):
    for i, out in enumerate(outs):
        plane = lax.rem(coords[2] + i, 2)
        out[0:3] = one[plane] + one_in[plane]
        out[3:6] = two[plane] + two_in[plane]


def pick_sum(coords, high, high_in, low, low_in, mine, sent):
    @pl.when(coords[2] >= 2)
    def _():
        mine[...] = high[...] + high_in[...]
        sent[...] = low[...] + low_in[...]

    @pl.when(coords[2] < 2)
    def _():
        mine[...] = low[...] + low_in[...]
        sent[...] = high[...] + high_in[...]


def renew_gains(grads, arrived, moments, gains, grads_out, moments_out, gains_out):
    for i in range(2):
        grad = grads[i] + arrived[i]
        moment = DECAY_RATE * moments[i : i + 1] + (1.0 - DECAY_RATE) * grad * grad
        grads_out[i : i + 1] = grad
        moments_out[i : i + 1] = moment
        gains_out[i : i + 1] = gains[i : i + 1] - GAIN_RATE * grad / (jnp.sqrt(moment) + 1e-08)


def sum_of(left, right, out):
    @pl.loop(0, left.shape[0])
    def _(i):
        out[i] = left[i] + right[i]


def run_split(coords, kept, arrived):
    shape = shape_of(kept.shape[0], 2, 3, BLOCK, STRIP)
    outs = call(
        split_sum,
        "split_sum",
        [SMEM, VMEM, VMEM],
        [(VMEM, shape)] * 4,
        [],
        math_size(kept.shape),
        (coords, kept, arrived),
        mib=4,
    )
    return outs[:2], outs[2:]


def run_again(coords, kept, arrived):
    shape = shape_of(kept[0].shape[0], 3, BLOCK, STRIP)
    outs = call(
        split_again,
        "split_again",
        [SMEM] + [VMEM] * 4,
        [(VMEM, shape)] * 4,
        [],
        2 * math_size(kept[0].shape),
        (coords, *kept, *arrived),
        mib=4,
    )
    return outs[:2], outs[2:]


def run_join(coords, kept, arrived):
    return call(
        join_sum,
        "join_sum",
        [SMEM] + [VMEM] * 4,
        [(VMEM, shape_of(OWN, BLOCK, STRIP))] * 2,
        [],
        2 * math_size(kept[0].shape),
        (coords, *kept, *arrived),
        mib=4,
    )


def run_pick(coords, high, high_in, low, low_in):
    return call(
        pick_sum,
        "pick_sum",
        [SMEM] + [VMEM] * 4,
        [(VMEM, shape_of(OWN, BLOCK, STRIP))] * 2,
        [],
        1,
        (coords, high, high_in, low, low_in),
        mib=4,
    )


def run_sum(left, right):
    return call(
        sum_of,
        "sum_of",
        [VMEM] * 2,
        [(VMEM, jax.ShapeDtypeStruct(left.shape, left.dtype))],
        [],
        math_size(left.shape),
        (left, right),
        mib=4,
    )[0]


def run_gains(grads, arrived, moments, gains):
    return call(
        renew_gains,
        "renew_gains",
        [VMEM] * 4,
        [(VMEM, shape_of(2, D, dtype=F32))] * 3,
        [],
        1,
        (grads, arrived, moments, gains),
        mib=4,
    )


def core_hop(sent):
    return lax.ppermute(sent, "dp", OTHER_CORE)


def first_hop(sent):
    return lax.ppermute(sent[0], "tensor", OTHER_Y), lax.ppermute(sent[1], "dp", OTHER_X)


def second_hop(sent):
    return lax.ppermute(sent[0], "dp", OTHER_X), lax.ppermute(sent[1], "tensor", OTHER_Y)


def precise(left, right, left_dim=1, right_dim=0):
    left_high, right_high = left.astype(BF16), right.astype(BF16)
    left_low = (left - left_high.astype(F32)).astype(BF16)
    right_low = (right - right_high.astype(F32)).astype(BF16)
    small = mm(left_high, right_low, left_dim, right_dim) + mm(
        left_low, right_high, left_dim, right_dim
    )
    return mm(left_high, right_high, left_dim, right_dim) + small


def update(mine, arrived, master, stat_left, stat_right, root_left, root_right, *outs):
    grad_out, left_out, right_out, master_out, copy_out = outs
    count = grad_out.shape[0]
    first = pl.program_id(0) * count
    grads = []
    for i in range(count // 4):
        strip = first // 4 + i
        grad = mine[strip].astype(F32) + arrived[strip].astype(F32)
        grads += [grad[:, j * BLOCK : (j + 1) * BLOCK] for j in range(4)]
    blocks = [first + i for i in range(count)]
    sides = [precise(g, root_right[block]) for g, block in zip(grads, blocks)]
    lefts = [precise(g, g, 1, 1) for g in grads]
    rights = [precise(g, g, 0, 0) for g in grads]
    directions = [precise(root_left[block], side) for side, block in zip(sides, blocks)]
    for i, block in enumerate(blocks):
        grad_out[i] = grads[i]
        left_out[i] = DECAY_RATE * stat_left[block] + (1.0 - DECAY_RATE) * lefts[i]
        right_out[i] = DECAY_RATE * stat_right[block] + (1.0 - DECAY_RATE) * rights[i]
        new = master[block] - STEP_RATE * directions[i]
        master_out[i] = new
        copy_out[i] = new.astype(BF16)


def run_update(sums, blocks):
    count = blocks[0].shape[0]
    step = 8 if count % 8 == 0 else 4
    tile = pl.BlockSpec((step, BLOCK, BLOCK), lambda i: (i, 0, 0))
    shape = shape_of(count, BLOCK, BLOCK, dtype=F32)
    return call(
        update,
        "update",
        [VMEM] * (len(sums) + len(blocks)),
        [(tile, shape)] * 4 + [(tile, shape_of(count, BLOCK, BLOCK))],
        [],
        12 * 2 * count * BLOCK**3,
        (*sums, *blocks),
        grid=(count // step,),
        mib=8,
    )


def sum_hops():
    hops = []
    for axis in ("tensor", "dp"):
        size, step = lax.axis_size(axis), 1
        while step < size:
            hops.append((axis, [(i, i ^ step) for i in range(size)]))
            step *= 2
    return hops


def plain_update(grad, master, stat_left, stat_right, root_left, root_right):
    left_new = DECAY_RATE * stat_left + (1.0 - DECAY_RATE) * jnp.einsum(
        "nij,nkj->nik", grad, grad, precision=PRECISE
    )
    right_new = DECAY_RATE * stat_right + (1.0 - DECAY_RATE) * jnp.einsum(
        "nji,njk->nik", grad, grad, precision=PRECISE
    )
    right_side = jnp.einsum("nij,njk->nik", grad, root_right, precision=PRECISE)
    direction = jnp.einsum("nij,njk->nik", root_left, right_side, precision=PRECISE)
    master_new = master - STEP_RATE * direction
    return grad, left_new, right_new, master_new, master_new.astype(BF16)


def body(
    tokens,
    token_mask,
    norm_gains,
    gain_moments,
    cotangent,
    master,
    stat_left,
    stat_right,
    root_left,
    root_right,
):
    rows = tokens.shape[0]
    own_caps = cotangent.shape[0]
    own = master.shape[0]
    split = lax.axis_size("dp") == 16 and lax.axis_size("tensor") == 2
    dp_pos, half = lax.axis_index("dp"), lax.axis_index("tensor")
    coords = jnp.stack([dp_pos % 2, dp_pos // 2 % 2, dp_pos // 4, half]).astype(jnp.int32)

    coords, master = fence(coords, master)
    first = functools.partial(run_prepare, coords, token_mask, cotangent, tokens, norm_gains)
    if split:
        strips, prepared = gather_split(master, coords, first)
    else:
        strips, prepared = gather_weights(master), first()
    mask, share, out_wide, inverse, normed = prepared
    qkv, attended, after, normed_two, after_pooled = run_forward(
        tokens, norm_gains, normed, mask, share, strips
    )
    hidden_pooled, grad_two, *held = run_mlp(coords, normed_two, out_wide, strips, split)
    hops = sum_hops()
    blocks = (master, stat_left, stat_right, root_left, root_right)
    if not split:
        grad_after, gain_two, grad_att, *held = run_output(
            coords, norm_gains, attended, after, cotangent, share, grad_two, strips, held, split
        )
        grad_mixed, *held = run_backward(coords, mask, normed, qkv, grad_att, held, split)
        input_grad, gain_grads = run_input(
            tokens, norm_gains, grad_mixed, grad_after, gain_two, strips
        )
        pooled = run_pool(after_pooled, hidden_pooled, inverse, strips)
        for hop in hops[:-1]:
            gain_grads = run_sum(gain_grads, lax.ppermute(gain_grads, *hop))
        gain_in = lax.ppermute(gain_grads, *hops[-1])
        gain_results = run_gains(gain_grads, gain_in, gain_moments, norm_gains)
        updated = plain_update(scatter_flat(held[0], own), *blocks)
    else:
        upper_kept, upper_sent, *lower = held
        upper_in = core_hop(upper_sent)
        grad_after, gain_two, grad_att, *lower = run_output(
            coords, norm_gains, attended, after, cotangent, share, grad_two, strips, lower, split
        )
        upper_in, grad_att, lower = fence(upper_in, grad_att, lower)

        upper_sent, upper_kept = run_split(coords, upper_kept, upper_in)
        upper_sent, grad_att, lower = fence(upper_sent, grad_att, lower)
        upper_in = first_hop(upper_sent)
        grad_mixed, *lower = run_backward(coords, mask, normed, qkv, grad_att, lower, split)
        input_grad, gain_grads = run_input(
            tokens, norm_gains, grad_mixed, grad_after, gain_two, strips
        )
        upper_in, gain_grads, lower = fence(upper_in, gain_grads, lower)

        lower_in = core_hop(lower[1])
        upper_sent, upper_kept = run_again(coords, upper_kept, upper_in)
        upper_in = second_hop(upper_sent)

        lower_sent, lower_kept = run_split(coords, lower[0], lower_in)
        lower_in = first_hop(lower_sent)

        gain_in = lax.ppermute(gain_grads, *hops[0])
        pooled = run_pool(after_pooled, hidden_pooled, inverse, strips)
        high, high_sent = run_join(coords, upper_kept, upper_in)
        high_in = lax.ppermute(high_sent, "dp", NEAR_Z)
        high_in, lower_in, gain_in, pooled = fence(high_in, lower_in, gain_in, pooled)

        lower_sent, lower_kept = run_again(coords, lower_kept, lower_in)
        lower_in = second_hop(lower_sent)
        gain_grads = run_sum(gain_grads, gain_in)
        gain_in = lax.ppermute(gain_grads, *hops[1])
        lower_in, gain_in = fence(lower_in, gain_in)

        low, low_sent = run_join(coords, lower_kept, lower_in)
        low_in = lax.ppermute(low_sent, "dp", NEAR_Z)
        gain_grads = run_sum(gain_grads, gain_in)
        gain_in = lax.ppermute(gain_grads, *hops[2])
        low_in, gain_in = fence(low_in, gain_in)

        mine, sent = run_pick(coords, high, high_in, low, low_in)
        arrived = lax.ppermute(sent, "dp", FAR_Z)
        gain_grads = run_sum(gain_grads, gain_in)
        gain_in = lax.ppermute(gain_grads, *hops[3])
        gain_grads = run_sum(gain_grads, gain_in)
        gain_in = lax.ppermute(gain_grads, *hops[4])
        gain_results = run_gains(gain_grads, gain_in, gain_moments, norm_gains)
        arrived, gain_results = fence(arrived, gain_results)

        updated = run_update((mine, arrived), blocks)
    return (pooled, input_grad, *gain_results, *updated)


def solution(mesh):
    rows = P(("dp", "tensor"), None)
    blocks = P(("dp", "tensor"), None, None)
    return jax.shard_map(
        body,
        mesh=mesh,
        in_specs=(rows, P("dp", None), P(), P(), rows) + (blocks,) * 5,
        out_specs=(rows, rows, P(), P(), P()) + (blocks,) * 5,
        check_vma=False,
    )
```
